32 devices in a mesh: groups: 2 (over x), slab: 16 (over z, y, core).
Axes of the slice: x: 2, y: 2, z: 4, core: 2. Of those that a mesh axis runs over, the one named last changes fastest.
Arguments:
- conc_init: float32 [128, 16384], P(('groups', 'slab')), parts along dimension 0, may hold values from 0.2 to 2
- cover_init: float32 [128, 256], P(('groups', 'slab')), parts along dimension 0, may hold values from 0 to 0.9
- rate_on: float32 [128, 256], P(('groups', 'slab')), parts along dimension 0, may hold values from 0.05 to 0.5
- rate_off: float32 [128, 256], P(('groups', 'slab')), parts along dimension 0, may hold values from 0.02 to 0.2
- site_mask: int32 [128, 256], P(('groups', 'slab')), parts along dimension 0, may hold values 0 or 1
- inlet_profiles: float32 [16, 64], P('groups'), parts along dimension 0, may hold values from 0.5 to 2.5
- inlet_index: int32 [512], P('groups'), parts along dimension 0, may hold values from 0 to 7
- lift: float32 [3, 64], replicated, may hold values from -4.6 to 4.6
- mode_weight: bfloat16 [2048, 2, 64, 64], P('slab'), may hold values from -0.5 to 0.5
- point_weight: bfloat16 [64, 64], replicated, may hold values from -0.75 to 0.75
- point_bias: float32 [64], replicated, may hold values from -3 to 3
- readout: float32 [64], replicated, may hold values from -0.75 to 0.75
- cotangent: float32 [128, 16384], P(('groups', 'slab')), parts along dimension 0, may hold values from -6 to 6
Outputs:
- concentration: float32 [128, 16384], P(('groups', 'slab')), parts along dimension 0
- coverage: float32 [128, 256], P(('groups', 'slab')), parts along dimension 0
- prediction: float32 [128, 16384], P(('groups', 'slab')), parts along dimension 0
- grad_modes: float32 [4096, 2, 64, 64], P(('groups', 'slab')), parts along dimension 0
- grad_point: float32 [128, 64], P('groups'), parts along dimension 0
The draws below stay inside these ranges and needn't reach their ends.
There are 2 independent parts, one for each index of `groups`. The reference program is written for one: setup_inputs(seed, part) draws one part's arguments, and reference() takes and returns one part's arrays. A program takes and returns all parts, laid end to end along the dimension named above; an argument that names none is the same for every part. Nothing has to cross between parts.
All inputs are finite; a program needn't handle non-finite values. No bound on the sum of `site_mask` on one device may be relied on, other than what follows from the above.
Results may differ from the reference program's by a relative error of at most 0.0061.
Values may be sent and summed in bfloat16 or wider, within the bound.
No kernel may reach another device: no remote copies, remote signals or barrier semaphores. Data moves between devices by JAX's collectives and lax.ppermute only.
A program may use at most 128 MiB of HBM per device.

```python
import math
import jax
import jax.numpy as jnp
from jax import lax

NY = 256
NZ = 64
CH = 64
KX = 16
KY = 16
KZ = 8
STEPS = 4
PROFILES = 8
NX = 64
MODES = 2048


def draw_conc_init(key, part):
    return jax.random.uniform(key, (NX, NY * NZ), jnp.float32, 0.2, 2.0)


def draw_lift(key, part):
    leading = jnp.clip(jax.random.normal(jax.random.fold_in(key, 11), (2, CH), jnp.float32), -4.0, 4.0)
    offsets = jnp.clip(jax.random.normal(jax.random.fold_in(key, 23), (CH,), jnp.float32), -4.0, 4.0)
    bias_row = -1.1 * leading[0] + 0.03 * offsets
    return jnp.concatenate([leading, bias_row[None]], axis=0)


def plant(drawn, stream_key, least, high):
    place = [jax.random.randint(jax.random.fold_in(stream_key, axis), (), 0, length) for axis, length in enumerate(drawn.shape)]
    widest = drawn.shape.index(max(drawn.shape))
    beside = place[:widest] + [(place[widest] + 1) % drawn.shape[widest]] + place[widest + 1:]
    return drawn.at[tuple(place)].set(least).at[tuple(beside)].set(high)


def steps_of(own_key, dims, cuts, low, largest):
    def one(position, shards_of):
        draws = jax.random.uniform(jax.random.fold_in(jax.random.fold_in(own_key, 6), position), (shards_of,), jnp.float32, low / len(cuts), largest / len(cuts))
        return jnp.repeat(jnp.exp(draws), dims[position] // shards_of).reshape((-1,) + (1,) * (len(dims) - position - 1))

    gain = one(*cuts[0])
    for cut in cuts[1:]:
        gain = gain * one(*cut)
    return gain


def scatter_about(rng, extent, scale, reach, shards=(), kind=jnp.bfloat16):
    drawn = scale * jax.random.normal(rng, extent, jnp.float32)
    if shards:
        drawn = drawn * steps_of(rng, extent, shards, -0.22, 0.18)
    return jnp.clip(drawn, -reach, reach).astype(kind)


def setup_inputs(seed: int = 0, part: int = 0) -> dict:
    keys = jax.random.split(jax.random.key(seed), 14)
    own_keys = jax.random.split(jax.random.fold_in(keys[13], part), 14)
    return {
        "conc_init": draw_conc_init(jax.random.fold_in(jax.random.fold_in(keys[13], part), 71), part),
        "cover_init": jnp.clip(0.9 * jax.random.uniform(own_keys[1], (NX, NY), jnp.float32) ** steps_of(own_keys[1], (NX, NY), ((0, 16),), -0.2, 0.2), 0.0, 0.9),
        "rate_on": jnp.clip(jnp.exp(math.log(0.5) - 2.3025851 * jax.random.uniform(own_keys[2], (NX, NY), jnp.float32) ** steps_of(own_keys[2], (NX, NY), ((0, 16),), -0.2, 0.2)), 0.05, 0.5),
        "rate_off": jnp.clip(jnp.exp(math.log(0.2) - 2.3025851 * jax.random.uniform(own_keys[3], (NX, NY), jnp.float32) ** steps_of(own_keys[3], (NX, NY), ((0, 16),), -0.2, 0.2)), 0.02, 0.2),
        "site_mask": plant((jax.random.randint(own_keys[4], (NX, NY), 0, 2) < 1).astype(jnp.int32), jax.random.fold_in(own_keys[4], 1), 0, 1),
        "inlet_profiles": jnp.clip(jax.random.uniform(own_keys[5], (PROFILES, NZ), jnp.float32, 0.5, 2.5), 0.5, 2.5),
        "inlet_index": plant(jax.random.randint(own_keys[6], (NY,), 0, PROFILES), jax.random.fold_in(own_keys[6], 1), 0, PROFILES - 1).astype(jnp.int32),
        "lift": draw_lift(jax.random.fold_in(keys[13], 71), part),
        "mode_weight": scatter_about(keys[8], (MODES, 2, CH, CH), (2 * CH) ** -0.5, 0.5, ((0, 16),)),
        "point_weight": scatter_about(keys[9], (CH, CH), CH ** -0.5, 0.75),
        "point_bias": scatter_about(keys[10], (CH,), 0.5, 3.0, (), jnp.float32),
        "readout": scatter_about(keys[11], (CH,), CH ** -0.5, 0.75, (), jnp.float32),
        "cotangent": scatter_about(own_keys[12], (NX, NY * NZ), 1.0, 6.0, ((0, 16),), jnp.float32),
    }


PEAK_SPEED = 0.6
DIFFUSIVITY = 0.06

def flow_speed(depth_cells):
    height = (jnp.arange(depth_cells, dtype=jnp.float32) + 0.5) / depth_cells
    return PEAK_SPEED * 4.0 * height * (1.0 - height)

def advance(padded, coverage, rate_on, rate_off, site_open, velocity):
    centre = padded[1:-1]
    behind = padded[:-2]
    ahead = padded[2:]
    left_cells = jnp.roll(centre, 1, axis=1)
    right_cells = jnp.roll(centre, -1, axis=1)
    below_cells = jnp.concatenate([centre[:, :, :1], centre[:, :, :-1]], axis=2)
    above_cells = jnp.concatenate([centre[:, :, 1:], centre[:, :, -1:]], axis=2)
    laplace = behind + ahead + left_cells + right_cells + below_cells + above_cells - 6.0 * centre
    uptake = site_open * (rate_on * centre[:, :, 0] * (1.0 - coverage) - rate_off * coverage)
    updated = centre + DIFFUSIVITY * laplace - velocity[None, None, :] * (centre - behind)
    wall_layer = updated[:, :, :1] - uptake[:, :, None]
    updated = jnp.concatenate([wall_layer, updated[:, :, 1:]], axis=2)
    return (updated, coverage + uptake)

def cross_basis(span_cells, depth_cells):
    y_index = jnp.arange(span_cells, dtype=jnp.int32)[:, None, None, None]
    z_index = jnp.arange(depth_cells, dtype=jnp.int32)[None, :, None, None]
    wave_y = jnp.arange(KY, dtype=jnp.int32)[None, None, :, None]
    wave_z = jnp.arange(KZ, dtype=jnp.int32)[None, None, None, :]
    fraction = (wave_y * y_index % span_cells).astype(jnp.float32) / span_cells + (wave_z * z_index % depth_cells).astype(jnp.float32) / depth_cells
    angles = 2.0 * math.pi * fraction
    basis = jnp.stack([jnp.cos(angles), -jnp.sin(angles)], axis=-1)
    return basis.reshape(span_cells * depth_cells, 2 * KY * KZ).astype(jnp.bfloat16)

def stream_factors(positions, length_x):
    wave_x = jnp.arange(KX, dtype=jnp.int32)[:, None]
    phases = 2.0 * math.pi * (wave_x * positions[None, :] % length_x).astype(jnp.float32) / length_x
    return (jnp.cos(phases), jnp.sin(phases))

def along_x_forward(columns, cos_table, sin_table):
    highest = lax.Precision.HIGHEST
    channels, stream_len, spread = columns.shape
    split = columns.reshape(channels, stream_len, spread // 2, 2)
    real_part = split[..., 0]
    imag_part = split[..., 1]
    out_real = jnp.einsum('kx,cxy->ykc', cos_table, real_part, precision=highest) + jnp.einsum('kx,cxy->ykc', sin_table, imag_part, precision=highest)
    out_imag = jnp.einsum('kx,cxy->ykc', cos_table, imag_part, precision=highest) - jnp.einsum('kx,cxy->ykc', sin_table, real_part, precision=highest)
    return jnp.concatenate([out_real, out_imag], axis=2).reshape(-1, 2 * channels)

def along_x_inverse(rows, cos_table, sin_table):
    highest = lax.Precision.HIGHEST
    channels = rows.shape[1] // 2
    stream_len = cos_table.shape[1]
    shaped = rows.reshape(-1, KX, 2 * channels)
    real_part = shaped[:, :, :channels]
    imag_part = shaped[:, :, channels:]
    out_real = jnp.einsum('kx,ykc->cxy', cos_table, real_part, precision=highest) - jnp.einsum('kx,ykc->cxy', sin_table, imag_part, precision=highest)
    out_imag = jnp.einsum('kx,ykc->cxy', sin_table, real_part, precision=highest) + jnp.einsum('kx,ykc->cxy', cos_table, imag_part, precision=highest)
    return jnp.stack([out_real, out_imag], axis=-1).reshape(channels, stream_len, -1)

def mode_mixing(spectrum, mode_weight):
    highest = lax.Precision.HIGHEST
    channels = spectrum.shape[1] // 2
    spec_real = spectrum[:, :channels]
    spec_imag = spectrum[:, channels:]
    weights = mode_weight.astype(jnp.float32)
    weight_real = weights[:, 0]
    weight_imag = weights[:, 1]
    out_real = jnp.einsum('mc,mco->mo', spec_real, weight_real, precision=highest) - jnp.einsum('mc,mco->mo', spec_imag, weight_imag, precision=highest)
    out_imag = jnp.einsum('mc,mco->mo', spec_real, weight_imag, precision=highest) + jnp.einsum('mc,mco->mo', spec_imag, weight_real, precision=highest)
    return jnp.concatenate([out_real, out_imag], axis=1).astype(jnp.bfloat16)

def outer_grad(spectrum, grad_spectrum):
    channels = spectrum.shape[1] // 2
    spec_real = spectrum[:, :channels, None]
    spec_imag = spectrum[:, channels:, None]
    grad_real = grad_spectrum[:, None, :channels]
    grad_imag = grad_spectrum[:, None, channels:]
    first = spec_real * grad_real + spec_imag * grad_imag
    second = spec_real * grad_imag - spec_imag * grad_real
    return jnp.stack([first, second], axis=1)

def lift_features(concentration, coverage, lift):
    depth_cells = concentration.shape[2]
    surface = (jnp.arange(depth_cells) == 0).astype(jnp.float32)
    wall = coverage[:, :, None] * surface[None, None, :]
    lifted = lift[0][:, None, None, None] * concentration[None] + lift[1][:, None, None, None] * wall[None] + lift[2][:, None, None, None]
    return lifted.astype(jnp.bfloat16)

def reference(conc_init, cover_init, rate_on, rate_off, site_mask, inlet_profiles, inlet_index, lift, mode_weight, point_weight, point_bias, readout, cotangent):
    velocity = flow_speed(NZ)
    site_open = site_mask.astype(jnp.float32)
    inlet_plane = inlet_profiles[inlet_index]
    concentration = conc_init.reshape(NX, NY, NZ)
    coverage = cover_init
    for substep in range(STEPS):
        padded = jnp.concatenate([inlet_plane[None], concentration, concentration[-1:]], axis=0)
        concentration, coverage = advance(padded, coverage, rate_on, rate_off, site_open, velocity)
    basis = cross_basis(NY, NZ)
    cos_all, sin_all = stream_factors(jnp.arange(NX, dtype=jnp.int32), NX)
    forward_scale = 1.0 / math.sqrt(NX * NY * NZ)
    inverse_scale = 1.0 / math.sqrt(KX * KY * KZ)
    channels = lift.shape[1]

    def forward_row(row_items):
        conc_row, cover_row = row_items
        features = lift_features(conc_row[None], cover_row[None], lift).reshape(channels, NY * NZ)
        return jnp.dot(features, basis, preferred_element_type=jnp.float32)
    columns = lax.map(forward_row, (concentration, coverage))
    spectrum = forward_scale * along_x_forward(jnp.transpose(columns, (1, 0, 2)), cos_all, sin_all)
    mixed = mode_mixing(spectrum, mode_weight)
    inverse = (inverse_scale * along_x_inverse(mixed.astype(jnp.float32), cos_all, sin_all)).astype(jnp.bfloat16)

    def backward_row(running, row_items):
        conc_row, cover_row, inverse_row, cot_row = row_items
        lifted = lift_features(conc_row[None], cover_row[None], lift).reshape(channels, NY * NZ)
        spectral = lax.dot_general(inverse_row, basis, (((1,), (1,)), ((), ())), preferred_element_type=jnp.float32)
        preact = spectral + jnp.dot(point_weight, lifted, preferred_element_type=jnp.float32) + point_bias[:, None]
        hidden, gelu_back = jax.vjp(jax.nn.gelu, preact)
        pred_row = lax.optimization_barrier(jnp.sum(readout[:, None] * hidden, axis=0))
        grad_pre, = gelu_back(readout[:, None] * cot_row.reshape(1, -1))
        grad_pre = grad_pre.astype(jnp.bfloat16)
        running = running + lax.dot_general(grad_pre, lifted, (((1,), (1,)), ((), ())), preferred_element_type=jnp.float32)
        grad_row = inverse_scale * jnp.dot(grad_pre, basis, preferred_element_type=jnp.float32)
        return (running, (pred_row, grad_row))
    start = jnp.zeros((channels, channels), jnp.float32)
    grad_point, outputs = lax.scan(backward_row, start, (concentration, coverage, jnp.transpose(inverse, (1, 0, 2)), cotangent))
    prediction, grad_rows = outputs
    grad_spectrum = along_x_forward(jnp.transpose(grad_rows, (1, 0, 2)), cos_all, sin_all)
    grad_modes = outer_grad(spectrum, grad_spectrum)
    return (concentration.reshape(NX, NY * NZ), coverage, prediction, grad_modes, grad_point)
```

```python
import functools
import math

import jax
import jax.numpy as jnp
import numpy as np
from jax import lax
from jax.experimental import pallas as pl
from jax.experimental.pallas import tpu as pltpu
from jax.sharding import PartitionSpec as P

KX = 16
KY = 16
KZ = 8
STEPS = 4
PROFILES = 8

PEAK_SPEED = 0.6
DIFFUSIVITY = 0.06
CENTRE = 1.1
ZG = 4

HI = lax.Precision.HIGHEST
F32 = jnp.float32
BF16 = jnp.bfloat16


def dot(a, b, precision=None):
    return jnp.dot(a, b, preferred_element_type=F32, precision=precision)


def dot_nt(a, b, precision=None):
    return lax.dot_general(a, b, (((1,), (1,)), ((), ())), preferred_element_type=F32, precision=precision)


def dot_tn(a, b, precision=None):
    return lax.dot_general(a, b, (((0,), (0,)), ((), ())), preferred_element_type=F32, precision=precision)


def tables(span, depth, total_x, devices, local_x):
    half = span // 2
    own_j = KY * KZ // devices
    tab = {}
    lane = np.arange(half)
    perm = np.zeros((half, 4 * half), np.float32)
    for h in range(2):
        for par in range(2):
            k = (h * half + lane - par) / 2.0
            good = (k == np.floor(k)) & (k >= 0)
            perm[lane[good], (2 * h + par) * half + k[good].astype(int)] = 1.0
    tab["perm"] = perm
    back = np.zeros((span, span), np.float32)
    for par in range(2):
        back[par * half + lane, 2 * lane + par] = 1.0
    tab["back"] = back
    ky = np.arange(KY)
    kz = np.arange(KZ)
    kx = np.arange(KX)
    y_of = np.concatenate([2 * lane, 2 * lane + 1])
    alpha = 2 * np.pi * ((y_of[:, None] * ky[None, :]) % span) / span
    tab["wave_y"] = np.concatenate([np.cos(alpha), np.sin(alpha)], axis=1).astype(np.float32)
    z = np.arange(depth)
    beta = 2 * np.pi * ((kz[:, None] * z[None, :]) % depth) / depth
    tab["wave_z"] = np.concatenate([np.cos(beta), np.sin(beta)], axis=0).astype(np.float32)
    pairs = 2 * KY
    ez = np.zeros((2 * KY * KZ, depth, KY, 2), np.float32)
    for j in range(KY * KZ):
        a, b = j // KZ, j % KZ
        row = (j // own_j) * 2 * own_j + j % own_j
        ez[row, :, a, 0] = np.cos(beta[b])
        ez[row + own_j, :, a, 0] = -np.sin(beta[b])
        ez[row, :, a, 1] = -np.sin(beta[b])
        ez[row + own_j, :, a, 1] = -np.cos(beta[b])
    tab["ez"] = ez.reshape(2 * KY * KZ, depth * pairs).astype(jnp.bfloat16)
    by = np.stack([np.cos(alpha), np.sin(alpha)], axis=2).reshape(span, pairs)
    fwd = np.zeros((ZG, ZG * pairs + 16, span), np.float32)
    bwd = np.zeros((ZG, span, ZG * pairs), np.float32)
    for i in range(ZG):
        fwd[i, i * pairs : (i + 1) * pairs] = by.T
        fwd[i, ZG * pairs : ZG * pairs + 2] = 1.0
        bwd[i, :, i * pairs : (i + 1) * pairs] = by
    tab["fwd"] = fwd.astype(jnp.bfloat16)
    tab["bwd"] = bwd.reshape(ZG * span, ZG * pairs).astype(jnp.bfloat16)
    x = np.arange(total_x)
    gamma = 2 * np.pi * ((x[:, None] * kx[None, :]) % total_x) / total_x
    cg, sg = np.cos(gamma), np.sin(gamma)
    scale = 1.0 / math.sqrt(total_x * span * depth)
    ax = np.zeros((total_x, 2, 2, KX))
    ax[:, 0, 0], ax[:, 1, 0] = cg, sg
    ax[:, 0, 1], ax[:, 1, 1] = -sg, cg
    rep = np.repeat(ax[:, :, :, None, :], own_j, axis=3) * scale
    tab["ax"] = rep.reshape(2 * total_x, 2 * own_j * KX).astype(np.float32)
    iscale = 1.0 / math.sqrt(KX * KY * KZ)
    bx = np.zeros((total_x, 2, 2, KX))
    bx[:, 0, 0], bx[:, 0, 1] = cg, -sg
    bx[:, 1, 0], bx[:, 1, 1] = sg, cg
    bx = bx.reshape(devices, local_x, 2, 2 * KX).transpose(1, 0, 2, 3) * iscale
    tab["bx"] = bx.reshape(2 * total_x, 2 * KX).astype(np.float32)
    gx = ax.reshape(devices, local_x, 2, 2 * KX).transpose(1, 3, 0, 2).reshape(local_x, 2 * KX, 2 * devices)
    high = gx.astype(np.float32).astype(jnp.bfloat16)
    low = (gx - high.astype(np.float64)).astype(np.float32).astype(jnp.bfloat16)
    tab["gx"] = np.concatenate([high, low], axis=1)
    return tab


def transport_kernel(
    flags, own, up, down, index, profiles, cot, perm, back, wave_y, wave_z,
    conc_out, cover_out, conc_z, cot_z, cover_z, wave_c, wave_w, buf,
):
    local_x = own.shape[0]
    half = cot.shape[2]
    depth = profiles.shape[1]
    rows = 3 * local_x
    packs = (up, own, down)
    for r in range(rows):
        buf[0, r] = packs[r // local_x][r % local_x, :half, :].T
    walls = jnp.concatenate(
        [packs[r // local_x][r % local_x, half:, :] for r in range(rows)]
        + [jnp.concatenate([index[...], jnp.zeros((6, half), F32)], axis=0)],
        axis=0,
    )
    spread = dot(walls, perm[...], HI)
    fields = [
        spread[8 * r : 8 * r + 4, : 2 * half] + spread[8 * r + 4 : 8 * r + 8, 2 * half :]
        for r in range(rows)
    ]
    chosen = spread[8 * rows : 8 * rows + 1, : 2 * half] + spread[8 * rows + 1 : 8 * rows + 2, 2 * half :]
    pick = lax.broadcasted_iota(jnp.int32, (PROFILES, 2 * half), 0).astype(F32)
    onehot = (jnp.abs(pick - chosen) < 0.5).astype(F32)
    inlet = dot_tn(profiles[...], onehot, HI)
    inlet = jnp.concatenate([inlet[:, :half], inlet[:, half:]], axis=0)
    height = lax.broadcasted_iota(jnp.int32, (depth, half), 0).astype(F32)
    height = (height + 0.5) / depth
    speed = PEAK_SPEED * 4.0 * height * (1.0 - height)
    speed = jnp.concatenate([speed, speed], axis=0)
    first = flags[0] == 1
    last = flags[1] == 1
    cover = [f[0:1] for f in fields]
    for step in range(STEPS):
        cur, nxt = step % 2, (step + 1) % 2
        for r in range(1 + step, rows - 1 - step):
            c = buf[cur, r]
            behind = buf[cur, r - 1]
            ahead = buf[cur, r + 1]
            if r == local_x:
                behind = jnp.where(first, inlet, behind)
            if r == 2 * local_x - 1:
                ahead = jnp.where(last, c, ahead)
            even, odd = c[:depth], c[depth:]
            side = jnp.concatenate(
                [odd + pltpu.roll(odd, 1, 1), even + pltpu.roll(even, half - 1, 1)], axis=0
            )
            below = jnp.concatenate(
                [even[:1], even[:-1], odd[:1], odd[:-1]], axis=0
            )
            above = jnp.concatenate(
                [even[1:], even[-1:], odd[1:], odd[-1:]], axis=0
            )
            laplace = behind + ahead + side + below + above - 6.0 * c
            f = fields[r]
            wall = jnp.concatenate([even[:1], odd[:1]], axis=1)
            uptake = f[3:4] * (f[1:2] * wall * (1.0 - cover[r]) - f[2:3] * cover[r])
            new = c + DIFFUSIVITY * laplace - speed * (c - behind)
            buf[nxt, r] = new
            buf[nxt, r, 0:1] = new[0:1] - uptake[:, :half]
            buf[nxt, r, depth : depth + 1] = new[depth : depth + 1] - uptake[:, half:]
            cover[r] = cover[r] + uptake
    cur = STEPS % 2
    covers = jnp.concatenate(cover[local_x : 2 * local_x], axis=0)
    cover_z[...] = covers
    cover_out[...] = dot(covers, back[...], HI)
    wave_w[...] = dot(covers, wave_y[...], HI)
    planes = [buf[cur, local_x + i] for i in range(local_x)]
    evens = jnp.concatenate([p[:depth] for p in planes], axis=0)
    odds = jnp.concatenate([p[depth:] for p in planes], axis=0)
    along_y = dot(evens, wave_y[:half], HI) + dot(odds, wave_y[half:], HI)
    for i in range(local_x):
        wave_c[i] = dot(wave_z[...], along_y[i * depth : (i + 1) * depth], HI)
        conc_out[i] = planes[i].T
        conc_z[:, i, :] = planes[i]
        cot_z[:, i, :] = cot[i].T


def mixing_kernel(place, waves, ax, bx, lift, weight, inv_out, spec_out, stage):
    modes = weight.shape[3]
    channels = weight.shape[1]
    own_j = modes // KX
    span2 = waves.shape[1]
    local_x = inv_out.shape[1] // channels
    blocks = inv_out.shape[0] // own_j
    spread = dot(waves[...], ax[...], HI)
    mode_j = lax.broadcasted_iota(jnp.int32, (own_j, 2 * modes), 1) % modes // KX
    keep = mode_j == lax.broadcasted_iota(jnp.int32, (own_j, 2 * modes), 0)
    rows = [
        jnp.sum(jnp.where(keep, spread[f * own_j : (f + 1) * own_j], 0.0), axis=0, keepdims=True)
        for f in range(2)
    ]
    lane = lax.broadcasted_iota(jnp.int32, (1, 2 * modes), 1)
    rows.append(jnp.where((lane == 0) & (place[0] == 0), place[1].astype(F32), 0.0))
    fields = jnp.concatenate(rows + [jnp.zeros((5, 2 * modes), F32)], axis=0)
    factors = jnp.concatenate([lift[...], jnp.zeros((5, channels), F32)], axis=0)
    spec = dot_tn(factors, fields, HI)
    spec_r, spec_i = spec[:, :modes], spec[:, modes:]
    spec_out[0] = spec_r
    spec_out[1] = spec_i

    acc_r = jnp.zeros((channels, modes), F32)
    acc_i = jnp.zeros((channels, modes), F32)
    for c in range(channels):
        wr = weight[0, c].astype(F32)
        wi = weight[1, c].astype(F32)
        vr = spec_r[c : c + 1]
        vi = spec_i[c : c + 1]
        acc_r = acc_r + (vr * wr - vi * wi)
        acc_i = acc_i + (vr * wi + vi * wr)
    mixed_r = acc_r.astype(BF16).astype(F32).T
    mixed_i = acc_i.astype(BF16).astype(F32).T
    for j in range(own_j):
        rhs = jnp.concatenate([mixed_r[j * KX : (j + 1) * KX], mixed_i[j * KX : (j + 1) * KX]], axis=0)
        out = dot(bx[...], rhs, HI)
        line = jnp.concatenate([out[i * blocks : (i + 1) * blocks] for i in range(local_x)], axis=1)
        if own_j == 1:
            stage[...] = line
        else:
            for h in range(line.shape[1] // 128):
                stage[h, pl.ds(j, blocks, own_j), :] = line[:, h * 128 : (h + 1) * 128]
    if own_j == 1:
        inv_out[...] = stage[...].astype(BF16)
    else:
        for h in range(stage.shape[0]):
            inv_out[:, h * 128 : (h + 1) * 128] = stage[h].astype(BF16)


def tail_blocks(own_j):
    return -(-3 // (2 * own_j))


def layer_kernel(
    own_j, inv, conc_z, cot_z, cover_z, lift, point_weight, bias, readout, ez, fwd, bwd,
    pred_out, grad_out, lhs, grads, ext_all, waves, pred, point,
):
    channels = lift.shape[1]
    local_x = cover_z.shape[0]
    half = cot_z.shape[2]
    span = 2 * half
    depth = cot_z.shape[0] // 2
    rows = local_x * channels
    wide = ZG * 2 * KY
    iscale = 1.0 / math.sqrt(KX * KY * KZ)

    factors = jnp.concatenate([lift[...], jnp.zeros((5, channels), F32)], axis=0)
    mapped = dot_nt(point_weight[...].astype(F32), factors, HI)
    eye = (
        lax.broadcasted_iota(jnp.int32, (channels, channels), 0)
        == lax.broadcasted_iota(jnp.int32, (channels, channels), 1)
    ).astype(F32)
    columns = dot_nt(eye, jnp.concatenate([bias[...], readout[...], jnp.zeros((6, channels), F32)], axis=0), HI)
    a0, a1 = mapped[:, 0:1], mapped[:, 1:2]
    a2 = mapped[:, 2:3] + columns[:, 0:1] + CENTRE * a0
    half_readout = 0.5 * columns[:, 1:2]

    def high(v):
        return v.astype(BF16).astype(F32)

    lane = lax.broadcasted_iota(jnp.int32, (channels, 32), 1)
    a0_high, a2_high = high(a0), high(a2)
    for x in range(local_x):
        block = jnp.zeros((channels, 32), F32)
        for at, value in (
            (0, a2_high), (1, a2 - a2_high),
            (16 + x, a0_high), (20 + x, a0_high), (24 + x, a0 - a0_high), (28 + x, a1),
        ):
            block = jnp.where(lane == at, value, block)
        block = block.astype(BF16)
        for g in range(depth // ZG):
            lhs[g, x * channels : (x + 1) * channels, wide : wide + 32] = block
    flipped = inv[...].astype(F32).T.astype(BF16)
    lifted = dot(flipped, ez[...]).astype(BF16)
    for g in range(depth // ZG):
        lhs[g, :, :wide] = lifted[:, g * wide : (g + 1) * wide]
    point[...] = jnp.zeros(point.shape, F32)
    scale_rows = jnp.broadcast_to(half_readout, (channels, span))
    c1 = math.sqrt(2.0 / math.pi)
    c2 = c1 * 0.044715

    def group(g, carry):
        for i in range(ZG):
            z = g * ZG + i
            conc = jnp.concatenate([conc_z[z], conc_z[depth + z]], axis=1) - CENTRE
            cot = jnp.concatenate([cot_z[z], cot_z[depth + z]], axis=1)
            conc_high = high(conc)
            wall = jnp.where(z == 0, cover_z[...], 0.0)
            ext = jnp.concatenate([conc_high, conc - conc_high, conc_high, wall], axis=0).astype(BF16)
            ext_all[:, i * span : (i + 1) * span] = ext
            pre = dot(lhs[g], jnp.concatenate([fwd[i], ext], axis=0))
            for x in range(local_x):
                v = pre[x * channels : (x + 1) * channels]
                p = c1 + c2 * (v * v)
                t = jnp.tanh(v * p)
                s = 1.0 + t
                line = jnp.sum(scale_rows * (v * s), axis=0, keepdims=True)
                pred[x, pl.ds(z, 1), :] = line[:, :half]
                pred[x, pl.ds(depth + z, 1), :] = line[:, half:]
                slope = v * (3.0 * p - 2.0 * c1)
                grad = s * (1.0 + slope * (1.0 - t)) * cot[x : x + 1]
                grads[x * channels : (x + 1) * channels, i * span : (i + 1) * span] = grad.astype(BF16)
        waves[g] = dot(grads[...], bwd[...]).astype(BF16)
        point[...] += dot_nt(grads[...], ext_all[...])
        return carry

    lax.fori_loop(0, depth // ZG, group, 0)
    for x in range(local_x):
        pred_out[x] = pred[x].T
    total = jnp.zeros((rows, ez.shape[0]), F32)
    for g in range(depth // ZG):
        total = total + dot_nt(waves[g], ez[:, g * wide : (g + 1) * wide])
    lane16 = lax.broadcasted_iota(jnp.int32, (channels, 16), 1)
    lane128 = lax.broadcasted_iota(jnp.int32, (channels, 128), 1)
    cols = []
    extra = []
    for x in range(local_x):
        here = slice(x * channels, (x + 1) * channels)
        pt = point[here, :]
        with_conc = jnp.sum(jnp.where((lane16 == x) | (lane16 == 4 + x), pt, 0.0), axis=1, keepdims=True)
        with_wall = jnp.sum(jnp.where(lane16 == 12 + x, pt, 0.0), axis=1, keepdims=True)
        alone = total[here, 0:1]
        e = jnp.where(lane128 == 0, with_conc, jnp.where(lane128 == 1, with_wall, jnp.where(lane128 == 2, alone, 0.0)))
        extra.append(half_readout * e)
        cols.append((iscale * half_readout) * total[here])
    sums = extra[0]
    for e in extra[1:]:
        sums = sums + e
    sums = sums.T[:16]
    sums_high = high(sums)
    both = jnp.concatenate([sums_high, sums - sums_high], axis=1).astype(BF16)
    out_rows = grad_out.shape[0]
    grad_out[:, :rows] = jnp.concatenate(cols, axis=0).T.astype(BF16)
    for b in range(tail_blocks(own_j)):
        row = lax.broadcasted_iota(jnp.int32, (out_rows, 16), 0) % (2 * own_j) + b * 2 * own_j
        pick = (row == lax.broadcasted_iota(jnp.int32, (out_rows, 16), 1)).astype(BF16)
        grad_out[:, rows + b * 128 : rows + (b + 1) * 128] = dot(pick, both).astype(BF16)


def outer_kernel(own_j, got, spec, gx, lift, modes_out, point_out, d_r, d_i, stage):
    channels = spec.shape[1]
    modes = spec.shape[2]
    rows = got.shape[1] - 128 * tail_blocks(own_j)
    local_x = rows // channels
    per = modes_out.shape[1]

    @pl.when(pl.program_id(0) == 0)
    def _():
        for h in range(rows // 128):
            stage[h] = got[:, h * 128 : (h + 1) * 128].astype(F32)
        blocks = got.shape[0] // own_j
        parts_r, parts_i = [], []
        for j in range(own_j):
            line = jnp.concatenate(
                [stage[h, pl.ds(j, blocks, own_j), :] if own_j > 1 else stage[h] for h in range(rows // 128)], axis=1
            ).astype(BF16)
            acc = jnp.zeros((4 * KX, channels), F32)
            for x in range(local_x):
                acc = acc + dot(gx[x], line[:, x * channels : (x + 1) * channels])
            acc = acc[: 2 * KX] + acc[2 * KX :]
            parts_r.append(acc[:KX])
            parts_i.append(acc[KX:])
        d_r[...] = jnp.concatenate(parts_r, axis=0).T
        d_i[...] = jnp.concatenate(parts_i, axis=0).T
        sums = jnp.zeros((8, 128), F32)
        for b in range(tail_blocks(own_j)):
            tail = got[:, rows + b * 128 : rows + (b + 1) * 128]
            at = lax.broadcasted_iota(jnp.int32, (8, got.shape[0]), 1) % (2 * own_j) + b * 2 * own_j
            pick = (at == lax.broadcasted_iota(jnp.int32, (8, got.shape[0]), 0)).astype(BF16)
            sums = sums + dot(pick, tail)
        sums = sums[:, :channels] + sums[:, channels:]
        row = lax.broadcasted_iota(jnp.int32, (8, channels), 0)
        base = jnp.concatenate([lift[...], jnp.zeros((5, channels), F32)], axis=0)
        base = jnp.where(row == 2, base + CENTRE * lift[0:1], base)
        point_out[...] = dot_tn(jnp.where(row < 3, sums, 0.0), base, HI)

    start = pl.program_id(0) * per
    dr = d_r[...]
    di = d_i[...]
    for c in range(per):
        vr = spec[0, pl.ds(start + c, 1), :]
        vi = spec[1, pl.ds(start + c, 1), :]
        modes_out[0, c] = vr * dr + vi * di
        modes_out[1, c] = vr * di - vi * dr


def params(**kw):
    return pltpu.CompilerParams(vmem_limit_bytes=56 * 1024 * 1024, **kw)


def vmem(count):
    return [pl.BlockSpec(memory_space=pltpu.VMEM) for _ in range(count)]


def body(
    conc_init, cover_init, rate_on, rate_off, site_mask, inlet_profiles, inlet_index, lift,
    mode_weight, point_weight, point_bias, readout, cotangent,
):
    devices = lax.axis_size("slab")
    position = lax.axis_index("slab")
    local_x, plane = conc_init.shape
    depth = inlet_profiles.shape[1]
    span = plane // depth
    half = span // 2
    channels = lift.shape[1]
    modes = mode_weight.shape[0]
    own_j = modes // KX
    total_x = local_x * devices
    tab = {k: jnp.asarray(v) for k, v in tables(span, depth, total_x, devices, local_x).items()}
    sds = jax.ShapeDtypeStruct
    smem = pl.BlockSpec(memory_space=pltpu.SMEM)

    walls = jnp.stack([cover_init, rate_on, rate_off, site_mask.astype(F32)], axis=1)
    walls = walls.reshape(local_x, 4, 2, half).transpose(0, 2, 1, 3).reshape(local_x, 8, half)
    pack = jnp.concatenate([conc_init.reshape(local_x, half, 2 * depth), walls], axis=1)
    up = lax.ppermute(pack, "slab", [(i, i + 1) for i in range(devices - 1)])
    down = lax.ppermute(pack, "slab", [(i + 1, i) for i in range(devices - 1)])
    flags = jnp.stack([position == 0, position == devices - 1]).astype(jnp.int32)
    index = inlet_index.astype(F32).reshape(2, half)
    conc_out, cover_out, conc_z, cot_z, cover_z, wave_c, wave_w = pl.pallas_call(
        transport_kernel,
        name="transport",
        out_shape=(
            sds((local_x, half, 2 * depth), F32),
            sds((local_x, span), F32),
            sds((2 * depth, local_x, half), F32),
            sds((2 * depth, local_x, half), F32),
            sds((local_x, span), F32),
            sds((local_x, 2 * KZ, 2 * KY), F32),
            sds((local_x, 2 * KY), F32),
        ),
        in_specs=[smem] + vmem(10),
        out_specs=vmem(7),
        scratch_shapes=[pltpu.VMEM((2, 3 * local_x, 2 * depth, half), F32)],
        compiler_params=params(),
    )(
        flags, pack, up, down, index, inlet_profiles, cotangent.reshape(local_x, half, 2 * depth),
        tab["perm"], tab["back"], tab["wave_y"], tab["wave_z"],
    )
    conc_re = wave_c[:, :KZ, :KY] - wave_c[:, KZ:, KY:]
    conc_im = -(wave_c[:, :KZ, KY:] + wave_c[:, KZ:, :KY])
    wall_re = jnp.broadcast_to(wave_w[:, None, :KY], conc_re.shape)
    wall_im = jnp.broadcast_to(-wave_w[:, None, KY:], conc_re.shape)
    send = jnp.stack([conc_re, conc_im, wall_re, wall_im], axis=0)
    send = send.transpose(3, 2, 0, 1).reshape(devices, own_j * 4 * local_x)
    got = lax.all_to_all(send, "slab", 0, 0, tiled=True)
    got = got.reshape(devices, own_j, 2, 2, local_x).transpose(2, 1, 0, 4, 3)
    got = got.reshape(2 * own_j, 2 * total_x)
    ones = math.sqrt(total_x * plane)
    place = jnp.stack([position.astype(F32), jnp.float32(ones)])
    inv, spec = pl.pallas_call(
        mixing_kernel,
        name="mixing",
        out_shape=(
            sds((2 * KY * KZ, local_x * channels), BF16),
            sds((2, channels, modes), F32),
        ),
        in_specs=[smem] + vmem(5),
        out_specs=vmem(2),
        scratch_shapes=[
            pltpu.VMEM((local_x * channels // 128, 2 * KY * KZ, 128), F32)
            if own_j > 1
            else pltpu.VMEM((2 * KY * KZ, local_x * channels), F32)
        ],
        compiler_params=params(),
    )(place, got, tab["ax"], tab["bx"], lift, mode_weight.transpose(1, 2, 3, 0))
    inv = lax.all_to_all(inv, "slab", 0, 0, tiled=True)
    rows = local_x * channels
    wide = ZG * 2 * KY
    pred, grad = pl.pallas_call(
        functools.partial(layer_kernel, own_j),
        name="layer",
        out_shape=(
            sds((local_x, half, 2 * depth), F32),
            sds((2 * KY * KZ, rows + 128 * tail_blocks(own_j)), BF16),
        ),
        in_specs=vmem(11),
        out_specs=vmem(2),
        scratch_shapes=[
            pltpu.VMEM((depth // ZG, rows, wide + 32), BF16),
            pltpu.VMEM((rows, ZG * span), BF16),
            pltpu.VMEM((16, ZG * span), BF16),
            pltpu.VMEM((depth // ZG, rows, wide), BF16),
            pltpu.VMEM((local_x, 2 * depth, half), F32),
            pltpu.VMEM((rows, 16), F32),
        ],
        compiler_params=params(),
    )(
        inv, conc_z, cot_z, cover_z, lift, point_weight, point_bias.reshape(1, -1), readout.reshape(1, -1),
        tab["ez"], tab["fwd"], tab["bwd"],
    )
    grad = lax.all_to_all(grad, "slab", 0, 0, tiled=True)
    blocks = 8
    per = channels // blocks
    whole = lambda s: pl.BlockSpec(s, lambda i: (0,) * len(s))
    grad_modes, grad_point = pl.pallas_call(
        functools.partial(outer_kernel, own_j),
        name="outer",
        grid=(blocks,),
        out_shape=(
            sds((2, channels, channels, modes), F32),
            sds((channels, channels), F32),
        ),
        in_specs=[whole(grad.shape), whole(spec.shape), whole(tab["gx"].shape), whole(lift.shape)],
        out_specs=(
            pl.BlockSpec((2, per, channels, modes), lambda i: (0, i, 0, 0)),
            whole((channels, channels)),
        ),
        scratch_shapes=[
            pltpu.VMEM((channels, modes), F32),
            pltpu.VMEM((channels, modes), F32),
            pltpu.VMEM((rows // 128, 2 * KY * KZ, 128), F32),
        ],
        compiler_params=params(),
    )(grad, spec, tab["gx"], lift)
    return (
        conc_out.reshape(local_x, plane),
        cover_out,
        pred.reshape(local_x, plane),
        grad_modes.transpose(3, 0, 1, 2),
        grad_point,
    )


def solution(mesh):
    placed = (
        P(("groups", "slab"), None),
        P(("groups", "slab"), None),
        P(("groups", "slab"), None),
        P(("groups", "slab"), None),
        P(("groups", "slab"), None),
        P("groups", None),
        P("groups"),
        P(),
        P("slab", None, None, None),
        P(),
        P(),
        P(),
        P(("groups", "slab"), None),
    )
    return jax.shard_map(
        body,
        mesh=mesh,
        in_specs=placed,
        out_specs=(
            P(("groups", "slab"), None),
            P(("groups", "slab"), None),
            P(("groups", "slab"), None),
            P(("groups", "slab"), None, None, None),
            P("groups", None),
        ),
        check_vma=False,
    )
```

```python
import functools
import math

import jax
import jax.numpy as jnp
import numpy as np
from jax import lax
from jax.experimental import pallas as pl
from jax.experimental.pallas import tpu as pltpu
from jax.sharding import PartitionSpec as P

KX = 16
KY = 16
KZ = 8
STEPS = 4
PROFILES = 8

PEAK_SPEED = 0.6
DIFFUSIVITY = 0.06
CENTRE = 1.1
ZG = 4

HI = lax.Precision.HIGHEST
F32 = jnp.float32
BF16 = jnp.bfloat16


def dot(a, b, precision=None):
    return jnp.dot(a, b, preferred_element_type=F32, precision=precision)


def dot_nt(a, b, precision=None):
    return lax.dot_general(a, b, (((1,), (1,)), ((), ())), preferred_element_type=F32, precision=precision)


def dot_tn(a, b, precision=None):
    return lax.dot_general(a, b, (((0,), (0,)), ((), ())), preferred_element_type=F32, precision=precision)


def split(table):
    high = table.astype(np.float32).astype(jnp.bfloat16)
    return high, (table - high.astype(np.float64)).astype(np.float32).astype(jnp.bfloat16)


def tables(span, depth, total_x, devices, local_x):
    half = span // 2
    own_j = KY * KZ // devices
    tab = {}
    lane = np.arange(half)
    perm = np.zeros((half, 4 * half), np.float32)
    for h in range(2):
        for par in range(2):
            k = (h * half + lane - par) / 2.0
            good = (k == np.floor(k)) & (k >= 0)
            perm[lane[good], (2 * h + par) * half + k[good].astype(int)] = 1.0
    tab["perm"] = perm
    back = np.zeros((span, span), np.float32)
    for par in range(2):
        back[par * half + lane, 2 * lane + par] = 1.0
    tab["back"] = back
    ky = np.arange(KY)
    kz = np.arange(KZ)
    kx = np.arange(KX)
    y_of = np.concatenate([2 * lane, 2 * lane + 1])
    alpha = 2 * np.pi * ((y_of[:, None] * ky[None, :]) % span) / span
    tab["wave_yt"] = np.concatenate([np.cos(alpha), np.sin(alpha)], axis=1).T.astype(np.float32)
    z = np.arange(depth)
    beta = 2 * np.pi * ((kz[:, None] * z[None, :]) % depth) / depth
    place_c = np.zeros((2, local_x, depth, 2, 2, local_x, KZ), np.float32)
    place_w = np.zeros((2, 8, 2, 2, local_x, KZ), np.float32)
    for i in range(local_x):
        place_c[0, i, :, 0, 0, i] = np.cos(beta).T
        place_c[1, i, :, 0, 0, i] = -np.sin(beta).T
        place_c[0, i, :, 0, 1, i] = -np.sin(beta).T
        place_c[1, i, :, 0, 1, i] = -np.cos(beta).T
        place_w[0, i, 1, 0, i] = 1.0
        place_w[1, i, 1, 1, i] = -1.0
    tab["place_c"] = place_c.reshape(2, local_x * depth, 4 * local_x * KZ)
    tab["place_w"] = place_w.reshape(2, 8, 4 * local_x * KZ)
    pairs = 2 * KY
    ez = np.zeros((2 * KY * KZ, depth, KY, 2), np.float32)
    for j in range(KY * KZ):
        a, b = j // KZ, j % KZ
        row = (j // own_j) * 2 * own_j + j % own_j
        ez[row, :, a, 0] = np.cos(beta[b])
        ez[row + own_j, :, a, 0] = -np.sin(beta[b])
        ez[row, :, a, 1] = -np.sin(beta[b])
        ez[row + own_j, :, a, 1] = -np.cos(beta[b])
    tab["ez"] = ez.reshape(2 * KY * KZ, depth * pairs).astype(jnp.bfloat16)
    by = np.stack([np.cos(alpha), np.sin(alpha)], axis=2).reshape(span, pairs)
    fwd = np.zeros((ZG, ZG * pairs + 16, span), np.float32)
    bwd = np.zeros((ZG, span, ZG * pairs), np.float32)
    for i in range(ZG):
        fwd[i, i * pairs : (i + 1) * pairs] = by.T
        fwd[i, ZG * pairs : ZG * pairs + 2] = 1.0
        bwd[i, :, i * pairs : (i + 1) * pairs] = by
    tab["fwd"] = fwd.astype(jnp.bfloat16)
    tab["bwd"] = bwd.reshape(ZG * span, ZG * pairs).astype(jnp.bfloat16)
    x = np.arange(total_x)
    gamma = 2 * np.pi * ((x[:, None] * kx[None, :]) % total_x) / total_x
    cg, sg = np.cos(gamma), np.sin(gamma)
    scale = 1.0 / math.sqrt(total_x * span * depth)
    ax = np.zeros((total_x, 2, 2, KX))
    ax[:, 0, 0], ax[:, 1, 0] = cg, sg
    ax[:, 0, 1], ax[:, 1, 1] = -sg, cg
    by_owner = ax.reshape(devices, local_x, 2, 2 * KX)
    tab["ax"] = (by_owner.transpose(0, 2, 1, 3) * scale).reshape(devices, -1).astype(np.float32)
    iscale = 1.0 / math.sqrt(KX * KY * KZ)
    bx = np.zeros((total_x, 2, 2, KX))
    bx[:, 0, 0], bx[:, 0, 1] = cg, -sg
    bx[:, 1, 0], bx[:, 1, 1] = sg, cg
    bx = bx.reshape(devices, local_x, 2, 2 * KX).transpose(1, 0, 2, 3) * iscale
    tab["bx"] = np.stack(split(bx.reshape(2 * total_x, 2 * KX)))
    gx = by_owner.transpose(3, 1, 0, 2).reshape(2 * KX, 2 * total_x)
    tab["gx"] = np.concatenate(split(gx), axis=0)
    return tab


def pack_kernel(conc, cover, rate_on, rate_off, mask, packed, conc_out, walls_out):
    local_x = conc.shape[0]
    half = conc_out.shape[1]
    for k in range(half):
        conc_out[:, k, :] = conc[:, k * 128 : (k + 1) * 128]
    for f, ref in enumerate((cover, rate_on, rate_off, mask)):
        for h in range(2):
            walls_out[:, h * 4 + f, :] = ref[:, h * half : (h + 1) * half].astype(F32)
    for x in range(local_x):
        packed[x, :half, :] = (conc_out[x] - CENTRE).astype(BF16)
        tail = jnp.concatenate([walls_out[x], jnp.zeros((8, half), F32)], axis=0)
        packed[x, half:, :] = tail.astype(BF16)


def prepare_kernel(cot, lift, weight, cot_z, mapped, flat):
    local_x = cot.shape[0]
    half = flat.shape[1]
    for k in range(half):
        flat[:, k, :] = cot[:, k * 128 : (k + 1) * 128]
    for x in range(local_x):
        cot_z[:, x, :] = flat[x].T
    channels = weight.shape[1]
    for p in range(2):
        acc = [jnp.zeros(weight.shape[2:], F32) for _ in range(3)]
        for c in range(channels):
            w = weight[p, c].astype(F32)
            acc = [acc[r] + lift[r, c] * w for r in range(3)]
        for r in range(3):
            mapped[r, p] = acc[r]


def transport_kernel(
    flags, own, own_walls, up, down, index, profiles, perm, back, wave_yt, place_c, place_w,
    conc_out, cover_out, conc_z, cover_z, send, buf,
):
    local_x = own.shape[0]
    half = own.shape[1]
    depth = profiles.shape[1]
    rows = 3 * local_x
    walls = []
    for r in range(rows):
        x = r % local_x
        if r // local_x == 1:
            buf[0, r] = own[x].T
            walls.append(own_walls[x])
        else:
            ref = up if r < local_x else down
            buf[0, r] = (ref[x, :half, :].astype(F32) + CENTRE).T
            walls.append(ref[x, half:, :].astype(F32)[:8])
    walls.append(jnp.concatenate([index[...], jnp.zeros((6, half), F32)], axis=0))
    spread = dot(jnp.concatenate(walls, axis=0), perm[...], HI)
    fields = [
        spread[8 * r : 8 * r + 4, : 2 * half] + spread[8 * r + 4 : 8 * r + 8, 2 * half :]
        for r in range(rows)
    ]
    chosen = spread[8 * rows : 8 * rows + 1, : 2 * half] + spread[8 * rows + 1 : 8 * rows + 2, 2 * half :]
    pick = lax.broadcasted_iota(jnp.int32, (PROFILES, 2 * half), 0).astype(F32)
    onehot = (jnp.abs(pick - chosen) < 0.5).astype(F32)
    inlet = dot_tn(profiles[...], onehot, HI)
    inlet = jnp.concatenate([inlet[:, :half], inlet[:, half:]], axis=0)
    height = lax.broadcasted_iota(jnp.int32, (depth, half), 0).astype(F32)
    height = (height + 0.5) / depth
    speed = PEAK_SPEED * 4.0 * height * (1.0 - height)
    speed = jnp.concatenate([speed, speed], axis=0)
    first = flags[0] == 1
    last = flags[1] == 1
    cover = [f[0:1] for f in fields]
    for step in range(STEPS):
        cur, nxt = step % 2, (step + 1) % 2
        for r in range(1 + step, rows - 1 - step):
            c = buf[cur, r]
            behind = buf[cur, r - 1]
            ahead = buf[cur, r + 1]
            if r == local_x:
                behind = jnp.where(first, inlet, behind)
            if r == 2 * local_x - 1:
                ahead = jnp.where(last, c, ahead)
            even, odd = c[:depth], c[depth:]
            side = jnp.concatenate(
                [odd + pltpu.roll(odd, 1, 1), even + pltpu.roll(even, half - 1, 1)], axis=0
            )
            below = jnp.concatenate([even[:1], even[:-1], odd[:1], odd[:-1]], axis=0)
            above = jnp.concatenate([even[1:], even[-1:], odd[1:], odd[-1:]], axis=0)
            laplace = behind + ahead + side + below + above - 6.0 * c
            f = fields[r]
            wall = jnp.concatenate([even[:1], odd[:1]], axis=1)
            uptake = f[3:4] * (f[1:2] * wall * (1.0 - cover[r]) - f[2:3] * cover[r])
            new = c + DIFFUSIVITY * laplace - speed * (c - behind)
            buf[nxt, r] = new
            buf[nxt, r, 0:1] = new[0:1] - uptake[:, :half]
            buf[nxt, r, depth : depth + 1] = new[depth : depth + 1] - uptake[:, half:]
            cover[r] = cover[r] + uptake
    cur = STEPS % 2
    covers = jnp.concatenate(cover[local_x : 2 * local_x], axis=0)
    cover_z[...] = covers
    planes = [buf[cur, local_x + i] for i in range(local_x)]
    evens = jnp.concatenate([p[:depth] for p in planes], axis=0)
    odds = jnp.concatenate([p[depth:] for p in planes], axis=0)
    along = dot_nt(wave_yt[:, :half], evens, HI) + dot_nt(wave_yt[:, half:], odds, HI)
    padded = jnp.concatenate([covers, jnp.zeros((8 - local_x, 2 * half), F32)], axis=0)
    walls_y = dot_nt(wave_yt[...], padded, HI)
    send[...] = (
        dot(along[:KY], place_c[0], HI)
        + dot(along[KY:], place_c[1], HI)
        + dot(walls_y[:KY], place_w[0], HI)
        + dot(walls_y[KY:], place_w[1], HI)
    )
    cover_out[...] = dot(covers, back[...], HI)
    for i in range(local_x):
        conc_out[i] = planes[i].T
        conc_z[:, i, :] = planes[i]


def mixing_kernel(place, got, ax, bx, mapped, inv_out, spec_out, stage):
    modes = mapped.shape[3]
    channels = mapped.shape[2]
    own_j = modes // KX
    local_x = inv_out.shape[1] // channels
    blocks = inv_out.shape[0] // own_j
    spread = dot_tn(got[...], ax[...], HI)
    keep = lax.broadcasted_iota(jnp.int32, (own_j, modes), 1) // KX == lax.broadcasted_iota(
        jnp.int32, (own_j, modes), 0
    )
    spec = []
    for f in range(2):
        acc = jnp.zeros((own_j, 2 * KX), F32)
        for k in range(2 * local_x):
            at = (f * 2 * local_x + k) * own_j
            acc = acc + spread[at : at + own_j, k * 2 * KX : (k + 1) * 2 * KX]
        for q in range(2):
            tiled = jnp.concatenate([acc[:, q * KX : (q + 1) * KX]] * own_j, axis=1)
            spec.append(jnp.sum(jnp.where(keep, tiled, 0.0), axis=0, keepdims=True))
    cr, ci, wr, wi = spec
    lane = lax.broadcasted_iota(jnp.int32, (1, modes), 1)
    ones = jnp.where((lane == 0) & (place[0] == 0.0), place[1], 0.0)
    zero = jnp.zeros((1, modes), F32)
    spec_out[:, :modes] = jnp.concatenate([cr, wr, ones] + [zero] * 5, axis=0)
    spec_out[:, modes:] = jnp.concatenate([ci, wi] + [zero] * 6, axis=0)
    mixed_r = cr * mapped[0, 0] - ci * mapped[0, 1] + wr * mapped[1, 0] - wi * mapped[1, 1] + ones * mapped[2, 0]
    mixed_i = cr * mapped[0, 1] + ci * mapped[0, 0] + wr * mapped[1, 1] + wi * mapped[1, 0] + ones * mapped[2, 1]
    mixed_r = mixed_r.astype(BF16).astype(F32).T
    mixed_i = mixed_i.astype(BF16).astype(F32).T
    for j in range(own_j):
        rhs = jnp.concatenate([mixed_r[j * KX : (j + 1) * KX], mixed_i[j * KX : (j + 1) * KX]], axis=0)
        rhs = rhs.astype(BF16)
        out = dot(bx[0], rhs) + dot(bx[1], rhs)
        line = jnp.concatenate([out[i * blocks : (i + 1) * blocks] for i in range(local_x)], axis=1)
        for h in range(line.shape[1] // 128):
            if own_j == 1:
                stage[h] = line[:, h * 128 : (h + 1) * 128]
            else:
                stage[h, pl.ds(j, blocks, own_j), :] = line[:, h * 128 : (h + 1) * 128]
    for h in range(stage.shape[0]):
        inv_out[:, h * 128 : (h + 1) * 128] = stage[h].astype(BF16)


def tail_blocks(own_j):
    return -(-3 // (2 * own_j))


def layer_kernel(
    own_j, inv, conc_z, cot_z, cover_z, lift, point_weight, bias, readout, ez, fwd, bwd,
    pred_out, grad_out, lhs, grads_a, grads_b, ext_a, ext_b, waves, pred, point, ahead,
):
    channels = lift.shape[1]
    local_x = cover_z.shape[0]
    half = cot_z.shape[2]
    span = 2 * half
    depth = cot_z.shape[0] // 2
    groups = depth // ZG
    rows = local_x * channels
    wide = ZG * 2 * KY
    iscale = 1.0 / math.sqrt(KX * KY * KZ)
    c1 = math.sqrt(2.0 / math.pi)
    unit = (c1 * 0.044715) ** (1.0 / 3.0)
    kappa = c1 / unit

    def high(v):
        return v.astype(BF16).astype(F32)

    factors = jnp.concatenate([lift[...], jnp.zeros((5, channels), F32)], axis=0)
    mapped = dot_nt(point_weight[...].astype(F32), factors, HI)
    eye = (
        lax.broadcasted_iota(jnp.int32, (channels, channels), 0)
        == lax.broadcasted_iota(jnp.int32, (channels, channels), 1)
    ).astype(F32)
    columns = dot_nt(eye, jnp.concatenate([bias[...], readout[...], jnp.zeros((6, channels), F32)], axis=0), HI)
    a0, a1 = unit * mapped[:, 0:1], unit * mapped[:, 1:2]
    a2 = unit * (mapped[:, 2:3] + columns[:, 0:1]) + CENTRE * a0
    half_readout = 0.5 * columns[:, 1:2]

    lane = lax.broadcasted_iota(jnp.int32, (channels, 32), 1)
    a0_high, a2_high = high(a0), high(a2)
    for x in range(local_x):
        block = jnp.zeros((channels, 32), F32)
        for at, value in (
            (0, a2_high), (1, a2 - a2_high),
            (16 + x, a0_high), (20 + x, a0_high), (24 + x, a0 - a0_high), (28 + x, a1),
        ):
            block = jnp.where(lane == at, value, block)
        block = block.astype(BF16)
        for g in range(groups):
            lhs[g, x * channels : (x + 1) * channels, wide : wide + 32] = block
    flipped = inv[...].astype(F32).T.astype(BF16)
    lifted = (unit * dot(flipped, ez[...])).astype(BF16)
    for g in range(groups):
        lhs[g, :, :wide] = lifted[:, g * wide : (g + 1) * wide]
    wide_readout = jnp.concatenate([(0.5 / unit) * readout[...]] * local_x, axis=1)
    owner = lax.broadcasted_iota(jnp.int32, (16, rows), 1) // channels
    slot = lax.broadcasted_iota(jnp.int32, (16, rows), 0)
    readout_high = high(wide_readout)
    weigh = jnp.where(
        slot == owner, readout_high, jnp.where(slot - 8 == owner, wide_readout - readout_high, 0.0)
    ).astype(BF16)
    point[...] = jnp.zeros(point.shape, F32)
    grads_b[...] = jnp.zeros(grads_b.shape, BF16)
    ext_b[...] = jnp.zeros(ext_b.shape, BF16)

    def before(g, i, ext_ref):
        z = g * ZG + i
        conc = jnp.concatenate([conc_z[z], conc_z[depth + z]], axis=1) - CENTRE
        conc_high = high(conc)
        wall = jnp.where(z == 0, cover_z[...], 0.0)
        ext = jnp.concatenate([conc_high, conc - conc_high, conc_high, wall], axis=0).astype(BF16)
        ext_ref[:, i * span : (i + 1) * span] = ext
        return dot(lhs[g], jnp.concatenate([fwd[i], ext], axis=0))

    def collect(at, grads, ext):
        waves[:, pl.ds(pl.multiple_of(at * wide, wide), wide)] = dot(grads[...], bwd[...]).astype(BF16)
        point[...] += dot_nt(grads[...], ext[...])

    def group(g, grads, ext, grads_other, ext_other):
        collect(jnp.maximum(g - 1, 0), grads_other, ext_other)
        for i in range(ZG):
            pre = ahead[...] if i == 0 else nxt
            if i < ZG - 1:
                nxt = before(g, i + 1, ext)
            else:
                nxt = before(jnp.minimum(g + 1, groups - 1), 0, ext_other)
            z = g * ZG + i
            cot = jnp.concatenate([cot_z[z], cot_z[depth + z]], axis=1)
            hidden = []
            for x in range(local_x):
                y = pre[x * channels : (x + 1) * channels]
                p = y * y + kappa
                t = jnp.tanh(y * p)
                s = 1.0 + t
                hidden.append((y * s).astype(BF16))
                slope = y * (3.0 * p - 2.0 * kappa)
                grad = s * (1.0 + slope * (1.0 - t)) * cot[x : x + 1]
                grads[x * channels : (x + 1) * channels, i * span : (i + 1) * span] = grad.astype(BF16)
            line = dot(weigh, jnp.concatenate(hidden, axis=0))
            line = line[:local_x] + line[8 : 8 + local_x]
            pred[z] = line[:, :half]
            pred[depth + z] = line[:, half:]
        ahead[...] = nxt

    ahead[...] = before(0, 0, ext_a)

    def pair(h, carry):
        group(2 * h, grads_a, ext_a, grads_b, ext_b)
        group(2 * h + 1, grads_b, ext_b, grads_a, ext_a)
        return carry

    lax.fori_loop(0, groups // 2, pair, 0)
    collect(groups - 1, grads_b, ext_b)
    for x in range(local_x):
        pred_out[x] = pred[:, x, :].T
    total = dot_nt(waves[...], ez[...])
    lane16 = lax.broadcasted_iota(jnp.int32, (channels, 16), 1)
    lane128 = lax.broadcasted_iota(jnp.int32, (channels, 128), 1)
    cols = []
    sums = jnp.zeros((channels, 128), F32)
    for x in range(local_x):
        here = slice(x * channels, (x + 1) * channels)
        pt = point[here, :]
        with_conc = jnp.sum(jnp.where((lane16 == x) | (lane16 == 4 + x), pt, 0.0), axis=1, keepdims=True)
        with_wall = jnp.sum(jnp.where(lane16 == 12 + x, pt, 0.0), axis=1, keepdims=True)
        alone = total[here, 0:1]
        sums = sums + jnp.where(
            lane128 == 0, with_conc, jnp.where(lane128 == 1, with_wall, jnp.where(lane128 == 2, alone, 0.0))
        )
        cols.append((iscale * half_readout) * total[here])
    sums = (half_readout * sums).T[:16]
    sums_high = high(sums)
    both = jnp.concatenate([sums_high, sums - sums_high], axis=1).astype(BF16)
    out_rows = grad_out.shape[0]
    grad_out[:, :rows] = jnp.concatenate(cols, axis=0).T.astype(BF16)
    for b in range(tail_blocks(own_j)):
        row = lax.broadcasted_iota(jnp.int32, (out_rows, 16), 0) % (2 * own_j) + b * 2 * own_j
        pick = (row == lax.broadcasted_iota(jnp.int32, (out_rows, 16), 1)).astype(BF16)
        grad_out[:, rows + b * 128 : rows + (b + 1) * 128] = dot(pick, both).astype(BF16)


def outer_kernel(own_j, got, spec, gx, lift, modes_out, point_out, v_r, v_i, d_r, d_i, stage):
    channels = lift.shape[1]
    modes = spec.shape[1] // 2
    rows = got.shape[1] - 128 * tail_blocks(own_j)
    local_x = rows // channels
    per = modes_out.shape[1]

    @pl.when(pl.program_id(0) == 0)
    def _():
        factors = jnp.concatenate([lift[...], jnp.zeros((5, channels), F32)], axis=0)
        v = dot_tn(factors, spec[...], HI)
        v_r[...] = v[:, :modes]
        v_i[...] = v[:, modes:]
        blocks = got.shape[0] // own_j
        halves = rows // 128
        for h in range(halves):
            stage[h] = got[:, h * 128 : (h + 1) * 128].astype(F32)
        lines = [
            [stage[h, pl.ds(j, blocks, own_j), :] if own_j > 1 else stage[h] for h in range(halves)]
            for j in range(own_j)
        ]
        per_half = 128 // channels
        parts_r, parts_i = [], []
        tall = []
        for x in range(local_x):
            h, at = x // per_half, (x % per_half) * channels
            tall.append(jnp.concatenate([lines[j][h][:, at : at + channels] for j in range(own_j)], axis=1))
        acc = dot(gx[...], jnp.concatenate(tall, axis=0).astype(BF16))
        acc = acc[: 2 * KX] + acc[2 * KX :]
        for j in range(own_j):
            parts_r.append(acc[:KX, j * channels : (j + 1) * channels])
            parts_i.append(acc[KX:, j * channels : (j + 1) * channels])
        d_r[...] = jnp.concatenate(parts_r, axis=0).T
        d_i[...] = jnp.concatenate(parts_i, axis=0).T
        sums = jnp.zeros((8, 128), F32)
        for b in range(tail_blocks(own_j)):
            tail = got[:, rows + b * 128 : rows + (b + 1) * 128]
            at = lax.broadcasted_iota(jnp.int32, (8, got.shape[0]), 1) % (2 * own_j) + b * 2 * own_j
            pick = (at == lax.broadcasted_iota(jnp.int32, (8, got.shape[0]), 0)).astype(BF16)
            sums = sums + dot(pick, tail)
        sums = sums[:, :channels] + sums[:, channels:]
        row = lax.broadcasted_iota(jnp.int32, (8, channels), 0)
        base = jnp.where(row == 2, factors + CENTRE * lift[0:1], factors)
        point_out[...] = dot_tn(jnp.where(row < 3, sums, 0.0), base, HI)

    start = pl.program_id(0) * per
    dr = d_r[...]
    di = d_i[...]
    for c in range(per):
        vr = v_r[pl.ds(start + c, 1), :]
        vi = v_i[pl.ds(start + c, 1), :]
        modes_out[0, c] = vr * dr + vi * di
        modes_out[1, c] = vr * di - vi * dr


def params(**kw):
    return pltpu.CompilerParams(vmem_limit_bytes=56 * 1024 * 1024, **kw)


def vmem(count):
    return [pl.BlockSpec(memory_space=pltpu.VMEM) for _ in range(count)]


def body(
    conc_init, cover_init, rate_on, rate_off, site_mask, inlet_profiles, inlet_index, lift,
    mode_weight, point_weight, point_bias, readout, cotangent,
):
    devices = lax.axis_size("slab")
    position = lax.axis_index("slab")
    local_x, plane = conc_init.shape
    depth = inlet_profiles.shape[1]
    span = plane // depth
    half = span // 2
    channels = lift.shape[1]
    modes = mode_weight.shape[0]
    own_j = modes // KX
    total_x = local_x * devices
    tab = {k: jnp.asarray(v) for k, v in tables(span, depth, total_x, devices, local_x).items()}
    sds = jax.ShapeDtypeStruct
    smem = pl.BlockSpec(memory_space=pltpu.SMEM)

    pack, conc, walls = pl.pallas_call(
        pack_kernel,
        name="pack",
        out_shape=(
            sds((local_x, half + 16, 2 * depth), BF16),
            sds((local_x, half, 2 * depth), F32),
            sds((local_x, 8, half), F32),
        ),
        in_specs=vmem(5),
        out_specs=vmem(3),
        compiler_params=params(),
    )(conc_init, cover_init, rate_on, rate_off, site_mask)
    up = lax.ppermute(pack, "slab", [(i, i + 1) for i in range(devices - 1)])
    down = lax.ppermute(pack, "slab", [(i + 1, i) for i in range(devices - 1)])
    cot_z, mapped = pl.pallas_call(
        prepare_kernel,
        name="prepare",
        out_shape=(
            sds((2 * depth, local_x, half), F32),
            sds((3, 2, channels, modes), F32),
        ),
        in_specs=vmem(1) + [smem] + vmem(1),
        out_specs=vmem(2),
        scratch_shapes=[pltpu.VMEM((local_x, half, 2 * depth), F32)],
        compiler_params=params(),
    )(cotangent, lift, mode_weight.transpose(1, 2, 3, 0))
    flags = jnp.stack([position == 0, position == devices - 1]).astype(jnp.int32)
    index = inlet_index.astype(F32).reshape(2, half)
    conc_out, cover_out, conc_z, cover_z, send = pl.pallas_call(
        transport_kernel,
        name="transport",
        out_shape=(
            sds((local_x, half, 2 * depth), F32),
            sds((local_x, span), F32),
            sds((2 * depth, local_x, half), F32),
            sds((local_x, span), F32),
            sds((KY, 4 * local_x * KZ), F32),
        ),
        in_specs=[smem] + vmem(11),
        out_specs=vmem(5),
        scratch_shapes=[pltpu.VMEM((2, 3 * local_x, 2 * depth, half), F32)],
        compiler_params=params(),
    )(
        flags, conc, walls, up, down, index, inlet_profiles,
        tab["perm"], tab["back"], tab["wave_yt"], tab["place_c"], tab["place_w"],
    )
    if own_j != KZ:
        send = send.reshape(KY, 4 * local_x, KZ // own_j, own_j).transpose(0, 2, 1, 3)
        send = send.reshape(devices, 4 * local_x * own_j)
    got = lax.all_to_all(send, "slab", 0, 0, tiled=True)
    ones = math.sqrt(total_x * plane)
    place = jnp.stack([position.astype(F32), jnp.float32(ones)])
    inv, spec = pl.pallas_call(
        mixing_kernel,
        name="mixing",
        out_shape=(
            sds((2 * KY * KZ, local_x * channels), BF16),
            sds((8, 2 * modes), F32),
        ),
        in_specs=[smem] + vmem(4),
        out_specs=vmem(2),
        scratch_shapes=[pltpu.VMEM((local_x * channels // 128, 2 * KY * KZ, 128), F32)],
        compiler_params=params(),
    )(place, got, tab["ax"], tab["bx"], mapped)
    inv = lax.all_to_all(inv, "slab", 0, 0, tiled=True)
    rows = local_x * channels
    wide = ZG * 2 * KY
    pred, grad = pl.pallas_call(
        functools.partial(layer_kernel, own_j),
        name="layer",
        out_shape=(
            sds((local_x, half, 2 * depth), F32),
            sds((2 * KY * KZ, rows + 128 * tail_blocks(own_j)), BF16),
        ),
        in_specs=vmem(11),
        out_specs=vmem(2),
        scratch_shapes=[
            pltpu.VMEM((depth // ZG, rows, wide + 32), BF16),
            pltpu.VMEM((rows, ZG * span), BF16),
            pltpu.VMEM((rows, ZG * span), BF16),
            pltpu.VMEM((16, ZG * span), BF16),
            pltpu.VMEM((16, ZG * span), BF16),
            pltpu.VMEM((rows, depth * 2 * KY), BF16),
            pltpu.VMEM((2 * depth, local_x, half), F32),
            pltpu.VMEM((rows, 16), F32),
            pltpu.VMEM((rows, span), F32),
        ],
        compiler_params=params(),
    )(
        inv, conc_z, cot_z, cover_z, lift, point_weight, point_bias.reshape(1, -1), readout.reshape(1, -1),
        tab["ez"], tab["fwd"], tab["bwd"],
    )
    grad = lax.all_to_all(grad, "slab", 0, 0, tiled=True)
    blocks = 8
    per = channels // blocks
    whole = lambda s: pl.BlockSpec(s, lambda i: (0,) * len(s))
    grad_modes, grad_point = pl.pallas_call(
        functools.partial(outer_kernel, own_j),
        name="outer",
        grid=(blocks,),
        out_shape=(
            sds((2, channels, channels, modes), F32),
            sds((channels, channels), F32),
        ),
        in_specs=[whole(grad.shape), whole(spec.shape), whole(tab["gx"].shape), whole(lift.shape)],
        out_specs=(
            pl.BlockSpec((2, per, channels, modes), lambda i: (0, i, 0, 0)),
            whole((channels, channels)),
        ),
        scratch_shapes=[
            pltpu.VMEM((channels, modes), F32),
            pltpu.VMEM((channels, modes), F32),
            pltpu.VMEM((channels, modes), F32),
            pltpu.VMEM((channels, modes), F32),
            pltpu.VMEM((rows // 128, 2 * KY * KZ, 128), F32),
        ],
        compiler_params=params(),
    )(grad, spec, tab["gx"], lift)
    return (
        conc_out.reshape(local_x, plane),
        cover_out,
        pred.reshape(local_x, plane),
        grad_modes.transpose(3, 0, 1, 2),
        grad_point,
    )


def solution(mesh):
    placed = (
        P(("groups", "slab"), None),
        P(("groups", "slab"), None),
        P(("groups", "slab"), None),
        P(("groups", "slab"), None),
        P(("groups", "slab"), None),
        P("groups", None),
        P("groups"),
        P(),
        P("slab", None, None, None),
        P(),
        P(),
        P(),
        P(("groups", "slab"), None),
    )
    return jax.shard_map(
        body,
        mesh=mesh,
        in_specs=placed,
        out_specs=(
            P(("groups", "slab"), None),
            P(("groups", "slab"), None),
            P(("groups", "slab"), None),
            P(("groups", "slab"), None, None, None),
            P("groups", None),
        ),
        check_vma=False,
    )
```

```python
import functools
import math

import jax
import jax.numpy as jnp
import numpy as np
from jax import lax
from jax.experimental import pallas as pl
from jax.experimental.pallas import tpu as pltpu
from jax.sharding import PartitionSpec as P

KX = 16
KY = 16
KZ = 8
STEPS = 4
PROFILES = 8

PEAK_SPEED = 0.6
DIFFUSIVITY = 0.06
CENTRE = 1.1
ZG = 4

HI = lax.Precision.HIGHEST
F32 = jnp.float32
BF16 = jnp.bfloat16


def dot(a, b, precision=None):
    return jnp.dot(a, b, preferred_element_type=F32, precision=precision)


def dot_nt(a, b, precision=None):
    return lax.dot_general(a, b, (((1,), (1,)), ((), ())), preferred_element_type=F32, precision=precision)


def dot_tn(a, b, precision=None):
    return lax.dot_general(a, b, (((0,), (0,)), ((), ())), preferred_element_type=F32, precision=precision)


def split(table):
    high = table.astype(np.float32).astype(jnp.bfloat16)
    return high, (table - high.astype(np.float64)).astype(np.float32).astype(jnp.bfloat16)


def tables(span, depth, total_x, devices, local_x):
    half = span // 2
    own_j = KY * KZ // devices
    tab = {}
    lane = np.arange(half)
    perm = np.zeros((half, 4 * half), np.float32)
    for h in range(2):
        for par in range(2):
            k = (h * half + lane - par) / 2.0
            good = (k == np.floor(k)) & (k >= 0)
            perm[lane[good], (2 * h + par) * half + k[good].astype(int)] = 1.0
    tab["perm"] = perm
    back = np.zeros((span, span), np.float32)
    for par in range(2):
        back[par * half + lane, 2 * lane + par] = 1.0
    tab["back"] = back
    ky = np.arange(KY)
    kz = np.arange(KZ)
    kx = np.arange(KX)
    y_of = np.concatenate([2 * lane, 2 * lane + 1])
    alpha = 2 * np.pi * ((y_of[:, None] * ky[None, :]) % span) / span
    tab["wave_yt"] = np.concatenate([np.cos(alpha), np.sin(alpha)], axis=1).T.astype(np.float32)
    z = np.arange(depth)
    beta = 2 * np.pi * ((kz[:, None] * z[None, :]) % depth) / depth
    place_c = np.zeros((2, local_x, depth, 2, 2, local_x, KZ), np.float32)
    place_w = np.zeros((2, 8, 2, 2, local_x, KZ), np.float32)
    for i in range(local_x):
        place_c[0, i, :, 0, 0, i] = np.cos(beta).T
        place_c[1, i, :, 0, 0, i] = -np.sin(beta).T
        place_c[0, i, :, 0, 1, i] = -np.sin(beta).T
        place_c[1, i, :, 0, 1, i] = -np.cos(beta).T
        place_w[0, i, 1, 0, i] = 1.0
        place_w[1, i, 1, 1, i] = -1.0
    tab["place_c"] = place_c.reshape(2, local_x * depth, 4 * local_x * KZ)
    tab["place_w"] = place_w.reshape(2, 8, 4 * local_x * KZ)
    pairs = 2 * KY
    ez = np.zeros((2 * KY * KZ, depth, KY, 2), np.float32)
    for j in range(KY * KZ):
        a, b = j // KZ, j % KZ
        row = (j // own_j) * 2 * own_j + j % own_j
        ez[row, :, a, 0] = np.cos(beta[b])
        ez[row + own_j, :, a, 0] = -np.sin(beta[b])
        ez[row, :, a, 1] = -np.sin(beta[b])
        ez[row + own_j, :, a, 1] = -np.cos(beta[b])
    tab["ez"] = ez.reshape(2 * KY * KZ, depth * pairs).astype(jnp.bfloat16)
    by = np.stack([np.cos(alpha), np.sin(alpha)], axis=2).reshape(span, pairs)
    fwd = np.zeros((ZG, ZG * pairs + 16, span), np.float32)
    for i in range(ZG):
        fwd[i, i * pairs : (i + 1) * pairs] = by.T
        fwd[i, ZG * pairs : ZG * pairs + 2] = 1.0
    tab["fwd"] = fwd.astype(jnp.bfloat16)
    x = np.arange(total_x)
    gamma = 2 * np.pi * ((x[:, None] * kx[None, :]) % total_x) / total_x
    cg, sg = np.cos(gamma), np.sin(gamma)
    scale = 1.0 / math.sqrt(total_x * span * depth)
    ax = np.zeros((total_x, 2, 2, KX))
    ax[:, 0, 0], ax[:, 1, 0] = cg, sg
    ax[:, 0, 1], ax[:, 1, 1] = -sg, cg
    by_owner = ax.reshape(devices, local_x, 2, 2 * KX)
    tab["ax"] = (by_owner.transpose(0, 2, 1, 3) * scale).reshape(devices, -1).astype(np.float32)
    iscale = 1.0 / math.sqrt(KX * KY * KZ)
    bx = np.zeros((total_x, 2, 2, KX))
    bx[:, 0, 0], bx[:, 0, 1] = cg, -sg
    bx[:, 1, 0], bx[:, 1, 1] = sg, cg
    bx = bx.reshape(devices, local_x, 2, 2 * KX).transpose(1, 0, 2, 3) * iscale
    tab["bx"] = np.stack(split(bx.reshape(2 * total_x, 2 * KX)))
    gx = by_owner.transpose(3, 1, 0, 2).reshape(2 * KX, 2 * total_x)
    tab["gx"] = np.concatenate(split(gx), axis=0)
    return tab


def pack_kernel(
    conc_hbm, cover_hbm, on_hbm, off_hbm, mask_hbm, packed, conc_out, walls_out,
    conc, cover, rate_on, rate_off, mask, sems,
):
    pairs = ((cover_hbm, cover), (on_hbm, rate_on), (off_hbm, rate_off), (mask_hbm, mask), (conc_hbm, conc))
    copies = [pltpu.make_async_copy(src, dst, sems.at[k]) for k, (src, dst) in enumerate(pairs)]
    for copy in copies:
        copy.start()
    for copy in copies:
        copy.wait()
    local_x = conc.shape[0]
    half = conc_out.shape[1]
    for k in range(half):
        conc_out[:, k, :] = conc[:, k * 128 : (k + 1) * 128]
    for f, ref in enumerate((cover, rate_on, rate_off, mask)):
        for h in range(2):
            walls_out[:, h * 4 + f, :] = ref[:, h * half : (h + 1) * half].astype(F32)
    for x in range(local_x):
        packed[x, :half, :] = (conc_out[x] - CENTRE).astype(BF16)
        tail = jnp.concatenate([walls_out[x], jnp.zeros((8, half), F32)], axis=0)
        packed[x, half:, :] = tail.astype(BF16)


def prepare_kernel(cot_hbm, lift, weight_hbm, cot_z, mapped, flat, cot, weight, sems):
    cot_copy = pltpu.make_async_copy(cot_hbm, cot, sems.at[0])
    halves = [pltpu.make_async_copy(weight_hbm.at[p], weight.at[p], sems.at[1 + p]) for p in range(2)]
    for copy in (cot_copy, *halves):
        copy.start()
    cot_copy.wait()
    local_x = cot.shape[0]
    half = flat.shape[1]
    for k in range(half):
        flat[:, k, :] = cot[:, k * 128 : (k + 1) * 128]
    for x in range(local_x):
        cot_z[:, x, :] = flat[x].T
    channels = weight.shape[1]
    for p in range(2):
        halves[p].wait()
        acc = [jnp.zeros(weight.shape[2:], F32) for _ in range(3)]
        for c in range(channels):
            w = weight[p, c].astype(F32)
            acc = [acc[r] + lift[r, c] * w for r in range(3)]
        for r in range(3):
            mapped[r, p] = acc[r]


def transport_kernel(
    devices, own, own_walls, up, down, index_hbm, profiles_hbm, perm_hbm, back_hbm, wave_hbm, place_c_hbm, place_w_hbm,
    conc_out, cover_out, conc_z, cover_z, send,
    buf, index, profiles, perm, back, wave_yt, place_c, place_w, sems,
):
    moves = (
        (index_hbm, index), (perm_hbm, perm), (profiles_hbm, profiles), (wave_hbm, wave_yt),
        (place_c_hbm, place_c), (place_w_hbm, place_w), (back_hbm, back),
    )
    copies = [pltpu.make_async_copy(src, dst, sems.at[k]) for k, (src, dst) in enumerate(moves)]
    for copy in copies:
        copy.start()
    local_x = own.shape[0]
    half = own.shape[1]
    depth = profiles.shape[1]
    rows = 3 * local_x
    walls = []
    for r in range(rows):
        x = r % local_x
        if r // local_x == 1:
            buf[0, r] = own[x].T
            walls.append(own_walls[x])
        else:
            ref = up if r < local_x else down
            buf[0, r] = (ref[x, :half, :].astype(F32) + CENTRE).T
            walls.append(ref[x, half:, :].astype(F32)[:8])
    for copy in copies[:3]:
        copy.wait()
    profile = index[...].astype(F32)
    walls.append(jnp.concatenate([profile[:, :half], profile[:, half:], jnp.zeros((6, half), F32)], axis=0))
    spread = dot(jnp.concatenate(walls, axis=0), perm[...], HI)
    fields = [
        spread[8 * r : 8 * r + 4, : 2 * half] + spread[8 * r + 4 : 8 * r + 8, 2 * half :]
        for r in range(rows)
    ]
    chosen = spread[8 * rows : 8 * rows + 1, : 2 * half] + spread[8 * rows + 1 : 8 * rows + 2, 2 * half :]
    pick = lax.broadcasted_iota(jnp.int32, (PROFILES, 2 * half), 0).astype(F32)
    onehot = (jnp.abs(pick - chosen) < 0.5).astype(F32)
    inlet = dot_tn(profiles[...], onehot, HI)
    inlet = jnp.concatenate([inlet[:, :half], inlet[:, half:]], axis=0)
    height = lax.broadcasted_iota(jnp.int32, (depth, half), 0).astype(F32)
    height = (height + 0.5) / depth
    speed = PEAK_SPEED * 4.0 * height * (1.0 - height)
    speed = jnp.concatenate([speed, speed], axis=0)
    first = lax.axis_index("slab") == 0
    last = lax.axis_index("slab") == devices - 1
    cover = [f[0:1] for f in fields]
    for step in range(STEPS):
        cur, nxt = step % 2, (step + 1) % 2
        for r in range(1 + step, rows - 1 - step):
            c = buf[cur, r]
            behind = buf[cur, r - 1]
            ahead = buf[cur, r + 1]
            if r == local_x:
                behind = jnp.where(first, inlet, behind)
            if r == 2 * local_x - 1:
                ahead = jnp.where(last, c, ahead)
            even, odd = c[:depth], c[depth:]
            side = jnp.concatenate(
                [odd + pltpu.roll(odd, 1, 1), even + pltpu.roll(even, half - 1, 1)], axis=0
            )
            below = jnp.concatenate([even[:1], even[:-1], odd[:1], odd[:-1]], axis=0)
            above = jnp.concatenate([even[1:], even[-1:], odd[1:], odd[-1:]], axis=0)
            laplace = behind + ahead + side + below + above - 6.0 * c
            f = fields[r]
            wall = jnp.concatenate([even[:1], odd[:1]], axis=1)
            uptake = f[3:4] * (f[1:2] * wall * (1.0 - cover[r]) - f[2:3] * cover[r])
            new = c + DIFFUSIVITY * laplace - speed * (c - behind)
            buf[nxt, r] = new
            buf[nxt, r, 0:1] = new[0:1] - uptake[:, :half]
            buf[nxt, r, depth : depth + 1] = new[depth : depth + 1] - uptake[:, half:]
            cover[r] = cover[r] + uptake
    for copy in copies[3:]:
        copy.wait()
    cur = STEPS % 2
    covers = jnp.concatenate(cover[local_x : 2 * local_x], axis=0)
    cover_z[...] = covers
    planes = [buf[cur, local_x + i] for i in range(local_x)]
    evens = jnp.concatenate([p[:depth] for p in planes], axis=0)
    odds = jnp.concatenate([p[depth:] for p in planes], axis=0)
    along = dot_nt(wave_yt[:, :half], evens, HI) + dot_nt(wave_yt[:, half:], odds, HI)
    padded = jnp.concatenate([covers, jnp.zeros((8 - local_x, 2 * half), F32)], axis=0)
    walls_y = dot_nt(wave_yt[...], padded, HI)
    send[...] = (
        dot(along[:KY], place_c[0], HI)
        + dot(along[KY:], place_c[1], HI)
        + dot(walls_y[:KY], place_w[0], HI)
        + dot(walls_y[KY:], place_w[1], HI)
    )
    cover_out[...] = dot(covers, back[...], HI)
    for i in range(local_x):
        conc_out[i] = planes[i].T
        conc_z[:, i, :] = planes[i]


def mixing_kernel(ones_value, got, ax, bx, mapped, inv_out, spec_out, stage):
    modes = mapped.shape[3]
    channels = mapped.shape[2]
    own_j = modes // KX
    local_x = inv_out.shape[1] // channels
    blocks = inv_out.shape[0] // own_j
    spread = dot_tn(got[...], ax[...], HI)
    keep = lax.broadcasted_iota(jnp.int32, (own_j, modes), 1) // KX == lax.broadcasted_iota(
        jnp.int32, (own_j, modes), 0
    )
    spec = []
    for f in range(2):
        acc = jnp.zeros((own_j, 2 * KX), F32)
        for k in range(2 * local_x):
            at = (f * 2 * local_x + k) * own_j
            acc = acc + spread[at : at + own_j, k * 2 * KX : (k + 1) * 2 * KX]
        for q in range(2):
            tiled = jnp.concatenate([acc[:, q * KX : (q + 1) * KX]] * own_j, axis=1)
            spec.append(jnp.sum(jnp.where(keep, tiled, 0.0), axis=0, keepdims=True))
    cr, ci, wr, wi = spec
    lane = lax.broadcasted_iota(jnp.int32, (1, modes), 1)
    ones = jnp.where((lane == 0) & (lax.axis_index("slab") == 0), ones_value, 0.0)
    zero = jnp.zeros((1, modes), F32)
    spec_out[:, :modes] = jnp.concatenate([cr, wr, ones] + [zero] * 5, axis=0)
    spec_out[:, modes:] = jnp.concatenate([ci, wi] + [zero] * 6, axis=0)
    mixed_r = cr * mapped[0, 0] - ci * mapped[0, 1] + wr * mapped[1, 0] - wi * mapped[1, 1] + ones * mapped[2, 0]
    mixed_i = cr * mapped[0, 1] + ci * mapped[0, 0] + wr * mapped[1, 1] + wi * mapped[1, 0] + ones * mapped[2, 1]
    mixed_r = mixed_r.astype(BF16).astype(F32).T
    mixed_i = mixed_i.astype(BF16).astype(F32).T
    for j in range(own_j):
        rhs = jnp.concatenate([mixed_r[j * KX : (j + 1) * KX], mixed_i[j * KX : (j + 1) * KX]], axis=0)
        rhs = rhs.astype(BF16)
        out = dot(bx[0], rhs) + dot(bx[1], rhs)
        line = jnp.concatenate([out[i * blocks : (i + 1) * blocks] for i in range(local_x)], axis=1)
        for h in range(line.shape[1] // 128):
            if own_j == 1:
                stage[h] = line[:, h * 128 : (h + 1) * 128]
            else:
                stage[h, pl.ds(j, blocks, own_j), :] = line[:, h * 128 : (h + 1) * 128]
    for h in range(stage.shape[0]):
        inv_out[:, h * 128 : (h + 1) * 128] = stage[h].astype(BF16)


def tail_blocks(own_j):
    return -(-3 // (2 * own_j))


def layer_kernel(
    own_j, inv, conc_z, cot_z, cover_z, lift, point_weight, bias, readout, ez, fwd,
    pred_out, grad_out, lhs, ext_all, waves, pred, point, pre_a, pre_b, hidden_a, hidden_b, grads_a, grads_b,
):
    channels = lift.shape[1]
    local_x = cover_z.shape[0]
    half = cot_z.shape[2]
    span = 2 * half
    depth = cot_z.shape[0] // 2
    groups = depth // ZG
    rows = local_x * channels
    pairs = 2 * KY
    wide = ZG * pairs
    iscale = 1.0 / math.sqrt(KX * KY * KZ)
    c1 = math.sqrt(2.0 / math.pi)
    unit = (c1 * 0.044715) ** (1.0 / 3.0)
    kappa = c1 / unit

    def high(v):
        return v.astype(BF16).astype(F32)

    factors = jnp.concatenate([lift[...], jnp.zeros((5, channels), F32)], axis=0)
    mapped = dot_nt(point_weight[...].astype(F32), factors, HI)
    eye = (
        lax.broadcasted_iota(jnp.int32, (channels, channels), 0)
        == lax.broadcasted_iota(jnp.int32, (channels, channels), 1)
    ).astype(F32)
    columns = dot_nt(eye, jnp.concatenate([bias[...], jnp.zeros((7, channels), F32)], axis=0), HI)
    a0, a1 = unit * mapped[:, 0:1], unit * mapped[:, 1:2]
    a2 = unit * (mapped[:, 2:3] + columns[:, 0:1]) + CENTRE * a0

    lane = lax.broadcasted_iota(jnp.int32, (channels, 32), 1)
    a0_high, a2_high = high(a0), high(a2)
    for x in range(local_x):
        block = jnp.zeros((channels, 32), F32)
        for at, value in (
            (0, a2_high), (1, a2 - a2_high),
            (16 + x, a0_high), (20 + x, a0_high), (24 + x, a0 - a0_high), (28 + x, a1),
        ):
            block = jnp.where(lane == at, value, block)
        block = block.astype(BF16)
        for g in range(groups):
            lhs[g, x * channels : (x + 1) * channels, wide : wide + 32] = block
    flipped = inv[...].astype(F32).T.astype(BF16)
    lifted = (unit * dot(flipped, ez[...])).astype(BF16)
    for g in range(groups):
        lhs[g, :, :wide] = lifted[:, g * wide : (g + 1) * wide]
    wide_readout = jnp.concatenate([readout[...]] * local_x, axis=1)
    owner = lax.broadcasted_iota(jnp.int32, (16, rows), 1) // channels
    slot = lax.broadcasted_iota(jnp.int32, (16, rows), 0)
    scaled = (0.5 / unit) * wide_readout
    weigh = jnp.where(slot == owner, high(scaled), jnp.where(slot - 8 == owner, scaled - high(scaled), 0.0))
    weigh = weigh.astype(BF16)
    point[...] = jnp.zeros(point.shape, F32)
    grads_b[...] = jnp.zeros(grads_b.shape, BF16)
    hidden_b[...] = jnp.zeros(hidden_b.shape, BF16)
    by = fwd[0, :pairs, :]
    pres, hiddens, grads = (pre_a, pre_b), (hidden_a, hidden_b), (grads_a, grads_b)

    def before(g, i, pre):
        z = g * ZG + i
        conc = jnp.concatenate([conc_z[z], conc_z[depth + z]], axis=1) - CENTRE
        conc_high = high(conc)
        wall = jnp.where(z == 0, cover_z[...], 0.0)
        ext = jnp.concatenate([conc_high, conc - conc_high, conc_high, wall], axis=0).astype(BF16)
        ext_all[z] = ext
        pre[...] = dot(lhs[g], jnp.concatenate([fwd[i], ext], axis=0))

    def after(z, hidden, grad):
        line = dot(weigh, hidden[...])
        line = line[:local_x] + line[8 : 8 + local_x]
        pred[z] = line[:, :half]
        pred[depth + z] = line[:, half:]
        sums = dot_nt(jnp.concatenate([by, ext_all[z]], axis=0), grad[...])
        waves[pl.ds(pl.multiple_of(z * pairs, pairs), pairs), :] = sums[:pairs].astype(BF16)
        point[:16] += sums[pairs:]
        point[16:] += sums[:8]

    before(0, 0, pre_a)

    def group(g, carry):
        for i in range(ZG):
            z = g * ZG + i
            this, other = i % 2, (i + 1) % 2
            if i < ZG - 1:
                before(g, i + 1, pres[other])
            else:
                before(jnp.minimum(g + 1, groups - 1), 0, pres[other])
            after(jnp.maximum(z - 1, 0), hiddens[other], grads[other])
            cot = jnp.concatenate([cot_z[z], cot_z[depth + z]], axis=1)
            for x in range(local_x):
                here = slice(x * channels, (x + 1) * channels)
                y = pres[this][here, :]
                u = y * (y * y + kappa)
                t = jnp.tanh(u)
                s = 1.0 + t
                hiddens[this][here, :] = (y * s).astype(BF16)
                slope = u - (2.0 / 3.0 * kappa) * y
                grad = s * (1.0 / 3.0 + slope * (1.0 - t)) * cot[x : x + 1]
                grads[this][here, :] = grad.astype(BF16)
        return carry

    lax.fori_loop(0, groups, group, 0)
    after(depth - 1, hidden_b, grads_b)
    for x in range(local_x):
        pred_out[x] = pred[:, x, :].T
    total = dot(ez[...], waves[...])
    grad_row = 1.5 * wide_readout
    grad_out[:, :rows] = (total * (iscale * grad_row)).astype(BF16)
    mine = point[:16]
    with_conc = jnp.sum(jnp.where((slot < 8) & (slot % 4 == owner), mine, 0.0), axis=0, keepdims=True)
    with_wall = jnp.sum(jnp.where(slot == 12 + owner, mine, 0.0), axis=0, keepdims=True)
    sums = jnp.concatenate([with_conc, with_wall, point[16:17], jnp.zeros((13, rows), F32)], axis=0) * grad_row
    parts = [sums[:, x * channels : (x + 1) * channels] for x in range(local_x)]
    sums = parts[0]
    for part in parts[1:]:
        sums = sums + part
    both = jnp.concatenate([high(sums), sums - high(sums)], axis=1).astype(BF16)
    out_rows = grad_out.shape[0]
    for b in range(tail_blocks(own_j)):
        row = lax.broadcasted_iota(jnp.int32, (out_rows, 16), 0) % (2 * own_j) + b * 2 * own_j
        pick = (row == lax.broadcasted_iota(jnp.int32, (out_rows, 16), 1)).astype(BF16)
        grad_out[:, rows + b * 128 : rows + (b + 1) * 128] = dot(pick, both).astype(BF16)


def outer_kernel(own_j, got, spec, gx, lift, modes_out, point_out, v_r, v_i, d_r, d_i, stage):
    channels = lift.shape[1]
    modes = spec.shape[1] // 2
    rows = got.shape[1] - 128 * tail_blocks(own_j)
    local_x = rows // channels
    per = modes_out.shape[1]

    @pl.when(pl.program_id(0) == 0)
    def _():
        factors = jnp.concatenate([lift[...], jnp.zeros((5, channels), F32)], axis=0)
        v = dot_tn(factors, spec[...], HI)
        v_r[...] = v[:, :modes]
        v_i[...] = v[:, modes:]
        blocks = got.shape[0] // own_j
        halves = rows // 128
        for h in range(halves):
            stage[h] = got[:, h * 128 : (h + 1) * 128].astype(F32)
        lines = [
            [stage[h, pl.ds(j, blocks, own_j), :] if own_j > 1 else stage[h] for h in range(halves)]
            for j in range(own_j)
        ]
        per_half = 128 // channels
        parts_r, parts_i = [], []
        tall = []
        for x in range(local_x):
            h, at = x // per_half, (x % per_half) * channels
            tall.append(jnp.concatenate([lines[j][h][:, at : at + channels] for j in range(own_j)], axis=1))
        acc = dot(gx[...], jnp.concatenate(tall, axis=0).astype(BF16))
        acc = acc[: 2 * KX] + acc[2 * KX :]
        for j in range(own_j):
            parts_r.append(acc[:KX, j * channels : (j + 1) * channels])
            parts_i.append(acc[KX:, j * channels : (j + 1) * channels])
        d_r[...] = jnp.concatenate(parts_r, axis=0).T
        d_i[...] = jnp.concatenate(parts_i, axis=0).T
        sums = jnp.zeros((8, 128), F32)
        for b in range(tail_blocks(own_j)):
            tail = got[:, rows + b * 128 : rows + (b + 1) * 128]
            at = lax.broadcasted_iota(jnp.int32, (8, got.shape[0]), 1) % (2 * own_j) + b * 2 * own_j
            pick = (at == lax.broadcasted_iota(jnp.int32, (8, got.shape[0]), 0)).astype(BF16)
            sums = sums + dot(pick, tail)
        sums = sums[:, :channels] + sums[:, channels:]
        row = lax.broadcasted_iota(jnp.int32, (8, channels), 0)
        base = jnp.where(row == 2, factors + CENTRE * lift[0:1], factors)
        point_out[...] = dot_tn(jnp.where(row < 3, sums, 0.0), base, HI)

    start = pl.program_id(0) * per
    dr = d_r[...]
    di = d_i[...]
    for c in range(per):
        vr = v_r[pl.ds(start + c, 1), :]
        vi = v_i[pl.ds(start + c, 1), :]
        modes_out[0, c] = vr * dr + vi * di
        modes_out[1, c] = vr * di - vi * dr


def params(mib):
    return pltpu.CompilerParams(vmem_limit_bytes=mib * 1024 * 1024)


def in_hbm(array):
    return pltpu.with_memory_space_constraint(array, pltpu.HBM)


def hbm(count):
    return [pl.BlockSpec(memory_space=pltpu.HBM) for _ in range(count)]


def vmem(count):
    return [pl.BlockSpec(memory_space=pltpu.VMEM) for _ in range(count)]


def body(
    conc_init, cover_init, rate_on, rate_off, site_mask, inlet_profiles, inlet_index, lift,
    mode_weight, point_weight, point_bias, readout, cotangent,
):
    devices = lax.axis_size("slab")
    local_x, plane = conc_init.shape
    depth = inlet_profiles.shape[1]
    span = plane // depth
    half = span // 2
    channels = lift.shape[1]
    modes = mode_weight.shape[0]
    own_j = modes // KX
    total_x = local_x * devices
    tab = {k: jnp.asarray(v) for k, v in tables(span, depth, total_x, devices, local_x).items()}
    sds = jax.ShapeDtypeStruct
    smem = pl.BlockSpec(memory_space=pltpu.SMEM)

    pack, conc, walls = pl.pallas_call(
        pack_kernel,
        name="pack",
        out_shape=(
            sds((local_x, half + 16, 2 * depth), BF16),
            sds((local_x, half, 2 * depth), F32),
            sds((local_x, 8, half), F32),
        ),
        in_specs=hbm(5),
        out_specs=vmem(3),
        scratch_shapes=[pltpu.VMEM(conc_init.shape, F32)]
        + [pltpu.VMEM(cover_init.shape, F32)] * 3
        + [pltpu.VMEM(site_mask.shape, jnp.int32), pltpu.SemaphoreType.DMA((5,))],
        compiler_params=params(4),
        cost_estimate=pl.CostEstimate(flops=180000000, transcendentals=0, bytes_accessed=1020000),
    )(*map(in_hbm, (conc_init, cover_init, rate_on, rate_off, site_mask)))
    up = lax.ppermute(pack, "slab", [(i, i + 1) for i in range(devices - 1)])
    down = lax.ppermute(pack, "slab", [(i + 1, i) for i in range(devices - 1)])
    cot_z, mapped = pl.pallas_call(
        prepare_kernel,
        name="prepare",
        out_shape=(
            sds((2 * depth, local_x, half), F32),
            sds((3, 2, channels, modes), F32),
        ),
        in_specs=hbm(1) + [smem] + hbm(1),
        out_specs=vmem(2),
        scratch_shapes=[
            pltpu.VMEM((local_x, half, 2 * depth), F32),
            pltpu.VMEM(cotangent.shape, F32),
            pltpu.VMEM((2, channels, channels, modes), BF16),
            pltpu.SemaphoreType.DMA((3,)),
        ],
        compiler_params=params(8),
        cost_estimate=pl.CostEstimate(flops=1200000000, transcendentals=0, bytes_accessed=6800000),
    )(in_hbm(cotangent), lift, in_hbm(mode_weight.transpose(1, 2, 3, 0)))
    fixed = (
        inlet_index.reshape(1, span), inlet_profiles,
        tab["perm"], tab["back"], tab["wave_yt"], tab["place_c"], tab["place_w"],
    )
    conc_out, cover_out, conc_z, cover_z, send = pl.pallas_call(
        functools.partial(transport_kernel, devices),
        name="transport",
        out_shape=(
            sds((local_x, half, 2 * depth), F32),
            sds((local_x, span), F32),
            sds((2 * depth, local_x, half), F32),
            sds((local_x, span), F32),
            sds((KY, 4 * local_x * KZ), F32),
        ),
        in_specs=vmem(4) + hbm(7),
        out_specs=vmem(5),
        scratch_shapes=[pltpu.VMEM((2, 3 * local_x, 2 * depth, half), F32)]
        + [pltpu.VMEM(v.shape, v.dtype) for v in fixed]
        + [pltpu.SemaphoreType.DMA((len(fixed),))],
        compiler_params=params(8),
        cost_estimate=pl.CostEstimate(flops=2220000000, transcendentals=0, bytes_accessed=12580000),
    )(
        conc, walls, up, down, *map(in_hbm, fixed),
    )
    if own_j != KZ:
        send = send.reshape(KY, 4 * local_x, KZ // own_j, own_j).transpose(0, 2, 1, 3)
        send = send.reshape(devices, 4 * local_x * own_j)
    got = lax.all_to_all(send, "slab", 0, 0, tiled=True)
    ones = math.sqrt(total_x * plane)
    inv, spec = pl.pallas_call(
        functools.partial(mixing_kernel, ones),
        name="mixing",
        out_shape=(
            sds((2 * KY * KZ, local_x * channels), BF16),
            sds((8, 2 * modes), F32),
        ),
        in_specs=vmem(4),
        out_specs=vmem(2),
        scratch_shapes=[pltpu.VMEM((local_x * channels // 128, 2 * KY * KZ, 128), F32)],
        compiler_params=params(4),
        cost_estimate=pl.CostEstimate(flops=960000000, transcendentals=0, bytes_accessed=5440000),
    )(got, tab["ax"], tab["bx"], mapped)
    inv = lax.all_to_all(inv, "slab", 0, 0, tiled=True)
    rows = local_x * channels
    wide = ZG * 2 * KY
    pred, grad = pl.pallas_call(
        functools.partial(layer_kernel, own_j),
        name="layer",
        out_shape=(
            sds((local_x, half, 2 * depth), F32),
            sds((2 * KY * KZ, rows + 128 * tail_blocks(own_j)), BF16),
        ),
        in_specs=vmem(10),
        out_specs=vmem(2),
        scratch_shapes=[
            pltpu.VMEM((depth // ZG, rows, wide + 32), BF16),
            pltpu.VMEM((depth, 16, span), BF16),
            pltpu.VMEM((depth * 2 * KY, rows), BF16),
            pltpu.VMEM((2 * depth, local_x, half), F32),
            pltpu.VMEM((24, rows), F32),
        ]
        + [pltpu.VMEM((rows, span), F32)] * 2
        + [pltpu.VMEM((rows, span), BF16)] * 4,
        compiler_params=params(16),
        cost_estimate=pl.CostEstimate(flops=7440000000, transcendentals=0, bytes_accessed=42160000),
    )(
        inv, conc_z, cot_z, cover_z, lift, point_weight, point_bias.reshape(1, -1), readout.reshape(1, -1),
        tab["ez"], tab["fwd"],
    )
    grad = lax.all_to_all(grad, "slab", 0, 0, tiled=True)
    blocks = 8
    per = channels // blocks
    whole = lambda s: pl.BlockSpec(s, lambda i: (0,) * len(s))
    grad_modes, grad_point = pl.pallas_call(
        functools.partial(outer_kernel, own_j),
        name="outer",
        grid=(blocks,),
        out_shape=(
            sds((2, channels, channels, modes), F32),
            sds((channels, channels), F32),
        ),
        in_specs=[whole(grad.shape), whole(spec.shape), whole(tab["gx"].shape), whole(lift.shape)],
        out_specs=(
            pl.BlockSpec((2, per, channels, modes), lambda i: (0, i, 0, 0)),
            whole((channels, channels)),
        ),
        scratch_shapes=[
            pltpu.VMEM((channels, modes), F32),
            pltpu.VMEM((channels, modes), F32),
            pltpu.VMEM((channels, modes), F32),
            pltpu.VMEM((channels, modes), F32),
            pltpu.VMEM((rows // 128, 2 * KY * KZ, 128), F32),
        ],
        compiler_params=params(8),
        cost_estimate=pl.CostEstimate(flops=2520000000, transcendentals=0, bytes_accessed=14280000),
    )(grad, spec, tab["gx"], lift)
    return (
        conc_out.reshape(local_x, plane),
        cover_out,
        pred.reshape(local_x, plane),
        grad_modes.transpose(3, 0, 1, 2),
        grad_point,
    )


def solution(mesh):
    placed = (
        P(("groups", "slab"), None),
        P(("groups", "slab"), None),
        P(("groups", "slab"), None),
        P(("groups", "slab"), None),
        P(("groups", "slab"), None),
        P("groups", None),
        P("groups"),
        P(),
        P("slab", None, None, None),
        P(),
        P(),
        P(),
        P(("groups", "slab"), None),
    )
    return jax.shard_map(
        body,
        mesh=mesh,
        in_specs=placed,
        out_specs=(
            P(("groups", "slab"), None),
            P(("groups", "slab"), None),
            P(("groups", "slab"), None),
            P(("groups", "slab"), None, None, None),
            P("groups", None),
        ),
        check_vma=False,
    )
```

```python
import functools
import math

import jax
import jax.numpy as jnp
import numpy as np
from jax import lax
from jax.experimental import pallas as pl
from jax.experimental.pallas import tpu as pltpu
from jax.sharding import PartitionSpec as P

KX = 16
KY = 16
KZ = 8
STEPS = 4
PROFILES = 8

PEAK_SPEED = 0.6
DIFFUSIVITY = 0.06
CENTRE = 1.1
OUT_BLOCKS = 8
ZG = 4

HI = lax.Precision.HIGHEST
F32 = jnp.float32
BF16 = jnp.bfloat16


def dot(a, b, precision=None):
    return jnp.dot(a, b, preferred_element_type=F32, precision=precision)


def dot_nt(a, b, precision=None):
    return lax.dot_general(a, b, (((1,), (1,)), ((), ())), preferred_element_type=F32, precision=precision)


def dot_tn(a, b, precision=None):
    return lax.dot_general(a, b, (((0,), (0,)), ((), ())), preferred_element_type=F32, precision=precision)


def split(table):
    high = table.astype(np.float32).astype(jnp.bfloat16)
    return high, (table - high.astype(np.float64)).astype(np.float32).astype(jnp.bfloat16)


def tables(span, depth, total_x, devices, local_x):
    half = span // 2
    own_j = KY * KZ // devices
    tab = {}
    lane = np.arange(half)
    perm = np.zeros((half, 4 * half), np.float32)
    for h in range(2):
        for par in range(2):
            k = (h * half + lane - par) / 2.0
            good = (k == np.floor(k)) & (k >= 0)
            perm[lane[good], (2 * h + par) * half + k[good].astype(int)] = 1.0
    tab["perm"] = perm
    back = np.zeros((span, span), np.float32)
    for par in range(2):
        back[par * half + lane, 2 * lane + par] = 1.0
    tab["back"] = back
    ky = np.arange(KY)
    kz = np.arange(KZ)
    kx = np.arange(KX)
    y_of = np.concatenate([2 * lane, 2 * lane + 1])
    alpha = 2 * np.pi * ((y_of[:, None] * ky[None, :]) % span) / span
    tab["wave_yt"] = np.concatenate([np.cos(alpha), np.sin(alpha)], axis=1).T.astype(np.float32)
    z = np.arange(depth)
    beta = 2 * np.pi * ((kz[:, None] * z[None, :]) % depth) / depth
    place_c = np.zeros((2, local_x, depth, 2, 2, local_x, KZ), np.float32)
    place_w = np.zeros((2, 8, 2, 2, local_x, KZ), np.float32)
    for i in range(local_x):
        place_c[0, i, :, 0, 0, i] = np.cos(beta).T
        place_c[1, i, :, 0, 0, i] = -np.sin(beta).T
        place_c[0, i, :, 0, 1, i] = -np.sin(beta).T
        place_c[1, i, :, 0, 1, i] = -np.cos(beta).T
        place_w[0, i, 1, 0, i] = 1.0
        place_w[1, i, 1, 1, i] = -1.0
    tab["place_c"] = place_c.reshape(2, local_x * depth, 4 * local_x * KZ)
    tab["place_w"] = place_w.reshape(2, 8, 4 * local_x * KZ)
    pairs = 2 * KY
    ez = np.zeros((2 * KY * KZ, depth, KY, 2), np.float32)
    for j in range(KY * KZ):
        a, b = j // KZ, j % KZ
        row = (j // own_j) * 2 * own_j + j % own_j
        ez[row, :, a, 0] = np.cos(beta[b])
        ez[row + own_j, :, a, 0] = -np.sin(beta[b])
        ez[row, :, a, 1] = -np.sin(beta[b])
        ez[row + own_j, :, a, 1] = -np.cos(beta[b])
    tab["ez"] = ez.reshape(2 * KY * KZ, depth * pairs).astype(jnp.bfloat16)
    by = np.stack([np.cos(alpha), np.sin(alpha)], axis=2).reshape(span, pairs)
    fwd = np.zeros((ZG, ZG * pairs + 16, span), np.float32)
    for i in range(ZG):
        fwd[i, i * pairs : (i + 1) * pairs] = by.T
        fwd[i, ZG * pairs : ZG * pairs + 2] = 1.0
    tab["fwd"] = fwd.astype(jnp.bfloat16)
    x = np.arange(total_x)
    gamma = 2 * np.pi * ((x[:, None] * kx[None, :]) % total_x) / total_x
    cg, sg = np.cos(gamma), np.sin(gamma)
    scale = 1.0 / math.sqrt(total_x * span * depth)
    ax = np.zeros((total_x, 2, 2, KX))
    ax[:, 0, 0], ax[:, 1, 0] = cg, sg
    ax[:, 0, 1], ax[:, 1, 1] = -sg, cg
    by_owner = ax.reshape(devices, local_x, 2, 2 * KX)
    tab["ax"] = (by_owner.transpose(0, 2, 1, 3) * scale).reshape(devices, -1).astype(np.float32)
    iscale = 1.0 / math.sqrt(KX * KY * KZ)
    bx = np.zeros((total_x, 2, 2, KX))
    bx[:, 0, 0], bx[:, 0, 1] = cg, -sg
    bx[:, 1, 0], bx[:, 1, 1] = sg, cg
    bx = bx.reshape(devices, local_x, 2, 2 * KX).transpose(1, 0, 2, 3) * iscale
    tab["bx"] = np.stack(split(bx.reshape(2 * total_x, 2 * KX)))
    gx = by_owner.transpose(3, 1, 0, 2).reshape(2 * KX, 2 * total_x)
    tab["gx"] = np.concatenate(split(gx), axis=0)
    return tab


def pack_kernel(
    conc_hbm, cover_hbm, on_hbm, off_hbm, mask_hbm, packed, conc_out, walls_out,
    conc, cover, rate_on, rate_off, mask, sems,
):
    pairs = ((cover_hbm, cover), (on_hbm, rate_on), (off_hbm, rate_off), (mask_hbm, mask), (conc_hbm, conc))
    copies = [pltpu.make_async_copy(src, dst, sems.at[k]) for k, (src, dst) in enumerate(pairs)]
    for copy in copies:
        copy.start()
    for copy in copies:
        copy.wait()
    local_x = conc.shape[0]
    half = conc_out.shape[1]
    for k in range(half):
        conc_out[:, k, :] = conc[:, k * 128 : (k + 1) * 128]
    for f, ref in enumerate((cover, rate_on, rate_off, mask)):
        for h in range(2):
            walls_out[:, h * 4 + f, :] = ref[:, h * half : (h + 1) * half].astype(F32)
    for x in range(local_x):
        packed[x, :half, :] = (conc_out[x] - CENTRE).astype(BF16)
        tail = jnp.concatenate([walls_out[x], jnp.zeros((8, half), F32)], axis=0)
        packed[x, half:, :] = tail.astype(BF16)


def tanh_units():
    c1 = math.sqrt(2.0 / math.pi)
    unit = (c1 * 0.044715) ** (1.0 / 3.0)
    return unit, c1 / unit


def high(v):
    return v.astype(BF16).astype(F32)


def prepare_kernel(
    cot_hbm, lift, weight_hbm, lift_rows, point_weight, bias, readout,
    cot_z, mapped, terms, weigh, flat, cot, weight, sems,
):
    cot_copy = pltpu.make_async_copy(cot_hbm, cot, sems.at[0])
    halves = [pltpu.make_async_copy(weight_hbm.at[p], weight.at[p], sems.at[1 + p]) for p in range(2)]
    for copy in (cot_copy, *halves):
        copy.start()
    cot_copy.wait()
    local_x = cot.shape[0]
    half = flat.shape[1]
    for k in range(half):
        flat[:, k, :] = cot[:, k * 128 : (k + 1) * 128]
    for x in range(local_x):
        cot_z[:, x, :] = flat[x].T
    channels = weight.shape[1]
    rows = local_x * channels
    unit, _ = tanh_units()
    factors = jnp.concatenate([lift_rows[...], jnp.zeros((5, channels), F32)], axis=0)
    pointwise = dot_nt(point_weight[...].astype(F32), factors, HI)
    eye = (
        lax.broadcasted_iota(jnp.int32, (channels, channels), 0)
        == lax.broadcasted_iota(jnp.int32, (channels, channels), 1)
    ).astype(F32)
    columns = dot_nt(eye, jnp.concatenate([bias[...], jnp.zeros((7, channels), F32)], axis=0), HI)
    a0, a1 = unit * pointwise[:, 0:1], unit * pointwise[:, 1:2]
    a2 = unit * (pointwise[:, 2:3] + columns[:, 0:1]) + CENTRE * a0
    lane = lax.broadcasted_iota(jnp.int32, (channels, 32), 1)
    a0_high, a2_high = high(a0), high(a2)
    for x in range(local_x):
        block = jnp.zeros((channels, 32), F32)
        for at, value in (
            (0, a2_high), (1, a2 - a2_high),
            (16 + x, a0_high), (20 + x, a0_high), (24 + x, a0 - a0_high), (28 + x, a1),
        ):
            block = jnp.where(lane == at, value, block)
        terms[x * channels : (x + 1) * channels, :] = block.astype(BF16)
    owner = lax.broadcasted_iota(jnp.int32, (16, rows), 1) // channels
    slot = lax.broadcasted_iota(jnp.int32, (16, rows), 0)
    scaled = (0.5 / unit) * jnp.concatenate([readout[...]] * local_x, axis=1)
    weigh[...] = jnp.where(
        slot == owner, high(scaled), jnp.where(slot - 8 == owner, scaled - high(scaled), 0.0)
    ).astype(BF16)
    for p in range(2):
        halves[p].wait()
        acc = [jnp.zeros(weight.shape[2:], F32) for _ in range(3)]
        for c in range(channels):
            w = weight[p, c].astype(F32)
            acc = [acc[r] + lift[r, c] * w for r in range(3)]
        for r in range(3):
            mapped[r, p] = acc[r]


def split_parity(spread, at, count):
    wide = spread.shape[1] // 2
    return spread[at : at + count, :wide] + spread[at + 4 : at + 4 + count, wide:]


def early_kernel(
    own, own_walls, index_hbm, profiles_hbm, perm_hbm, back_hbm, wave_hbm, place_c_hbm, place_w_hbm,
    planes, fields, inlet, perm, back, wave_yt, place_c, place_w, index, profiles, sems,
):
    moves = (
        (index_hbm, index), (perm_hbm, perm), (profiles_hbm, profiles), (wave_hbm, wave_yt),
        (place_c_hbm, place_c), (place_w_hbm, place_w), (back_hbm, back),
    )
    copies = [pltpu.make_async_copy(src, dst, sems.at[k]) for k, (src, dst) in enumerate(moves)]
    for copy in copies:
        copy.start()
    local_x = own.shape[0]
    half = own.shape[1]
    for x in range(local_x):
        planes[x] = own[x].T
    for copy in copies[:3]:
        copy.wait()
    profile = index[...].astype(F32)
    gap = jnp.zeros((3, half), F32)
    walls = [own_walls[x] for x in range(local_x)]
    walls.append(jnp.concatenate([profile[:, :half], gap, profile[:, half:], gap], axis=0))
    spread = dot(jnp.concatenate(walls, axis=0), perm[...], HI)
    for x in range(local_x):
        fields[4 * x : 4 * x + 4] = split_parity(spread, 8 * x, 4)
    chosen = split_parity(spread, 8 * local_x, 1)
    pick = lax.broadcasted_iota(jnp.int32, (PROFILES, 2 * half), 0).astype(F32)
    onehot = (jnp.abs(pick - chosen) < 0.5).astype(F32)
    plane = dot_tn(profiles[...], onehot, HI)
    inlet[...] = jnp.concatenate([plane[:, :half], plane[:, half:]], axis=0)
    for copy in copies[3:]:
        copy.wait()


def transport_kernel(
    devices, up, down, own, own_fields, inlet, perm, back, wave_yt, place_c, place_w,
    conc_out, cover_out, conc_z, cover_z, send, buf,
):
    local_x = own.shape[0]
    half = own.shape[2]
    depth = own.shape[1] // 2
    rows = 3 * local_x
    sides = [r for r in range(rows) if r // local_x != 1]
    walls = []
    for r in sides:
        ref = up if r < local_x else down
        buf[0, r] = (ref[r % local_x, :half, :].astype(F32) + CENTRE).T
        walls.append(ref[r % local_x, half:, :].astype(F32)[:8])
    for x in range(local_x):
        buf[0, local_x + x] = own[x]
    spread = dot(jnp.concatenate(walls, axis=0), perm[...], HI)
    fields = [own_fields[4 * (r % local_x) : 4 * (r % local_x) + 4] for r in range(rows)]
    for k, r in enumerate(sides):
        fields[r] = split_parity(spread, 8 * k, 4)
    height = lax.broadcasted_iota(jnp.int32, (depth, half), 0).astype(F32)
    height = (height + 0.5) / depth
    speed = PEAK_SPEED * 4.0 * height * (1.0 - height)
    speed = jnp.concatenate([speed, speed], axis=0)
    keep = (1.0 - 6.0 * DIFFUSIVITY) - speed
    carried = DIFFUSIVITY + speed
    first = lax.axis_index("slab") == 0
    last = lax.axis_index("slab") == devices - 1
    cover = [f[0:1] for f in fields]
    for step in range(STEPS):
        cur, nxt = step % 2, (step + 1) % 2
        for r in range(1 + step, rows - 1 - step):
            c = buf[cur, r]
            behind = buf[cur, r - 1]
            ahead = buf[cur, r + 1]
            if r == local_x:
                behind = jnp.where(first, inlet[...], behind)
            if r == 2 * local_x - 1:
                ahead = jnp.where(last, c, ahead)
            even, odd = c[:depth], c[depth:]
            side = jnp.concatenate(
                [odd + pltpu.roll(odd, 1, 1), even + pltpu.roll(even, half - 1, 1)], axis=0
            )
            below = jnp.concatenate([even[:1], even[:-1], odd[:1], odd[:-1]], axis=0)
            above = jnp.concatenate([even[1:], even[-1:], odd[1:], odd[-1:]], axis=0)
            around = ahead + side + below + above
            f = fields[r]
            wall = jnp.concatenate([even[:1], odd[:1]], axis=1)
            uptake = f[3:4] * (f[1:2] * wall * (1.0 - cover[r]) - f[2:3] * cover[r])
            new = keep * c + carried * behind + DIFFUSIVITY * around
            buf[nxt, r] = new
            buf[nxt, r, 0:1] = new[0:1] - uptake[:, :half]
            buf[nxt, r, depth : depth + 1] = new[depth : depth + 1] - uptake[:, half:]
            cover[r] = cover[r] + uptake
    cur = STEPS % 2
    covers = jnp.concatenate(cover[local_x : 2 * local_x], axis=0)
    cover_z[...] = covers
    planes = [buf[cur, local_x + i] for i in range(local_x)]
    evens = jnp.concatenate([p[:depth] for p in planes], axis=0)
    odds = jnp.concatenate([p[depth:] for p in planes], axis=0)
    along = dot_nt(wave_yt[:, :half], evens, HI) + dot_nt(wave_yt[:, half:], odds, HI)
    padded = jnp.concatenate([covers, jnp.zeros((8 - local_x, 2 * half), F32)], axis=0)
    walls_y = dot_nt(wave_yt[...], padded, HI)
    send[...] = (
        dot(along[:KY], place_c[0], HI)
        + dot(along[KY:], place_c[1], HI)
        + dot(walls_y[:KY], place_w[0], HI)
        + dot(walls_y[KY:], place_w[1], HI)
    )
    cover_out[...] = dot(covers, back[...], HI)
    for i in range(local_x):
        conc_out[i] = planes[i].T
        conc_z[:, i, :] = planes[i]


def mixing_kernel(ones_value, got, ax, bx, mapped, inv_out, spec_out, stage):
    modes = mapped.shape[3]
    channels = mapped.shape[2]
    own_j = modes // KX
    local_x = inv_out.shape[1] // channels
    blocks = inv_out.shape[0] // own_j
    spread = dot_tn(got[...], ax[...], HI)
    keep = lax.broadcasted_iota(jnp.int32, (own_j, modes), 1) // KX == lax.broadcasted_iota(
        jnp.int32, (own_j, modes), 0
    )
    spec = []
    for f in range(2):
        acc = jnp.zeros((own_j, 2 * KX), F32)
        for k in range(2 * local_x):
            at = (f * 2 * local_x + k) * own_j
            acc = acc + spread[at : at + own_j, k * 2 * KX : (k + 1) * 2 * KX]
        for q in range(2):
            tiled = jnp.concatenate([acc[:, q * KX : (q + 1) * KX]] * own_j, axis=1)
            spec.append(jnp.sum(jnp.where(keep, tiled, 0.0), axis=0, keepdims=True))
    cr, ci, wr, wi = spec
    lane = lax.broadcasted_iota(jnp.int32, (1, modes), 1)
    ones = jnp.where((lane == 0) & (lax.axis_index("slab") == 0), ones_value, 0.0)
    zero = jnp.zeros((1, modes), F32)
    spec_out[:, :modes] = jnp.concatenate([cr, wr, ones] + [zero] * 5, axis=0)
    spec_out[:, modes:] = jnp.concatenate([ci, wi] + [zero] * 6, axis=0)
    mixed_r = cr * mapped[0, 0] - ci * mapped[0, 1] + wr * mapped[1, 0] - wi * mapped[1, 1] + ones * mapped[2, 0]
    mixed_i = cr * mapped[0, 1] + ci * mapped[0, 0] + wr * mapped[1, 1] + wi * mapped[1, 0] + ones * mapped[2, 1]
    mixed_r = mixed_r.astype(BF16).astype(F32).T
    mixed_i = mixed_i.astype(BF16).astype(F32).T
    for j in range(own_j):
        rhs = jnp.concatenate([mixed_r[j * KX : (j + 1) * KX], mixed_i[j * KX : (j + 1) * KX]], axis=0)
        rhs = rhs.astype(BF16)
        out = dot(bx[0], rhs) + dot(bx[1], rhs)
        line = jnp.concatenate([out[i * blocks : (i + 1) * blocks] for i in range(local_x)], axis=1)
        for h in range(line.shape[1] // 128):
            if own_j == 1:
                stage[h] = line[:, h * 128 : (h + 1) * 128]
            else:
                stage[h, pl.ds(j, blocks, own_j), :] = line[:, h * 128 : (h + 1) * 128]
    for h in range(stage.shape[0]):
        inv_out[:, h * 128 : (h + 1) * 128] = stage[h].astype(BF16)


def tail_blocks(own_j):
    return -(-3 // (2 * own_j))


def layer_kernel(
    own_j, inv, conc_z, cot_z, cover_z, terms, weigh, readout, ez, fwd,
    pred_out, grad_out, lhs, ext_all, waves, pred, point, pre_a, pre_b, hidden_a, hidden_b, grads_a, grads_b,
):
    channels = readout.shape[1]
    local_x = cover_z.shape[0]
    half = cot_z.shape[2]
    span = 2 * half
    depth = cot_z.shape[0] // 2
    groups = depth // ZG
    rows = local_x * channels
    pairs = 2 * KY
    wide = ZG * pairs
    iscale = 1.0 / math.sqrt(KX * KY * KZ)
    unit, kappa = tanh_units()
    flipped = inv[...].astype(F32).T.astype(BF16)
    lifted = (unit * dot(flipped, ez[...])).astype(BF16)
    for g in range(groups):
        lhs[g] = lifted[:, g * wide : (g + 1) * wide]
    wide_readout = jnp.concatenate([readout[...]] * local_x, axis=1)
    owner = lax.broadcasted_iota(jnp.int32, (16, rows), 1) // channels
    slot = lax.broadcasted_iota(jnp.int32, (16, rows), 0)
    point[...] = jnp.zeros(point.shape, F32)
    grads_b[...] = jnp.zeros(grads_b.shape, BF16)
    hidden_b[...] = jnp.zeros(hidden_b.shape, BF16)
    by = fwd[0, :pairs, :]
    pres, hiddens, grads = (pre_a, pre_b), (hidden_a, hidden_b), (grads_a, grads_b)

    def before(g, i, pre):
        z = g * ZG + i
        conc = jnp.concatenate([conc_z[z], conc_z[depth + z]], axis=1) - CENTRE
        conc_high = high(conc)
        wall = jnp.where(z == 0, cover_z[...], 0.0)
        ext = jnp.concatenate([conc_high, conc - conc_high, conc_high, wall], axis=0).astype(BF16)
        ext_all[z] = ext
        both = jnp.concatenate([lhs[g], terms[...]], axis=1)
        pre[...] = dot(both, jnp.concatenate([fwd[i], ext], axis=0))

    def after(z, hidden, grad):
        line = dot(weigh[...], hidden[...])
        line = line[:local_x] + line[8 : 8 + local_x]
        pred[z] = line[:, :half]
        pred[depth + z] = line[:, half:]
        sums = dot_nt(jnp.concatenate([by, ext_all[z]], axis=0), grad[...])
        waves[pl.ds(pl.multiple_of(z * pairs, pairs), pairs), :] = sums[:pairs].astype(BF16)
        point[:16] += sums[pairs:]
        point[16:] += sums[:8]

    before(0, 0, pre_a)

    def group(g, carry):
        for i in range(ZG):
            z = g * ZG + i
            this, other = i % 2, (i + 1) % 2
            if i < ZG - 1:
                before(g, i + 1, pres[other])
            else:
                before(jnp.minimum(g + 1, groups - 1), 0, pres[other])
            after(jnp.maximum(z - 1, 0), hiddens[other], grads[other])
            cot = jnp.concatenate([cot_z[z], cot_z[depth + z]], axis=1)
            for x in range(local_x):
                here = slice(x * channels, (x + 1) * channels)
                y = pres[this][here, :]
                u = y * (y * y + kappa)
                t = jnp.tanh(u)
                s = 1.0 + t
                hiddens[this][here, :] = (y * s).astype(BF16)
                slope = u - (2.0 / 3.0 * kappa) * y
                grad = s * (1.0 / 3.0 + slope * (1.0 - t)) * cot[x : x + 1]
                grads[this][here, :] = grad.astype(BF16)
        return carry

    lax.fori_loop(0, groups, group, 0)
    after(depth - 1, hidden_b, grads_b)
    for x in range(local_x):
        pred_out[x] = pred[:, x, :].T
    total = dot(ez[...], waves[...])
    grad_row = 1.5 * wide_readout
    grad_out[:, :rows] = (total * (iscale * grad_row)).astype(BF16)
    mine = point[:16]
    with_conc = jnp.sum(jnp.where((slot < 8) & (slot % 4 == owner), mine, 0.0), axis=0, keepdims=True)
    with_wall = jnp.sum(jnp.where(slot == 12 + owner, mine, 0.0), axis=0, keepdims=True)
    sums = jnp.concatenate([with_conc, with_wall, point[16:17], jnp.zeros((13, rows), F32)], axis=0) * grad_row
    parts = [sums[:, x * channels : (x + 1) * channels] for x in range(local_x)]
    sums = parts[0]
    for part in parts[1:]:
        sums = sums + part
    both = jnp.concatenate([high(sums), sums - high(sums)], axis=1).astype(BF16)
    out_rows = grad_out.shape[0]
    for b in range(tail_blocks(own_j)):
        row = lax.broadcasted_iota(jnp.int32, (out_rows, 16), 0) % (2 * own_j) + b * 2 * own_j
        pick = (row == lax.broadcasted_iota(jnp.int32, (out_rows, 16), 1)).astype(BF16)
        grad_out[:, rows + b * 128 : rows + (b + 1) * 128] = dot(pick, both).astype(BF16)


def outer_kernel(own_j, got, spec, gx, lift, modes_hbm, point_out, result, factor, stage, sems):
    channels = lift.shape[1]
    modes = spec.shape[1] // 2
    rows = got.shape[1] - 128 * tail_blocks(own_j)
    local_x = rows // channels
    factors = jnp.concatenate([lift[...], jnp.zeros((5, channels), F32)], axis=0)
    v = dot_tn(factors, spec[...], HI)
    v_r, v_i = v[:, :modes], v[:, modes:]
    blocks = got.shape[0] // own_j
    halves = rows // 128
    for h in range(halves):
        stage[h] = got[:, h * 128 : (h + 1) * 128].astype(F32)
    lines = [
        [stage[h, pl.ds(j, blocks, own_j), :] if own_j > 1 else stage[h] for h in range(halves)]
        for j in range(own_j)
    ]
    per_half = 128 // channels
    parts_r, parts_i = [], []
    tall = []
    for x in range(local_x):
        h, at = x // per_half, (x % per_half) * channels
        tall.append(jnp.concatenate([lines[j][h][:, at : at + channels] for j in range(own_j)], axis=1))
    acc = dot(gx[...], jnp.concatenate(tall, axis=0).astype(BF16))
    acc = acc[: 2 * KX] + acc[2 * KX :]
    for j in range(own_j):
        parts_r.append(acc[:KX, j * channels : (j + 1) * channels])
        parts_i.append(acc[KX:, j * channels : (j + 1) * channels])
    dr = jnp.concatenate(parts_r, axis=0).T
    di = jnp.concatenate(parts_i, axis=0).T
    factor[0], factor[1] = v_r, v_i
    per = channels // OUT_BLOCKS

    def leave(b, q):
        here = pl.ds(b * per, per)
        return pltpu.make_async_copy(result.at[q, here], modes_hbm.at[q, here], sems.at[q, b])

    def block(b, carry):
        for k in range(per):
            c = b * per + k
            vr, vi = factor[0, pl.ds(c, 1), :], factor[1, pl.ds(c, 1), :]
            result[0, c] = vr * dr + vi * di
            result[1, c] = vr * di - vi * dr
        leave(b, 0).start()
        leave(b, 1).start()
        return carry

    lax.fori_loop(0, OUT_BLOCKS, block, 0)
    sums = jnp.zeros((8, 128), F32)
    for b in range(tail_blocks(own_j)):
        tail = got[:, rows + b * 128 : rows + (b + 1) * 128]
        at = lax.broadcasted_iota(jnp.int32, (8, got.shape[0]), 1) % (2 * own_j) + b * 2 * own_j
        pick = (at == lax.broadcasted_iota(jnp.int32, (8, got.shape[0]), 0)).astype(BF16)
        sums = sums + dot(pick, tail)
    sums = sums[:, :channels] + sums[:, channels:]
    row = lax.broadcasted_iota(jnp.int32, (8, channels), 0)
    base = jnp.where(row == 2, factors + CENTRE * lift[0:1], factors)
    point_out[...] = dot_tn(jnp.where(row < 3, sums, 0.0), base, HI)
    for b in range(OUT_BLOCKS):
        leave(b, 0).wait()
        leave(b, 1).wait()


def params(mib):
    return pltpu.CompilerParams(vmem_limit_bytes=mib * 1024 * 1024)


def cost(micros):
    return pl.CostEstimate(flops=int(micros * 6e8), transcendentals=0, bytes_accessed=int(micros * 3.4e6))


def in_hbm(array):
    return pltpu.with_memory_space_constraint(array, pltpu.HBM)


def hbm(count):
    return [pl.BlockSpec(memory_space=pltpu.HBM) for _ in range(count)]


def vmem(count):
    return [pl.BlockSpec(memory_space=pltpu.VMEM) for _ in range(count)]


def body(
    conc_init, cover_init, rate_on, rate_off, site_mask, inlet_profiles, inlet_index, lift,
    mode_weight, point_weight, point_bias, readout, cotangent,
):
    devices = lax.axis_size("slab")
    local_x, plane = conc_init.shape
    depth = inlet_profiles.shape[1]
    span = plane // depth
    half = span // 2
    channels = lift.shape[1]
    modes = mode_weight.shape[0]
    own_j = modes // KX
    total_x = local_x * devices
    tab = {k: jnp.asarray(v) for k, v in tables(span, depth, total_x, devices, local_x).items()}
    sds = jax.ShapeDtypeStruct
    smem = pl.BlockSpec(memory_space=pltpu.SMEM)

    pack, conc, walls = pl.pallas_call(
        pack_kernel,
        name="pack",
        out_shape=(
            sds((local_x, half + 16, 2 * depth), BF16),
            sds((local_x, half, 2 * depth), F32),
            sds((local_x, 8, half), F32),
        ),
        in_specs=hbm(5),
        out_specs=vmem(3),
        scratch_shapes=[pltpu.VMEM(conc_init.shape, F32)]
        + [pltpu.VMEM(cover_init.shape, F32)] * 3
        + [pltpu.VMEM(site_mask.shape, jnp.int32), pltpu.SemaphoreType.DMA((5,))],
        compiler_params=params(4),
        cost_estimate=cost(0.3),
    )(*map(in_hbm, (conc_init, cover_init, rate_on, rate_off, site_mask)))
    up = lax.ppermute(pack, "slab", [(i, i + 1) for i in range(devices - 1)])
    down = lax.ppermute(pack, "slab", [(i + 1, i) for i in range(devices - 1)])
    cot_z, mapped, terms, weigh = pl.pallas_call(
        prepare_kernel,
        name="prepare",
        out_shape=(
            sds((2 * depth, local_x, half), F32),
            sds((3, 2, channels, modes), F32),
            sds((local_x * channels, 32), BF16),
            sds((16, local_x * channels), BF16),
        ),
        in_specs=hbm(1) + [smem] + hbm(1) + vmem(4),
        out_specs=vmem(4),
        scratch_shapes=[
            pltpu.VMEM((local_x, half, 2 * depth), F32),
            pltpu.VMEM(cotangent.shape, F32),
            pltpu.VMEM((2, channels, channels, modes), BF16),
            pltpu.SemaphoreType.DMA((3,)),
        ],
        compiler_params=params(8),
        cost_estimate=cost(2.0),
    )(
        in_hbm(cotangent), lift, in_hbm(mode_weight.transpose(1, 2, 3, 0)),
        lift, point_weight, point_bias.reshape(1, -1), readout.reshape(1, -1),
    )
    constants = [tab[k] for k in ("perm", "back", "wave_yt", "place_c", "place_w")]
    early = pl.pallas_call(
        early_kernel,
        name="early",
        out_shape=(
            sds((local_x, 2 * depth, half), F32),
            sds((4 * local_x, span), F32),
            sds((2 * depth, half), F32),
            *(sds(v.shape, v.dtype) for v in constants),
        ),
        in_specs=vmem(2) + hbm(7),
        out_specs=vmem(8),
        scratch_shapes=[
            pltpu.VMEM((1, span), jnp.int32), pltpu.VMEM(inlet_profiles.shape, F32), pltpu.SemaphoreType.DMA((7,)),
        ],
        compiler_params=params(8),
        cost_estimate=cost(1.5),
    )(conc, walls, *map(in_hbm, (inlet_index.reshape(1, span), inlet_profiles, *constants)))
    conc_out, cover_out, conc_z, cover_z, send = pl.pallas_call(
        functools.partial(transport_kernel, devices),
        name="transport",
        out_shape=(
            sds((local_x, half, 2 * depth), F32),
            sds((local_x, span), F32),
            sds((2 * depth, local_x, half), F32),
            sds((local_x, span), F32),
            sds((KY, 4 * local_x * KZ), F32),
        ),
        in_specs=vmem(10),
        out_specs=vmem(5),
        scratch_shapes=[pltpu.VMEM((2, 3 * local_x, 2 * depth, half), F32)],
        compiler_params=params(8),
        cost_estimate=cost(3.0),
    )(up, down, *early)
    if own_j != KZ:
        send = send.reshape(KY, 4 * local_x, KZ // own_j, own_j).transpose(0, 2, 1, 3)
        send = send.reshape(devices, 4 * local_x * own_j)
    got = lax.all_to_all(send, "slab", 0, 0, tiled=True)
    ones = math.sqrt(total_x * plane)
    inv, spec = pl.pallas_call(
        functools.partial(mixing_kernel, ones),
        name="mixing",
        out_shape=(
            sds((2 * KY * KZ, local_x * channels), BF16),
            sds((8, 2 * modes), F32),
        ),
        in_specs=vmem(4),
        out_specs=vmem(2),
        scratch_shapes=[pltpu.VMEM((local_x * channels // 128, 2 * KY * KZ, 128), F32)],
        compiler_params=params(4),
        cost_estimate=cost(1.6),
    )(got, tab["ax"], tab["bx"], mapped)
    inv = lax.all_to_all(inv, "slab", 0, 0, tiled=True)
    rows = local_x * channels
    wide = ZG * 2 * KY
    pred, grad = pl.pallas_call(
        functools.partial(layer_kernel, own_j),
        name="layer",
        out_shape=(
            sds((local_x, half, 2 * depth), F32),
            sds((2 * KY * KZ, rows + 128 * tail_blocks(own_j)), BF16),
        ),
        in_specs=vmem(9),
        out_specs=vmem(2),
        scratch_shapes=[
            pltpu.VMEM((depth // ZG, rows, wide), BF16),
            pltpu.VMEM((depth, 16, span), BF16),
            pltpu.VMEM((depth * 2 * KY, rows), BF16),
            pltpu.VMEM((2 * depth, local_x, half), F32),
            pltpu.VMEM((24, rows), F32),
        ]
        + [pltpu.VMEM((rows, span), F32)] * 2
        + [pltpu.VMEM((rows, span), BF16)] * 4,
        compiler_params=params(16),
        cost_estimate=cost(12.4),
    )(
        inv, conc_z, cot_z, cover_z, terms, weigh, readout.reshape(1, -1), tab["ez"], tab["fwd"],
    )
    grad = lax.all_to_all(grad, "slab", 0, 0, tiled=True)
    grad_modes, grad_point = pl.pallas_call(
        functools.partial(outer_kernel, own_j),
        name="outer",
        out_shape=(
            sds((2, channels, channels, modes), F32),
            sds((channels, channels), F32),
        ),
        in_specs=vmem(4),
        out_specs=hbm(1) + vmem(1),
        scratch_shapes=[
            pltpu.VMEM((2, channels, channels, modes), F32),
            pltpu.VMEM((2, channels, modes), F32),
            pltpu.VMEM((rows // 128, 2 * KY * KZ, 128), F32),
            pltpu.SemaphoreType.DMA((2, OUT_BLOCKS)),
        ],
        compiler_params=params(12),
        cost_estimate=cost(3.0),
    )(grad, spec, tab["gx"], lift)
    return (
        conc_out.reshape(local_x, plane),
        cover_out,
        pred.reshape(local_x, plane),
        grad_modes.transpose(3, 0, 1, 2),
        grad_point,
    )


def solution(mesh):
    placed = (
        P(("groups", "slab"), None),
        P(("groups", "slab"), None),
        P(("groups", "slab"), None),
        P(("groups", "slab"), None),
        P(("groups", "slab"), None),
        P("groups", None),
        P("groups"),
        P(),
        P("slab", None, None, None),
        P(),
        P(),
        P(),
        P(("groups", "slab"), None),
    )
    return jax.shard_map(
        body,
        mesh=mesh,
        in_specs=placed,
        out_specs=(
            P(("groups", "slab"), None),
            P(("groups", "slab"), None),
            P(("groups", "slab"), None),
            P(("groups", "slab"), None, None, None),
            P("groups", None),
        ),
        check_vma=False,
    )
```

```python
import functools
import math

import jax
import jax.numpy as jnp
import numpy as np
from jax import lax
from jax.experimental import pallas as pl
from jax.experimental.pallas import tpu as pltpu
from jax.sharding import PartitionSpec as P

KX = 16
KY = 16
KZ = 8
STEPS = 4
PROFILES = 8

PEAK_SPEED = 0.6
DIFFUSIVITY = 0.06
CENTRE = 1.1
OUT_BLOCKS = 8
ZG = 4

HI = lax.Precision.HIGHEST
F32 = jnp.float32
BF16 = jnp.bfloat16


def dot(a, b, precision=None):
    return jnp.dot(a, b, preferred_element_type=F32, precision=precision)


def dot_nt(a, b, precision=None):
    return lax.dot_general(a, b, (((1,), (1,)), ((), ())), preferred_element_type=F32, precision=precision)


def dot_tn(a, b, precision=None):
    return lax.dot_general(a, b, (((0,), (0,)), ((), ())), preferred_element_type=F32, precision=precision)


def split(table):
    high = table.astype(np.float32).astype(jnp.bfloat16)
    return high, (table - high.astype(np.float64)).astype(np.float32).astype(jnp.bfloat16)


def tables(span, depth, total_x, devices, local_x):
    half = span // 2
    own_j = KY * KZ // devices
    tab = {}
    lane = np.arange(half)
    perm = np.zeros((half, 4 * half), np.float32)
    for h in range(2):
        for par in range(2):
            k = (h * half + lane - par) / 2.0
            good = (k == np.floor(k)) & (k >= 0)
            perm[lane[good], (2 * h + par) * half + k[good].astype(int)] = 1.0
    tab["perm"] = perm
    back = np.zeros((span, span), np.float32)
    for par in range(2):
        back[par * half + lane, 2 * lane + par] = 1.0
    tab["back"] = back
    ky = np.arange(KY)
    kz = np.arange(KZ)
    kx = np.arange(KX)
    y_of = np.concatenate([2 * lane, 2 * lane + 1])
    alpha = 2 * np.pi * ((y_of[:, None] * ky[None, :]) % span) / span
    tab["wave_yt"] = np.concatenate([np.cos(alpha), np.sin(alpha)], axis=1).T.astype(np.float32)
    z = np.arange(depth)
    beta = 2 * np.pi * ((kz[:, None] * z[None, :]) % depth) / depth
    place_c = np.zeros((2, local_x, depth, 2, 2, local_x, KZ), np.float32)
    place_w = np.zeros((2, 8, 2, 2, local_x, KZ), np.float32)
    for i in range(local_x):
        place_c[0, i, :, 0, 0, i] = np.cos(beta).T
        place_c[1, i, :, 0, 0, i] = -np.sin(beta).T
        place_c[0, i, :, 0, 1, i] = -np.sin(beta).T
        place_c[1, i, :, 0, 1, i] = -np.cos(beta).T
        place_w[0, i, 1, 0, i] = 1.0
        place_w[1, i, 1, 1, i] = -1.0
    tab["place_c"] = place_c.reshape(2, local_x * depth, 4 * local_x * KZ)
    tab["place_w"] = place_w.reshape(2, 8, 4 * local_x * KZ)
    pairs = 2 * KY
    ez = np.zeros((2 * KY * KZ, depth, KY, 2), np.float32)
    for j in range(KY * KZ):
        a, b = j // KZ, j % KZ
        row = (j // own_j) * 2 * own_j + j % own_j
        ez[row, :, a, 0] = np.cos(beta[b])
        ez[row + own_j, :, a, 0] = -np.sin(beta[b])
        ez[row, :, a, 1] = -np.sin(beta[b])
        ez[row + own_j, :, a, 1] = -np.cos(beta[b])
    tab["ez"] = ez.reshape(2 * KY * KZ, depth * pairs).astype(jnp.bfloat16)
    by = np.stack([np.cos(alpha), np.sin(alpha)], axis=2).reshape(span, pairs)
    fwd = np.zeros((ZG, ZG * pairs + 16, span), np.float32)
    for i in range(ZG):
        fwd[i, i * pairs : (i + 1) * pairs] = by.T
        fwd[i, ZG * pairs : ZG * pairs + 2] = 1.0
    tab["fwd"] = fwd.astype(jnp.bfloat16)
    x = np.arange(total_x)
    gamma = 2 * np.pi * ((x[:, None] * kx[None, :]) % total_x) / total_x
    cg, sg = np.cos(gamma), np.sin(gamma)
    scale = 1.0 / math.sqrt(total_x * span * depth)
    ax = np.zeros((total_x, 2, 2, KX))
    ax[:, 0, 0], ax[:, 1, 0] = cg, sg
    ax[:, 0, 1], ax[:, 1, 1] = -sg, cg
    by_owner = ax.reshape(devices, local_x, 2, 2 * KX)
    tab["ax"] = (by_owner.transpose(0, 2, 1, 3) * scale).reshape(devices, -1).astype(np.float32)
    iscale = 1.0 / math.sqrt(KX * KY * KZ)
    bx = np.zeros((total_x, 2, 2, KX))
    bx[:, 0, 0], bx[:, 0, 1] = cg, -sg
    bx[:, 1, 0], bx[:, 1, 1] = sg, cg
    bx = bx.reshape(devices, local_x, 2, 2 * KX).transpose(1, 0, 2, 3) * iscale
    tab["bx"] = np.stack(split(bx.reshape(2 * total_x, 2 * KX)))
    gx = by_owner.transpose(3, 1, 0, 2).reshape(2 * KX, 2 * total_x)
    tab["gx"] = np.concatenate(split(gx), axis=0)
    return tab


def pack_kernel(
    conc_hbm, cover_hbm, on_hbm, off_hbm, mask_hbm, packed, conc_out, walls_out,
    conc, cover, rate_on, rate_off, mask, sems,
):
    pairs = ((cover_hbm, cover), (on_hbm, rate_on), (off_hbm, rate_off), (mask_hbm, mask), (conc_hbm, conc))
    copies = [pltpu.make_async_copy(src, dst, sems.at[k]) for k, (src, dst) in enumerate(pairs)]
    for copy in copies:
        copy.start()
    for copy in copies:
        copy.wait()
    local_x = conc.shape[0]
    half = conc_out.shape[1]
    for k in range(half):
        conc_out[:, k, :] = conc[:, k * 128 : (k + 1) * 128]
    for f, ref in enumerate((cover, rate_on, rate_off, mask)):
        for h in range(2):
            walls_out[:, h * 4 + f, :] = ref[:, h * half : (h + 1) * half].astype(F32)
    for x in range(local_x):
        packed[x, :half, :] = (conc_out[x] - CENTRE).astype(BF16)
        tail = jnp.concatenate([walls_out[x], jnp.zeros((8, half), F32)], axis=0)
        packed[x, half:, :] = tail.astype(BF16)


def tanh_units():
    c1 = math.sqrt(2.0 / math.pi)
    unit = (c1 * 0.044715) ** (1.0 / 3.0)
    return unit, c1 / unit


def high(v):
    return v.astype(BF16).astype(F32)


def prepare_kernel(
    cot_hbm, lift, weight_hbm, lift_rows, point_weight, bias, readout, conc_z,
    cot_z, mapped, terms, weigh, conc_out, flat, cot, weight, sems,
):
    cot_copy = pltpu.make_async_copy(cot_hbm, cot, sems.at[0])
    halves = [pltpu.make_async_copy(weight_hbm.at[p], weight.at[p], sems.at[1 + p]) for p in range(2)]
    for copy in (cot_copy, *halves):
        copy.start()
    cot_copy.wait()
    local_x = cot.shape[0]
    half = flat.shape[1]
    for k in range(half):
        flat[:, k, :] = cot[:, k * 128 : (k + 1) * 128]
    for x in range(local_x):
        cot_z[:, x, :] = flat[x].T
    for x in range(local_x):
        flat[x] = conc_z[:, x, :].T
    for k in range(half):
        conc_out[:, k * 128 : (k + 1) * 128] = flat[:, k, :]
    channels = weight.shape[1]
    rows = local_x * channels
    unit, _ = tanh_units()
    factors = jnp.concatenate([lift_rows[...], jnp.zeros((5, channels), F32)], axis=0)
    pointwise = dot_nt(point_weight[...].astype(F32), factors, HI)
    eye = (
        lax.broadcasted_iota(jnp.int32, (channels, channels), 0)
        == lax.broadcasted_iota(jnp.int32, (channels, channels), 1)
    ).astype(F32)
    columns = dot_nt(eye, jnp.concatenate([bias[...], jnp.zeros((7, channels), F32)], axis=0), HI)
    a0, a1 = unit * pointwise[:, 0:1], unit * pointwise[:, 1:2]
    a2 = unit * (pointwise[:, 2:3] + columns[:, 0:1]) + CENTRE * a0
    lane = lax.broadcasted_iota(jnp.int32, (channels, 32), 1)
    a0_high, a2_high = high(a0), high(a2)
    for x in range(local_x):
        block = jnp.zeros((channels, 32), F32)
        for at, value in (
            (0, a2_high), (1, a2 - a2_high),
            (16 + x, a0_high), (20 + x, a0_high), (24 + x, a0 - a0_high), (28 + x, a1),
        ):
            block = jnp.where(lane == at, value, block)
        terms[x * channels : (x + 1) * channels, :] = block.astype(BF16)
    owner = lax.broadcasted_iota(jnp.int32, (16, rows), 1) // channels
    slot = lax.broadcasted_iota(jnp.int32, (16, rows), 0)
    scaled = (0.5 / unit) * jnp.concatenate([readout[...]] * local_x, axis=1)
    weigh[...] = jnp.where(
        slot == owner, high(scaled), jnp.where(slot - 8 == owner, scaled - high(scaled), 0.0)
    ).astype(BF16)
    for p in range(2):
        halves[p].wait()
        acc = [jnp.zeros(weight.shape[2:], F32) for _ in range(3)]
        for c in range(channels):
            w = weight[p, c].astype(F32)
            acc = [acc[r] + lift[r, c] * w for r in range(3)]
        for r in range(3):
            mapped[r, p] = acc[r]


def split_parity(spread, at, count):
    wide = spread.shape[1] // 2
    return spread[at : at + count, :wide] + spread[at + 4 : at + 4 + count, wide:]


def early_kernel(
    own, own_walls, index_hbm, profiles_hbm, perm_hbm, back_hbm, wave_hbm, place_c_hbm, place_w_hbm,
    planes, fields, inlet, perm, back, wave_yt, place_c, place_w, index, profiles, sems,
):
    moves = (
        (index_hbm, index), (perm_hbm, perm), (profiles_hbm, profiles), (wave_hbm, wave_yt),
        (place_c_hbm, place_c), (place_w_hbm, place_w), (back_hbm, back),
    )
    copies = [pltpu.make_async_copy(src, dst, sems.at[k]) for k, (src, dst) in enumerate(moves)]
    for copy in copies:
        copy.start()
    local_x = own.shape[0]
    half = own.shape[1]
    for x in range(local_x):
        planes[x] = own[x].T
    for copy in copies[:3]:
        copy.wait()
    profile = index[...].astype(F32)
    gap = jnp.zeros((3, half), F32)
    walls = [own_walls[x] for x in range(local_x)]
    walls.append(jnp.concatenate([profile[:, :half], gap, profile[:, half:], gap], axis=0))
    spread = dot(jnp.concatenate(walls, axis=0), perm[...], HI)
    for x in range(local_x):
        fields[4 * x : 4 * x + 4] = split_parity(spread, 8 * x, 4)
    chosen = split_parity(spread, 8 * local_x, 1)
    pick = lax.broadcasted_iota(jnp.int32, (PROFILES, 2 * half), 0).astype(F32)
    onehot = (jnp.abs(pick - chosen) < 0.5).astype(F32)
    plane = dot_tn(profiles[...], onehot, HI)
    inlet[...] = jnp.concatenate([plane[:, :half], plane[:, half:]], axis=0)
    for copy in copies[3:]:
        copy.wait()


def transport_kernel(
    devices, across, within, own, own_fields, inlet, perm, back, wave_yt, place_c, place_w,
    cover_out, conc_z, cover_z, send, buf,
):
    local_x = own.shape[0]
    half = own.shape[2]
    depth = own.shape[1] // 2
    rows = 3 * local_x
    sides = [r for r in range(rows) if r // local_x != 1]
    walls = []
    even = lax.axis_index("slab") % 2 == 0
    for r in sides:
        x = r % local_x
        near, far = within[x].astype(F32), across[x].astype(F32)
        here = jnp.where(even, far, near) if r < local_x else jnp.where(even, near, far)
        buf[0, r] = (here[:half] + CENTRE).T
        walls.append(here[half : half + 8])
    for x in range(local_x):
        buf[0, local_x + x] = own[x]
    spread = dot(jnp.concatenate(walls, axis=0), perm[...], HI)
    fields = [own_fields[4 * (r % local_x) : 4 * (r % local_x) + 4] for r in range(rows)]
    for k, r in enumerate(sides):
        fields[r] = split_parity(spread, 8 * k, 4)
    height = lax.broadcasted_iota(jnp.int32, (depth, half), 0).astype(F32)
    height = (height + 0.5) / depth
    speed = PEAK_SPEED * 4.0 * height * (1.0 - height)
    speed = jnp.concatenate([speed, speed], axis=0)
    keep = (1.0 - 6.0 * DIFFUSIVITY) - speed
    carried = DIFFUSIVITY + speed
    first = lax.axis_index("slab") == 0
    last = lax.axis_index("slab") == devices - 1
    cover = [f[0:1] for f in fields]
    for step in range(STEPS):
        cur, nxt = step % 2, (step + 1) % 2
        for r in range(1 + step, rows - 1 - step):
            c = buf[cur, r]
            behind = buf[cur, r - 1]
            ahead = buf[cur, r + 1]
            if r == local_x:
                behind = jnp.where(first, inlet[...], behind)
            if r == 2 * local_x - 1:
                ahead = jnp.where(last, c, ahead)
            even, odd = c[:depth], c[depth:]
            side = jnp.concatenate(
                [odd + pltpu.roll(odd, 1, 1), even + pltpu.roll(even, half - 1, 1)], axis=0
            )
            below = jnp.concatenate([even[:1], even[:-1], odd[:1], odd[:-1]], axis=0)
            above = jnp.concatenate([even[1:], even[-1:], odd[1:], odd[-1:]], axis=0)
            around = ahead + side + below + above
            f = fields[r]
            wall = jnp.concatenate([even[:1], odd[:1]], axis=1)
            uptake = f[3:4] * (f[1:2] * wall * (1.0 - cover[r]) - f[2:3] * cover[r])
            new = keep * c + carried * behind + DIFFUSIVITY * around
            buf[nxt, r] = new
            buf[nxt, r, 0:1] = new[0:1] - uptake[:, :half]
            buf[nxt, r, depth : depth + 1] = new[depth : depth + 1] - uptake[:, half:]
            cover[r] = cover[r] + uptake
    cur = STEPS % 2
    covers = jnp.concatenate(cover[local_x : 2 * local_x], axis=0)
    cover_z[...] = covers
    planes = [buf[cur, local_x + i] for i in range(local_x)]
    evens = jnp.concatenate([p[:depth] for p in planes], axis=0)
    odds = jnp.concatenate([p[depth:] for p in planes], axis=0)
    along = dot_nt(wave_yt[:, :half], evens, HI) + dot_nt(wave_yt[:, half:], odds, HI)
    padded = jnp.concatenate([covers, jnp.zeros((8 - local_x, 2 * half), F32)], axis=0)
    walls_y = dot_nt(wave_yt[...], padded, HI)
    send[...] = (
        dot(along[:KY], place_c[0], HI)
        + dot(along[KY:], place_c[1], HI)
        + dot(walls_y[:KY], place_w[0], HI)
        + dot(walls_y[KY:], place_w[1], HI)
    )
    cover_out[...] = dot(covers, back[...], HI)
    for i in range(local_x):
        conc_z[:, i, :] = planes[i]


def mixing_kernel(ones_value, got, ax, bx, mapped, inv_out, spec_out, stage):
    modes = mapped.shape[3]
    channels = mapped.shape[2]
    own_j = modes // KX
    local_x = inv_out.shape[1] // channels
    blocks = inv_out.shape[0] // own_j
    spread = dot_tn(got[...], ax[...], HI)
    keep = lax.broadcasted_iota(jnp.int32, (own_j, modes), 1) // KX == lax.broadcasted_iota(
        jnp.int32, (own_j, modes), 0
    )
    spec = []
    for f in range(2):
        acc = jnp.zeros((own_j, 2 * KX), F32)
        for k in range(2 * local_x):
            at = (f * 2 * local_x + k) * own_j
            acc = acc + spread[at : at + own_j, k * 2 * KX : (k + 1) * 2 * KX]
        for q in range(2):
            tiled = jnp.concatenate([acc[:, q * KX : (q + 1) * KX]] * own_j, axis=1)
            spec.append(jnp.sum(jnp.where(keep, tiled, 0.0), axis=0, keepdims=True))
    cr, ci, wr, wi = spec
    lane = lax.broadcasted_iota(jnp.int32, (1, modes), 1)
    ones = jnp.where((lane == 0) & (lax.axis_index("slab") == 0), ones_value, 0.0)
    zero = jnp.zeros((1, modes), F32)
    spec_out[:, :modes] = jnp.concatenate([cr, wr, ones] + [zero] * 5, axis=0)
    spec_out[:, modes:] = jnp.concatenate([ci, wi] + [zero] * 6, axis=0)
    mixed_r = cr * mapped[0, 0] - ci * mapped[0, 1] + wr * mapped[1, 0] - wi * mapped[1, 1] + ones * mapped[2, 0]
    mixed_i = cr * mapped[0, 1] + ci * mapped[0, 0] + wr * mapped[1, 1] + wi * mapped[1, 0] + ones * mapped[2, 1]
    mixed_r = mixed_r.astype(BF16).astype(F32).T
    mixed_i = mixed_i.astype(BF16).astype(F32).T
    for j in range(own_j):
        rhs = jnp.concatenate([mixed_r[j * KX : (j + 1) * KX], mixed_i[j * KX : (j + 1) * KX]], axis=0)
        rhs = rhs.astype(BF16)
        out = dot(bx[0], rhs) + dot(bx[1], rhs)
        line = jnp.concatenate([out[i * blocks : (i + 1) * blocks] for i in range(local_x)], axis=1)
        for h in range(line.shape[1] // 128):
            if own_j == 1:
                stage[h] = line[:, h * 128 : (h + 1) * 128]
            else:
                stage[h, pl.ds(j, blocks, own_j), :] = line[:, h * 128 : (h + 1) * 128]
    for h in range(stage.shape[0]):
        inv_out[:, h * 128 : (h + 1) * 128] = stage[h].astype(BF16)


def tail_blocks(own_j):
    return -(-3 // (2 * own_j))


def extra_rows(conc_z, cover_z, z):
    depth = conc_z.shape[0] // 2
    conc = jnp.concatenate([conc_z[z], conc_z[depth + z]], axis=1) - CENTRE
    wall = jnp.where(z == 0, cover_z[...], 0.0)
    return jnp.concatenate([high(conc), conc - high(conc), high(conc), wall], axis=0).astype(BF16)


def layer_kernel(
    own_j, inv, conc_z, cot_z, cover_z, terms, readout, ez, fwd,
    grad_out, lhs, waves, ext_all, point, pre_a, pre_b, grads_a, grads_b,
):
    channels = readout.shape[1]
    local_x = cover_z.shape[0]
    half = cot_z.shape[2]
    span = 2 * half
    depth = cot_z.shape[0] // 2
    groups = depth // ZG
    rows = local_x * channels
    pairs = 2 * KY
    wide = ZG * pairs
    iscale = 1.0 / math.sqrt(KX * KY * KZ)
    unit, kappa = tanh_units()
    flipped = inv[...].astype(F32).T.astype(BF16)
    lifted = (unit * dot(flipped, ez[...])).astype(BF16)
    for g in range(groups):
        lhs[g] = lifted[:, g * wide : (g + 1) * wide]
    wide_readout = jnp.concatenate([readout[...]] * local_x, axis=1)
    owner = lax.broadcasted_iota(jnp.int32, (16, rows), 1) // channels
    slot = lax.broadcasted_iota(jnp.int32, (16, rows), 0)
    point[...] = jnp.zeros(point.shape, F32)
    grads_b[...] = jnp.zeros(grads_b.shape, BF16)
    by = fwd[0, :pairs, :]
    pres, grads = (pre_a, pre_b), (grads_a, grads_b)

    def before(g, i, pre):
        z = g * ZG + i
        ext = extra_rows(conc_z, cover_z, z)
        ext_all[z] = ext
        both = jnp.concatenate([lhs[g], terms[...]], axis=1)
        pre[...] = dot(both, jnp.concatenate([fwd[i], ext], axis=0))

    def after(z, grad):
        sums = dot_nt(jnp.concatenate([by, ext_all[z]], axis=0), grad[...])
        waves[pl.ds(pl.multiple_of(z * pairs, pairs), pairs), :] = sums[:pairs].astype(BF16)
        point[:16] += sums[pairs:]
        point[16:] += sums[:8]

    before(0, 0, pre_a)

    def group(g, carry):
        for i in range(ZG):
            z = g * ZG + i
            this, other = i % 2, (i + 1) % 2
            if i < ZG - 1:
                before(g, i + 1, pres[other])
            else:
                before(jnp.minimum(g + 1, groups - 1), 0, pres[other])
            after(jnp.maximum(z - 1, 0), grads[other])
            cot = jnp.concatenate([cot_z[z], cot_z[depth + z]], axis=1)
            for x in range(local_x):
                here = slice(x * channels, (x + 1) * channels)
                y = pres[this][here, :]
                u = y * (y * y + kappa)
                t = jnp.tanh(u)
                s = 1.0 + t
                slope = u - (2.0 / 3.0 * kappa) * y
                grad = s * (1.0 / 3.0 + slope * (1.0 - t)) * cot[x : x + 1]
                grads[this][here, :] = grad.astype(BF16)
        return carry

    lax.fori_loop(0, groups, group, 0)
    after(depth - 1, grads_b)
    total = dot(ez[...], waves[...])
    grad_row = 1.5 * wide_readout
    grad_out[:, :rows] = (total * (iscale * grad_row)).astype(BF16)
    mine = point[:16]
    with_conc = jnp.sum(jnp.where((slot < 8) & (slot % 4 == owner), mine, 0.0), axis=0, keepdims=True)
    with_wall = jnp.sum(jnp.where(slot == 12 + owner, mine, 0.0), axis=0, keepdims=True)
    sums = jnp.concatenate([with_conc, with_wall, point[16:17], jnp.zeros((13, rows), F32)], axis=0) * grad_row
    parts = [sums[:, x * channels : (x + 1) * channels] for x in range(local_x)]
    sums = parts[0]
    for part in parts[1:]:
        sums = sums + part
    both = jnp.concatenate([high(sums), sums - high(sums)], axis=1).astype(BF16)
    out_rows = grad_out.shape[0]
    for b in range(tail_blocks(own_j)):
        row = lax.broadcasted_iota(jnp.int32, (out_rows, 16), 0) % (2 * own_j) + b * 2 * own_j
        pick = (row == lax.broadcasted_iota(jnp.int32, (out_rows, 16), 1)).astype(BF16)
        grad_out[:, rows + b * 128 : rows + (b + 1) * 128] = dot(pick, both).astype(BF16)


def predict_kernel(
    lhs, conc_z, cover_z, terms, weigh, fwd, pred_out, pred, flat, pre_a, pre_b, hidden_a, hidden_b
):
    local_x = pred_out.shape[0]
    half = conc_z.shape[2]
    groups = lhs.shape[0]
    depth = groups * ZG
    _, kappa = tanh_units()
    pres, hiddens = (pre_a, pre_b), (hidden_a, hidden_b)
    hidden_b[...] = jnp.zeros(hidden_b.shape, BF16)

    def before(g, i, pre):
        both = jnp.concatenate([lhs[g], terms[...]], axis=1)
        pre[...] = dot(both, jnp.concatenate([fwd[i], extra_rows(conc_z, cover_z, g * ZG + i)], axis=0))

    def after(z, hidden):
        line = dot(weigh[...], hidden[...])
        line = line[:local_x] + line[8 : 8 + local_x]
        pred[z] = line[:, :half]
        pred[depth + z] = line[:, half:]

    before(0, 0, pre_a)

    def group(g, carry):
        for i in range(ZG):
            z = g * ZG + i
            this, other = i % 2, (i + 1) % 2
            if i < ZG - 1:
                before(g, i + 1, pres[other])
            else:
                before(jnp.minimum(g + 1, groups - 1), 0, pres[other])
            after(jnp.maximum(z - 1, 0), hiddens[other])
            for k in range(local_x):
                here = slice(k * pre_a.shape[0] // local_x, (k + 1) * pre_a.shape[0] // local_x)
                y = pres[this][here, :]
                t = jnp.tanh(y * (y * y + kappa))
                hiddens[this][here, :] = (y * (1.0 + t)).astype(BF16)
        return carry

    lax.fori_loop(0, groups, group, 0)
    after(depth - 1, hidden_b)
    for x in range(local_x):
        flat[x] = pred[:, x, :].T
    for k in range(half):
        pred_out[:, k * 128 : (k + 1) * 128] = flat[:, k, :]


def outer_kernel(own_j, got, spec, gx, lift, modes_hbm, point_out, result, factor, stage, sems):
    channels = lift.shape[1]
    modes = spec.shape[1] // 2
    rows = got.shape[1] - 128 * tail_blocks(own_j)
    local_x = rows // channels
    factors = jnp.concatenate([lift[...], jnp.zeros((5, channels), F32)], axis=0)
    v = dot_tn(factors, spec[...], HI)
    v_r, v_i = v[:, :modes], v[:, modes:]
    blocks = got.shape[0] // own_j
    halves = rows // 128
    for h in range(halves):
        stage[h] = got[:, h * 128 : (h + 1) * 128].astype(F32)
    lines = [
        [stage[h, pl.ds(j, blocks, own_j), :] if own_j > 1 else stage[h] for h in range(halves)]
        for j in range(own_j)
    ]
    per_half = 128 // channels
    parts_r, parts_i = [], []
    tall = []
    for x in range(local_x):
        h, at = x // per_half, (x % per_half) * channels
        tall.append(jnp.concatenate([lines[j][h][:, at : at + channels] for j in range(own_j)], axis=1))
    acc = dot(gx[...], jnp.concatenate(tall, axis=0).astype(BF16))
    acc = acc[: 2 * KX] + acc[2 * KX :]
    for j in range(own_j):
        parts_r.append(acc[:KX, j * channels : (j + 1) * channels])
        parts_i.append(acc[KX:, j * channels : (j + 1) * channels])
    dr = jnp.concatenate(parts_r, axis=0).T
    di = jnp.concatenate(parts_i, axis=0).T
    factor[0], factor[1] = v_r, v_i
    per = channels // OUT_BLOCKS

    def leave(b, q):
        here = pl.ds(b * per, per)
        return pltpu.make_async_copy(result.at[q, here], modes_hbm.at[q, here], sems.at[q, b])

    def block(b, carry):
        for k in range(per):
            c = b * per + k
            vr, vi = factor[0, pl.ds(c, 1), :], factor[1, pl.ds(c, 1), :]
            result[0, c] = vr * dr + vi * di
            result[1, c] = vr * di - vi * dr
        leave(b, 0).start()
        leave(b, 1).start()
        return carry

    lax.fori_loop(0, OUT_BLOCKS, block, 0)
    sums = jnp.zeros((8, 128), F32)
    for b in range(tail_blocks(own_j)):
        tail = got[:, rows + b * 128 : rows + (b + 1) * 128]
        at = lax.broadcasted_iota(jnp.int32, (8, got.shape[0]), 1) % (2 * own_j) + b * 2 * own_j
        pick = (at == lax.broadcasted_iota(jnp.int32, (8, got.shape[0]), 0)).astype(BF16)
        sums = sums + dot(pick, tail)
    sums = sums[:, :channels] + sums[:, channels:]
    row = lax.broadcasted_iota(jnp.int32, (8, channels), 0)
    base = jnp.where(row == 2, factors + CENTRE * lift[0:1], factors)
    point_out[...] = dot_tn(jnp.where(row < 3, sums, 0.0), base, HI)
    for b in range(OUT_BLOCKS):
        leave(b, 0).wait()
        leave(b, 1).wait()


def params(mib):
    return pltpu.CompilerParams(vmem_limit_bytes=mib * 1024 * 1024)


def cost(micros):
    return pl.CostEstimate(flops=int(micros * 6e8), transcendentals=0, bytes_accessed=int(micros * 3.4e6))


def in_hbm(array):
    return pltpu.with_memory_space_constraint(array, pltpu.HBM)


def hbm(count):
    return [pl.BlockSpec(memory_space=pltpu.HBM) for _ in range(count)]


def vmem(count):
    return [pl.BlockSpec(memory_space=pltpu.VMEM) for _ in range(count)]


def body(
    conc_init, cover_init, rate_on, rate_off, site_mask, inlet_profiles, inlet_index, lift,
    mode_weight, point_weight, point_bias, readout, cotangent,
):
    devices = lax.axis_size("slab")
    local_x, plane = conc_init.shape
    depth = inlet_profiles.shape[1]
    span = plane // depth
    half = span // 2
    channels = lift.shape[1]
    modes = mode_weight.shape[0]
    own_j = modes // KX
    total_x = local_x * devices
    tab = {k: jnp.asarray(v) for k, v in tables(span, depth, total_x, devices, local_x).items()}
    sds = jax.ShapeDtypeStruct
    smem = pl.BlockSpec(memory_space=pltpu.SMEM)

    pack, conc, walls = pl.pallas_call(
        pack_kernel,
        name="pack",
        out_shape=(
            sds((local_x, half + 16, 2 * depth), BF16),
            sds((local_x, half, 2 * depth), F32),
            sds((local_x, 8, half), F32),
        ),
        in_specs=hbm(5),
        out_specs=vmem(3),
        scratch_shapes=[pltpu.VMEM(conc_init.shape, F32)]
        + [pltpu.VMEM(cover_init.shape, F32)] * 3
        + [pltpu.VMEM(site_mask.shape, jnp.int32), pltpu.SemaphoreType.DMA((5,))],
        compiler_params=params(4),
        cost_estimate=cost(0.3),
    )(*map(in_hbm, (conc_init, cover_init, rate_on, rate_off, site_mask)))
    seams = [(i, i + 1) for i in range(1, devices - 1, 2)]
    across = lax.ppermute(pack, "slab", seams + [(j, i) for i, j in seams])
    within = lax.ppermute(pack, "slab", [(i, i ^ 1) for i in range(devices)])
    constants = [tab[k] for k in ("perm", "back", "wave_yt", "place_c", "place_w")]
    early = pl.pallas_call(
        early_kernel,
        name="early",
        out_shape=(
            sds((local_x, 2 * depth, half), F32),
            sds((4 * local_x, span), F32),
            sds((2 * depth, half), F32),
            *(sds(v.shape, v.dtype) for v in constants),
        ),
        in_specs=vmem(2) + hbm(7),
        out_specs=vmem(8),
        scratch_shapes=[
            pltpu.VMEM((1, span), jnp.int32), pltpu.VMEM(inlet_profiles.shape, F32), pltpu.SemaphoreType.DMA((7,)),
        ],
        compiler_params=params(8),
        cost_estimate=cost(1.5),
    )(conc, walls, *map(in_hbm, (inlet_index.reshape(1, span), inlet_profiles, *constants)))
    cover_out, conc_z, cover_z, send = pl.pallas_call(
        functools.partial(transport_kernel, devices),
        name="transport",
        out_shape=(
            sds((local_x, span), F32),
            sds((2 * depth, local_x, half), F32),
            sds((local_x, span), F32),
            sds((KY, 4 * local_x * KZ), F32),
        ),
        in_specs=vmem(10),
        out_specs=vmem(4),
        scratch_shapes=[pltpu.VMEM((2, 3 * local_x, 2 * depth, half), F32)],
        compiler_params=params(8),
        cost_estimate=cost(3.0),
    )(across, within, *early)
    cot_z, mapped, terms, weigh, conc_out = pl.pallas_call(
        prepare_kernel,
        name="prepare",
        out_shape=(
            sds((2 * depth, local_x, half), F32),
            sds((3, 2, channels, modes), F32),
            sds((local_x * channels, 32), BF16),
            sds((16, local_x * channels), BF16),
            sds(conc_init.shape, F32),
        ),
        in_specs=hbm(1) + [smem] + hbm(1) + vmem(5),
        out_specs=vmem(5),
        scratch_shapes=[
            pltpu.VMEM((local_x, half, 2 * depth), F32),
            pltpu.VMEM(cotangent.shape, F32),
            pltpu.VMEM((2, channels, channels, modes), BF16),
            pltpu.SemaphoreType.DMA((3,)),
        ],
        compiler_params=params(8),
        cost_estimate=cost(2.0),
    )(
        in_hbm(cotangent), lift, in_hbm(mode_weight.transpose(1, 2, 3, 0)),
        lift, point_weight, point_bias.reshape(1, -1), readout.reshape(1, -1), conc_z,
    )
    if own_j != KZ:
        send = send.reshape(KY, 4 * local_x, KZ // own_j, own_j).transpose(0, 2, 1, 3)
        send = send.reshape(devices, 4 * local_x * own_j)
    got = lax.all_to_all(send, "slab", 0, 0, tiled=True)
    ones = math.sqrt(total_x * plane)
    inv, spec = pl.pallas_call(
        functools.partial(mixing_kernel, ones),
        name="mixing",
        out_shape=(
            sds((2 * KY * KZ, local_x * channels), BF16),
            sds((8, 2 * modes), F32),
        ),
        in_specs=vmem(4),
        out_specs=vmem(2),
        scratch_shapes=[pltpu.VMEM((local_x * channels // 128, 2 * KY * KZ, 128), F32)],
        compiler_params=params(4),
        cost_estimate=cost(1.6),
    )(got, tab["ax"], tab["bx"], mapped)
    inv = lax.all_to_all(inv, "slab", 0, 0, tiled=True)
    rows = local_x * channels
    wide = ZG * 2 * KY
    grad, lhs = pl.pallas_call(
        functools.partial(layer_kernel, own_j),
        name="layer",
        out_shape=(
            sds((2 * KY * KZ, rows + 128 * tail_blocks(own_j)), BF16),
            sds((depth // ZG, rows, wide), BF16),
        ),
        in_specs=vmem(8),
        out_specs=vmem(2),
        scratch_shapes=[
            pltpu.VMEM((depth * 2 * KY, rows), BF16),
            pltpu.VMEM((depth, 16, span), BF16),
            pltpu.VMEM((24, rows), F32),
        ]
        + [pltpu.VMEM((rows, span), F32)] * 2
        + [pltpu.VMEM((rows, span), BF16)] * 2,
        compiler_params=params(16),
        cost_estimate=cost(11.0),
    )(inv, conc_z, cot_z, cover_z, terms, readout.reshape(1, -1), tab["ez"], tab["fwd"])
    grad = lax.all_to_all(grad, "slab", 0, 0, tiled=True)
    pred = pl.pallas_call(
        predict_kernel,
        name="predict",
        out_shape=sds((local_x, plane), F32),
        in_specs=vmem(6),
        out_specs=pl.BlockSpec(memory_space=pltpu.VMEM),
        scratch_shapes=[pltpu.VMEM((2 * depth, local_x, half), F32), pltpu.VMEM((local_x, half, 2 * depth), F32)]
        + [pltpu.VMEM((rows, span), F32)] * 2
        + [pltpu.VMEM((rows, span), BF16)] * 2,
        compiler_params=params(8),
        cost_estimate=cost(5.5),
    )(lhs, conc_z, cover_z, terms, weigh, tab["fwd"])
    grad_modes, grad_point = pl.pallas_call(
        functools.partial(outer_kernel, own_j),
        name="outer",
        out_shape=(
            sds((2, channels, channels, modes), F32),
            sds((channels, channels), F32),
        ),
        in_specs=vmem(4),
        out_specs=hbm(1) + vmem(1),
        scratch_shapes=[
            pltpu.VMEM((2, channels, channels, modes), F32),
            pltpu.VMEM((2, channels, modes), F32),
            pltpu.VMEM((rows // 128, 2 * KY * KZ, 128), F32),
            pltpu.SemaphoreType.DMA((2, OUT_BLOCKS)),
        ],
        compiler_params=params(12),
        cost_estimate=cost(3.0),
    )(grad, spec, tab["gx"], lift)
    return (
        conc_out,
        cover_out,
        pred,
        grad_modes.transpose(3, 0, 1, 2),
        grad_point,
    )


def solution(mesh):
    placed = (
        P(("groups", "slab"), None),
        P(("groups", "slab"), None),
        P(("groups", "slab"), None),
        P(("groups", "slab"), None),
        P(("groups", "slab"), None),
        P("groups", None),
        P("groups"),
        P(),
        P("slab", None, None, None),
        P(),
        P(),
        P(),
        P(("groups", "slab"), None),
    )
    return jax.shard_map(
        body,
        mesh=mesh,
        in_specs=placed,
        out_specs=(
            P(("groups", "slab"), None),
            P(("groups", "slab"), None),
            P(("groups", "slab"), None),
            P(("groups", "slab"), None, None, None),
            P("groups", None),
        ),
        check_vma=False,
    )
```

```python
import functools
import math

import jax
import jax.numpy as jnp
import numpy as np
from jax import lax
from jax.experimental import pallas as pl
from jax.experimental.pallas import tpu as pltpu
from jax.sharding import PartitionSpec as P

KX = 16
KY = 16
KZ = 8
STEPS = 4
PROFILES = 8

PEAK_SPEED = 0.6
DIFFUSIVITY = 0.06
CENTRE = 1.1
OUT_BLOCKS = 8
ZG = 4

HI = lax.Precision.HIGHEST
F32 = jnp.float32
BF16 = jnp.bfloat16


def dot(a, b, precision=None):
    return jnp.dot(a, b, preferred_element_type=F32, precision=precision)


def dot_nt(a, b, precision=None):
    return lax.dot_general(a, b, (((1,), (1,)), ((), ())), preferred_element_type=F32, precision=precision)


def dot_tn(a, b, precision=None):
    return lax.dot_general(a, b, (((0,), (0,)), ((), ())), preferred_element_type=F32, precision=precision)


def split(table):
    high = table.astype(np.float32).astype(jnp.bfloat16)
    return high, (table - high.astype(np.float64)).astype(np.float32).astype(jnp.bfloat16)


def tables(span, depth, total_x, devices, local_x):
    half = span // 2
    own_j = KY * KZ // devices
    tab = {}
    lane = np.arange(half)
    perm = np.zeros((half, 4 * half), np.float32)
    for h in range(2):
        for par in range(2):
            k = (h * half + lane - par) / 2.0
            good = (k == np.floor(k)) & (k >= 0)
            perm[lane[good], (2 * h + par) * half + k[good].astype(int)] = 1.0
    tab["perm"] = perm
    back = np.zeros((span, span), np.float32)
    for par in range(2):
        back[par * half + lane, 2 * lane + par] = 1.0
    tab["back"] = back
    ky = np.arange(KY)
    kz = np.arange(KZ)
    kx = np.arange(KX)
    y_of = np.concatenate([2 * lane, 2 * lane + 1])
    alpha = 2 * np.pi * ((y_of[:, None] * ky[None, :]) % span) / span
    tab["wave_yt"] = np.concatenate([np.cos(alpha), np.sin(alpha)], axis=1).T.astype(np.float32)
    z = np.arange(depth)
    beta = 2 * np.pi * ((kz[:, None] * z[None, :]) % depth) / depth
    place_c = np.zeros((2, local_x, depth, 2, 2, local_x, KZ), np.float32)
    place_w = np.zeros((2, 8, 2, 2, local_x, KZ), np.float32)
    for i in range(local_x):
        place_c[0, i, :, 0, 0, i] = np.cos(beta).T
        place_c[1, i, :, 0, 0, i] = -np.sin(beta).T
        place_c[0, i, :, 0, 1, i] = -np.sin(beta).T
        place_c[1, i, :, 0, 1, i] = -np.cos(beta).T
        place_w[0, i, 1, 0, i] = 1.0
        place_w[1, i, 1, 1, i] = -1.0
    tab["place_c"] = place_c.reshape(2, local_x * depth, 4 * local_x * KZ)
    tab["place_w"] = place_w.reshape(2, 8, 4 * local_x * KZ)
    pairs = 2 * KY
    ez = np.zeros((2 * KY * KZ, depth, KY, 2), np.float32)
    for j in range(KY * KZ):
        a, b = j // KZ, j % KZ
        row = (j // own_j) * 2 * own_j + j % own_j
        ez[row, :, a, 0] = np.cos(beta[b])
        ez[row + own_j, :, a, 0] = -np.sin(beta[b])
        ez[row, :, a, 1] = -np.sin(beta[b])
        ez[row + own_j, :, a, 1] = -np.cos(beta[b])
    tab["ez"] = ez.reshape(2 * KY * KZ, depth * pairs).astype(jnp.bfloat16)
    by = np.stack([np.cos(alpha), np.sin(alpha)], axis=2).reshape(span, pairs)
    fwd = np.zeros((ZG, ZG * pairs + 16, span), np.float32)
    for i in range(ZG):
        fwd[i, i * pairs : (i + 1) * pairs] = by.T
        fwd[i, ZG * pairs : ZG * pairs + 2] = 1.0
    tab["fwd"] = fwd.astype(jnp.bfloat16)
    x = np.arange(total_x)
    gamma = 2 * np.pi * ((x[:, None] * kx[None, :]) % total_x) / total_x
    cg, sg = np.cos(gamma), np.sin(gamma)
    scale = 1.0 / math.sqrt(total_x * span * depth)
    ax = np.zeros((total_x, 2, 2, KX))
    ax[:, 0, 0], ax[:, 1, 0] = cg, sg
    ax[:, 0, 1], ax[:, 1, 1] = -sg, cg
    by_owner = ax.reshape(devices, local_x, 2, 2 * KX)
    tab["ax"] = (by_owner.transpose(0, 2, 1, 3) * scale).reshape(devices, -1).astype(np.float32)
    iscale = 1.0 / math.sqrt(KX * KY * KZ)
    bx = np.zeros((total_x, 2, 2, KX))
    bx[:, 0, 0], bx[:, 0, 1] = cg, -sg
    bx[:, 1, 0], bx[:, 1, 1] = sg, cg
    bx = bx.reshape(devices, local_x, 2, 2 * KX).transpose(1, 0, 2, 3) * iscale
    tab["bx"] = np.stack(split(bx.reshape(2 * total_x, 2 * KX)))
    gx = by_owner.transpose(3, 1, 0, 2).reshape(2 * KX, 2 * total_x)
    tab["gx"] = np.concatenate(split(gx), axis=0)
    return tab


def pack_kernel(
    conc_hbm, cover_hbm, on_hbm, off_hbm, mask_hbm, packed, conc_out, walls_out,
    conc, cover, rate_on, rate_off, mask, sems,
):
    pairs = ((cover_hbm, cover), (on_hbm, rate_on), (off_hbm, rate_off), (mask_hbm, mask), (conc_hbm, conc))
    copies = [pltpu.make_async_copy(src, dst, sems.at[k]) for k, (src, dst) in enumerate(pairs)]
    for copy in copies:
        copy.start()
    for copy in copies:
        copy.wait()
    local_x = conc.shape[0]
    half = conc_out.shape[1]
    for k in range(half):
        conc_out[:, k, :] = conc[:, k * 128 : (k + 1) * 128]
    for f, ref in enumerate((cover, rate_on, rate_off, mask)):
        for h in range(2):
            walls_out[:, h * 4 + f, :] = ref[:, h * half : (h + 1) * half].astype(F32)
    for x in range(local_x):
        packed[x, :half, :] = (conc_out[x] - CENTRE).astype(BF16)
        tail = jnp.concatenate([walls_out[x], jnp.zeros((8, half), F32)], axis=0)
        packed[x, half:, :] = tail.astype(BF16)


def tanh_units():
    c1 = math.sqrt(2.0 / math.pi)
    unit = (c1 * 0.044715) ** (1.0 / 3.0)
    return unit, c1 / unit


def high(v):
    return v.astype(BF16).astype(F32)


def prepare_kernel(
    cot_hbm, lift, weight_hbm, lift_rows, point_weight, bias, readout, conc_z,
    cot_z, mapped, terms, weigh, conc_out, flat, cot, weight, sems,
):
    cot_copy = pltpu.make_async_copy(cot_hbm, cot, sems.at[0])
    halves = [pltpu.make_async_copy(weight_hbm.at[p], weight.at[p], sems.at[1 + p]) for p in range(2)]
    for copy in (cot_copy, *halves):
        copy.start()
    cot_copy.wait()
    local_x = cot.shape[0]
    half = flat.shape[1]
    for k in range(half):
        flat[:, k, :] = cot[:, k * 128 : (k + 1) * 128]
    for x in range(local_x):
        cot_z[:, x, :] = flat[x].T
    for x in range(local_x):
        flat[x] = conc_z[:, x, :].T
    for k in range(half):
        conc_out[:, k * 128 : (k + 1) * 128] = flat[:, k, :]
    channels = weight.shape[1]
    rows = local_x * channels
    unit, _ = tanh_units()
    factors = jnp.concatenate([lift_rows[...], jnp.zeros((5, channels), F32)], axis=0)
    pointwise = dot_nt(point_weight[...].astype(F32), factors, HI)
    eye = (
        lax.broadcasted_iota(jnp.int32, (channels, channels), 0)
        == lax.broadcasted_iota(jnp.int32, (channels, channels), 1)
    ).astype(F32)
    columns = dot_nt(eye, jnp.concatenate([bias[...], jnp.zeros((7, channels), F32)], axis=0), HI)
    a0, a1 = unit * pointwise[:, 0:1], unit * pointwise[:, 1:2]
    a2 = unit * (pointwise[:, 2:3] + columns[:, 0:1]) + CENTRE * a0
    lane = lax.broadcasted_iota(jnp.int32, (channels, 32), 1)
    a0_high, a2_high = high(a0), high(a2)
    for x in range(local_x):
        block = jnp.zeros((channels, 32), F32)
        for at, value in (
            (0, a2_high), (1, a2 - a2_high),
            (16 + x, a0_high), (20 + x, a0_high), (24 + x, a0 - a0_high), (28 + x, a1),
        ):
            block = jnp.where(lane == at, value, block)
        terms[x * channels : (x + 1) * channels, :] = block.astype(BF16)
    owner = lax.broadcasted_iota(jnp.int32, (16, rows), 1) // channels
    slot = lax.broadcasted_iota(jnp.int32, (16, rows), 0)
    scaled = (0.5 / unit) * jnp.concatenate([readout[...]] * local_x, axis=1)
    weigh[...] = jnp.where(
        slot == owner, high(scaled), jnp.where(slot - 8 == owner, scaled - high(scaled), 0.0)
    ).astype(BF16)
    for p in range(2):
        halves[p].wait()
        acc = [jnp.zeros(weight.shape[2:], F32) for _ in range(3)]
        for c in range(channels):
            w = weight[p, c].astype(F32)
            acc = [acc[r] + lift[r, c] * w for r in range(3)]
        for r in range(3):
            mapped[r, p] = acc[r]


def split_parity(spread, at, count):
    wide = spread.shape[1] // 2
    return spread[at : at + count, :wide] + spread[at + 4 : at + 4 + count, wide:]


def early_kernel(
    own, own_walls, index_hbm, profiles_hbm, perm_hbm, back_hbm, wave_hbm, place_c_hbm, place_w_hbm,
    planes, fields, inlet, perm, back, wave_yt, place_c, place_w, index, profiles, sems,
):
    moves = (
        (index_hbm, index), (perm_hbm, perm), (profiles_hbm, profiles), (wave_hbm, wave_yt),
        (place_c_hbm, place_c), (place_w_hbm, place_w), (back_hbm, back),
    )
    copies = [pltpu.make_async_copy(src, dst, sems.at[k]) for k, (src, dst) in enumerate(moves)]
    for copy in copies:
        copy.start()
    local_x = own.shape[0]
    half = own.shape[1]
    for x in range(local_x):
        planes[x] = own[x].T
    for copy in copies[:3]:
        copy.wait()
    profile = index[...].astype(F32)
    gap = jnp.zeros((3, half), F32)
    walls = [own_walls[x] for x in range(local_x)]
    walls.append(jnp.concatenate([profile[:, :half], gap, profile[:, half:], gap], axis=0))
    spread = dot(jnp.concatenate(walls, axis=0), perm[...], HI)
    for x in range(local_x):
        fields[4 * x : 4 * x + 4] = split_parity(spread, 8 * x, 4)
    chosen = split_parity(spread, 8 * local_x, 1)
    pick = lax.broadcasted_iota(jnp.int32, (PROFILES, 2 * half), 0).astype(F32)
    onehot = (jnp.abs(pick - chosen) < 0.5).astype(F32)
    plane = dot_tn(profiles[...], onehot, HI)
    inlet[...] = jnp.concatenate([plane[:, :half], plane[:, half:]], axis=0)
    for copy in copies[3:]:
        copy.wait()


def transport_kernel(
    devices, across, within, own, own_fields, inlet, perm, back, wave_yt, place_c, place_w,
    cover_out, conc_z, cover_z, send, buf,
):
    local_x = own.shape[0]
    half = own.shape[2]
    depth = own.shape[1] // 2
    rows = 3 * local_x
    sides = [r for r in range(rows) if r // local_x != 1]
    walls = []
    even = lax.axis_index("slab") % 2 == 0
    for r in sides:
        x = r % local_x
        near, far = within[x].astype(F32), across[x].astype(F32)
        here = jnp.where(even, far, near) if r < local_x else jnp.where(even, near, far)
        buf[0, r] = (here[:half] + CENTRE).T
        walls.append(here[half : half + 8])
    for x in range(local_x):
        buf[0, local_x + x] = own[x]
    spread = dot(jnp.concatenate(walls, axis=0), perm[...], HI)
    fields = [own_fields[4 * (r % local_x) : 4 * (r % local_x) + 4] for r in range(rows)]
    for k, r in enumerate(sides):
        fields[r] = split_parity(spread, 8 * k, 4)
    height = lax.broadcasted_iota(jnp.int32, (depth, half), 0).astype(F32)
    height = (height + 0.5) / depth
    speed = PEAK_SPEED * 4.0 * height * (1.0 - height)
    speed = jnp.concatenate([speed, speed], axis=0)
    keep = (1.0 - 6.0 * DIFFUSIVITY) - speed
    carried = DIFFUSIVITY + speed
    first = lax.axis_index("slab") == 0
    last = lax.axis_index("slab") == devices - 1
    cover = [f[0:1] for f in fields]
    for step in range(STEPS):
        cur, nxt = step % 2, (step + 1) % 2
        for r in range(1 + step, rows - 1 - step):
            c = buf[cur, r]
            behind = buf[cur, r - 1]
            ahead = buf[cur, r + 1]
            if r == local_x:
                behind = jnp.where(first, inlet[...], behind)
            if r == 2 * local_x - 1:
                ahead = jnp.where(last, c, ahead)
            even, odd = c[:depth], c[depth:]
            side = jnp.concatenate(
                [odd + pltpu.roll(odd, 1, 1), even + pltpu.roll(even, half - 1, 1)], axis=0
            )
            below = jnp.concatenate([even[:1], even[:-1], odd[:1], odd[:-1]], axis=0)
            above = jnp.concatenate([even[1:], even[-1:], odd[1:], odd[-1:]], axis=0)
            around = ahead + side + below + above
            f = fields[r]
            wall = jnp.concatenate([even[:1], odd[:1]], axis=1)
            uptake = f[3:4] * (f[1:2] * wall * (1.0 - cover[r]) - f[2:3] * cover[r])
            new = keep * c + carried * behind + DIFFUSIVITY * around
            buf[nxt, r] = new
            buf[nxt, r, 0:1] = new[0:1] - uptake[:, :half]
            buf[nxt, r, depth : depth + 1] = new[depth : depth + 1] - uptake[:, half:]
            cover[r] = cover[r] + uptake
    cur = STEPS % 2
    covers = jnp.concatenate(cover[local_x : 2 * local_x], axis=0)
    cover_z[...] = covers
    planes = [buf[cur, local_x + i] for i in range(local_x)]
    evens = jnp.concatenate([p[:depth] for p in planes], axis=0)
    odds = jnp.concatenate([p[depth:] for p in planes], axis=0)
    along = dot_nt(wave_yt[:, :half], evens, HI) + dot_nt(wave_yt[:, half:], odds, HI)
    padded = jnp.concatenate([covers, jnp.zeros((8 - local_x, 2 * half), F32)], axis=0)
    walls_y = dot_nt(wave_yt[...], padded, HI)
    send[...] = (
        dot(along[:KY], place_c[0], HI)
        + dot(along[KY:], place_c[1], HI)
        + dot(walls_y[:KY], place_w[0], HI)
        + dot(walls_y[KY:], place_w[1], HI)
    )
    cover_out[...] = dot(covers, back[...], HI)
    for i in range(local_x):
        conc_z[:, i, :] = planes[i]


def mixing_kernel(ones_value, got, ax, bx, mapped, inv_out, spec_out, stage):
    modes = mapped.shape[3]
    channels = mapped.shape[2]
    own_j = modes // KX
    local_x = inv_out.shape[1] // channels
    blocks = inv_out.shape[0] // own_j
    spread = dot_tn(got[...], ax[...], HI)
    keep = lax.broadcasted_iota(jnp.int32, (own_j, modes), 1) // KX == lax.broadcasted_iota(
        jnp.int32, (own_j, modes), 0
    )
    spec = []
    for f in range(2):
        acc = jnp.zeros((own_j, 2 * KX), F32)
        for k in range(2 * local_x):
            at = (f * 2 * local_x + k) * own_j
            acc = acc + spread[at : at + own_j, k * 2 * KX : (k + 1) * 2 * KX]
        for q in range(2):
            tiled = jnp.concatenate([acc[:, q * KX : (q + 1) * KX]] * own_j, axis=1)
            spec.append(jnp.sum(jnp.where(keep, tiled, 0.0), axis=0, keepdims=True))
    cr, ci, wr, wi = spec
    lane = lax.broadcasted_iota(jnp.int32, (1, modes), 1)
    ones = jnp.where((lane == 0) & (lax.axis_index("slab") == 0), ones_value, 0.0)
    zero = jnp.zeros((1, modes), F32)
    spec_out[:, :modes] = jnp.concatenate([cr, wr, ones] + [zero] * 5, axis=0)
    spec_out[:, modes:] = jnp.concatenate([ci, wi] + [zero] * 6, axis=0)
    mixed_r = cr * mapped[0, 0] - ci * mapped[0, 1] + wr * mapped[1, 0] - wi * mapped[1, 1] + ones * mapped[2, 0]
    mixed_i = cr * mapped[0, 1] + ci * mapped[0, 0] + wr * mapped[1, 1] + wi * mapped[1, 0] + ones * mapped[2, 1]
    mixed_r = mixed_r.astype(BF16).astype(F32).T
    mixed_i = mixed_i.astype(BF16).astype(F32).T
    for j in range(own_j):
        rhs = jnp.concatenate([mixed_r[j * KX : (j + 1) * KX], mixed_i[j * KX : (j + 1) * KX]], axis=0)
        rhs = rhs.astype(BF16)
        out = dot(bx[0], rhs) + dot(bx[1], rhs)
        line = jnp.concatenate([out[i * blocks : (i + 1) * blocks] for i in range(local_x)], axis=1)
        for h in range(line.shape[1] // 128):
            if own_j == 1:
                stage[h] = line[:, h * 128 : (h + 1) * 128]
            else:
                stage[h, pl.ds(j, blocks, own_j), :] = line[:, h * 128 : (h + 1) * 128]
    for h in range(stage.shape[0]):
        inv_out[:, h * 128 : (h + 1) * 128] = stage[h].astype(BF16)


def tail_blocks(own_j):
    return -(-3 // (2 * own_j))


def extra_rows(conc_z, cover_z, z):
    depth = conc_z.shape[0] // 2
    conc = jnp.concatenate([conc_z[z], conc_z[depth + z]], axis=1) - CENTRE
    wall = jnp.where(z == 0, cover_z[...], 0.0)
    return jnp.concatenate([high(conc), conc - high(conc), high(conc), wall], axis=0).astype(BF16)


def layer_kernel(
    own_j, inv, conc_z, cot_z, cover_z, terms, readout, ez, fwd,
    grad_out, lhs, waves, ext_all, point, pre_a, pre_b, grads_a, grads_b,
):
    channels = readout.shape[1]
    local_x = cover_z.shape[0]
    half = cot_z.shape[2]
    span = 2 * half
    depth = cot_z.shape[0] // 2
    groups = depth // ZG
    rows = local_x * channels
    pairs = 2 * KY
    wide = ZG * pairs
    iscale = 1.0 / math.sqrt(KX * KY * KZ)
    unit, kappa = tanh_units()
    flipped = inv[...].astype(F32).T.astype(BF16)
    lifted = (unit * dot(flipped, ez[...])).astype(BF16)
    for g in range(groups):
        lhs[g] = lifted[:, g * wide : (g + 1) * wide]
    wide_readout = jnp.concatenate([readout[...]] * local_x, axis=1)
    owner = lax.broadcasted_iota(jnp.int32, (16, rows), 1) // channels
    slot = lax.broadcasted_iota(jnp.int32, (16, rows), 0)
    point[...] = jnp.zeros(point.shape, F32)
    grads_b[...] = jnp.zeros(grads_b.shape, BF16)
    by = fwd[0, :pairs, :]
    pres, grads = (pre_a, pre_b), (grads_a, grads_b)

    def before(g, i, pre):
        z = g * ZG + i
        ext = extra_rows(conc_z, cover_z, z)
        ext_all[z] = ext
        both = jnp.concatenate([lhs[g], terms[...]], axis=1)
        pre[...] = dot(both, jnp.concatenate([fwd[i], ext], axis=0))

    def after(z, grad):
        sums = dot_nt(jnp.concatenate([by, ext_all[z]], axis=0), grad[...])
        waves[pl.ds(pl.multiple_of(z * pairs, pairs), pairs), :] = sums[:pairs].astype(BF16)
        point[:16] += sums[pairs:]
        point[16:] += sums[:8]

    before(0, 0, pre_a)

    def group(g, carry):
        for i in range(ZG):
            z = g * ZG + i
            this, other = i % 2, (i + 1) % 2
            if i < ZG - 1:
                before(g, i + 1, pres[other])
            else:
                before(jnp.minimum(g + 1, groups - 1), 0, pres[other])
            after(jnp.maximum(z - 1, 0), grads[other])
            cot = jnp.concatenate([cot_z[z], cot_z[depth + z]], axis=1)
            for x in range(local_x):
                here = slice(x * channels, (x + 1) * channels)
                y = pres[this][here, :]
                u = y * (y * y + kappa)
                t = jnp.tanh(u)
                s = 1.0 + t
                slope = u - (2.0 / 3.0 * kappa) * y
                grad = s * (1.0 / 3.0 + slope * (1.0 - t)) * cot[x : x + 1]
                grads[this][here, :] = grad.astype(BF16)
        return carry

    def pair(h, carry):
        return group(2 * h + 1, group(2 * h, carry))

    lax.fori_loop(0, groups // 2, pair, 0)
    after(depth - 1, grads_b)
    total = dot(ez[...], waves[...])
    grad_row = 1.5 * wide_readout
    grad_out[:, :rows] = (total * (iscale * grad_row)).astype(BF16)
    mine = point[:16]
    with_conc = jnp.sum(jnp.where((slot < 8) & (slot % 4 == owner), mine, 0.0), axis=0, keepdims=True)
    with_wall = jnp.sum(jnp.where(slot == 12 + owner, mine, 0.0), axis=0, keepdims=True)
    sums = jnp.concatenate([with_conc, with_wall, point[16:17], jnp.zeros((13, rows), F32)], axis=0) * grad_row
    parts = [sums[:, x * channels : (x + 1) * channels] for x in range(local_x)]
    sums = parts[0]
    for part in parts[1:]:
        sums = sums + part
    both = jnp.concatenate([high(sums), sums - high(sums)], axis=1).astype(BF16)
    out_rows = grad_out.shape[0]
    for b in range(tail_blocks(own_j)):
        row = lax.broadcasted_iota(jnp.int32, (out_rows, 16), 0) % (2 * own_j) + b * 2 * own_j
        pick = (row == lax.broadcasted_iota(jnp.int32, (out_rows, 16), 1)).astype(BF16)
        grad_out[:, rows + b * 128 : rows + (b + 1) * 128] = dot(pick, both).astype(BF16)


def predict_kernel(
    lhs, conc_z, cover_z, terms, weigh, fwd, pred_out, pred, flat, pre_a, pre_b, hidden_a, hidden_b
):
    local_x = pred_out.shape[0]
    half = conc_z.shape[2]
    groups = lhs.shape[0]
    depth = groups * ZG
    _, kappa = tanh_units()
    pres, hiddens = (pre_a, pre_b), (hidden_a, hidden_b)
    hidden_b[...] = jnp.zeros(hidden_b.shape, BF16)

    def before(g, i, pre):
        both = jnp.concatenate([lhs[g], terms[...]], axis=1)
        pre[...] = dot(both, jnp.concatenate([fwd[i], extra_rows(conc_z, cover_z, g * ZG + i)], axis=0))

    def after(z, hidden):
        line = dot(weigh[...], hidden[...])
        line = line[:local_x] + line[8 : 8 + local_x]
        pred[z] = line[:, :half]
        pred[depth + z] = line[:, half:]

    before(0, 0, pre_a)

    def group(g, carry):
        for i in range(ZG):
            z = g * ZG + i
            this, other = i % 2, (i + 1) % 2
            if i < ZG - 1:
                before(g, i + 1, pres[other])
            else:
                before(jnp.minimum(g + 1, groups - 1), 0, pres[other])
            after(jnp.maximum(z - 1, 0), hiddens[other])
            for k in range(local_x):
                here = slice(k * pre_a.shape[0] // local_x, (k + 1) * pre_a.shape[0] // local_x)
                y = pres[this][here, :]
                t = jnp.tanh(y * (y * y + kappa))
                hiddens[this][here, :] = (y * (1.0 + t)).astype(BF16)
        return carry

    def pair(h, carry):
        return group(2 * h + 1, group(2 * h, carry))

    lax.fori_loop(0, groups // 2, pair, 0)
    after(depth - 1, hidden_b)
    for x in range(local_x):
        flat[x] = pred[:, x, :].T
    for k in range(half):
        pred_out[:, k * 128 : (k + 1) * 128] = flat[:, k, :]


def outer_kernel(own_j, got, spec, gx, lift, modes_hbm, point_out, result, factor, stage, sems):
    channels = lift.shape[1]
    modes = spec.shape[1] // 2
    rows = got.shape[1] - 128 * tail_blocks(own_j)
    local_x = rows // channels
    factors = jnp.concatenate([lift[...], jnp.zeros((5, channels), F32)], axis=0)
    v = dot_tn(factors, spec[...], HI)
    v_r, v_i = v[:, :modes], v[:, modes:]
    blocks = got.shape[0] // own_j
    halves = rows // 128
    for h in range(halves):
        stage[h] = got[:, h * 128 : (h + 1) * 128].astype(F32)
    lines = [
        [stage[h, pl.ds(j, blocks, own_j), :] if own_j > 1 else stage[h] for h in range(halves)]
        for j in range(own_j)
    ]
    per_half = 128 // channels
    parts_r, parts_i = [], []
    tall = []
    for x in range(local_x):
        h, at = x // per_half, (x % per_half) * channels
        tall.append(jnp.concatenate([lines[j][h][:, at : at + channels] for j in range(own_j)], axis=1))
    acc = dot(gx[...], jnp.concatenate(tall, axis=0).astype(BF16))
    acc = acc[: 2 * KX] + acc[2 * KX :]
    for j in range(own_j):
        parts_r.append(acc[:KX, j * channels : (j + 1) * channels])
        parts_i.append(acc[KX:, j * channels : (j + 1) * channels])
    dr = jnp.concatenate(parts_r, axis=0).T
    di = jnp.concatenate(parts_i, axis=0).T
    factor[0], factor[1] = v_r, v_i
    per = channels // OUT_BLOCKS

    def leave(b, q):
        here = pl.ds(b * per, per)
        return pltpu.make_async_copy(result.at[q, here], modes_hbm.at[q, here], sems.at[q, b])

    def block(b, carry):
        for k in range(per):
            c = b * per + k
            vr, vi = factor[0, pl.ds(c, 1), :], factor[1, pl.ds(c, 1), :]
            result[0, c] = vr * dr + vi * di
            result[1, c] = vr * di - vi * dr
        leave(b, 0).start()
        leave(b, 1).start()
        return carry

    lax.fori_loop(0, OUT_BLOCKS, block, 0)
    sums = jnp.zeros((8, 128), F32)
    for b in range(tail_blocks(own_j)):
        tail = got[:, rows + b * 128 : rows + (b + 1) * 128]
        at = lax.broadcasted_iota(jnp.int32, (8, got.shape[0]), 1) % (2 * own_j) + b * 2 * own_j
        pick = (at == lax.broadcasted_iota(jnp.int32, (8, got.shape[0]), 0)).astype(BF16)
        sums = sums + dot(pick, tail)
    sums = sums[:, :channels] + sums[:, channels:]
    row = lax.broadcasted_iota(jnp.int32, (8, channels), 0)
    base = jnp.where(row == 2, factors + CENTRE * lift[0:1], factors)
    point_out[...] = dot_tn(jnp.where(row < 3, sums, 0.0), base, HI)
    for b in range(OUT_BLOCKS):
        leave(b, 0).wait()
        leave(b, 1).wait()


def params(mib):
    return pltpu.CompilerParams(vmem_limit_bytes=mib * 1024 * 1024)


def cost(micros):
    return pl.CostEstimate(flops=int(micros * 6e8), transcendentals=0, bytes_accessed=int(micros * 3.4e6))


def in_hbm(array):
    return pltpu.with_memory_space_constraint(array, pltpu.HBM)


def hbm(count):
    return [pl.BlockSpec(memory_space=pltpu.HBM) for _ in range(count)]


def vmem(count):
    return [pl.BlockSpec(memory_space=pltpu.VMEM) for _ in range(count)]


def body(
    conc_init, cover_init, rate_on, rate_off, site_mask, inlet_profiles, inlet_index, lift,
    mode_weight, point_weight, point_bias, readout, cotangent,
):
    devices = lax.axis_size("slab")
    local_x, plane = conc_init.shape
    depth = inlet_profiles.shape[1]
    span = plane // depth
    half = span // 2
    channels = lift.shape[1]
    modes = mode_weight.shape[0]
    own_j = modes // KX
    total_x = local_x * devices
    tab = {k: jnp.asarray(v) for k, v in tables(span, depth, total_x, devices, local_x).items()}
    sds = jax.ShapeDtypeStruct
    smem = pl.BlockSpec(memory_space=pltpu.SMEM)

    pack, conc, walls = pl.pallas_call(
        pack_kernel,
        name="pack",
        out_shape=(
            sds((local_x, half + 16, 2 * depth), BF16),
            sds((local_x, half, 2 * depth), F32),
            sds((local_x, 8, half), F32),
        ),
        in_specs=hbm(5),
        out_specs=vmem(3),
        scratch_shapes=[pltpu.VMEM(conc_init.shape, F32)]
        + [pltpu.VMEM(cover_init.shape, F32)] * 3
        + [pltpu.VMEM(site_mask.shape, jnp.int32), pltpu.SemaphoreType.DMA((5,))],
        compiler_params=params(4),
        cost_estimate=cost(0.3),
    )(*map(in_hbm, (conc_init, cover_init, rate_on, rate_off, site_mask)))
    seams = [(i, i + 1) for i in range(1, devices - 1, 2)]
    across = lax.ppermute(pack, "slab", seams + [(j, i) for i, j in seams])
    within = lax.ppermute(pack, "slab", [(i, i ^ 1) for i in range(devices)])
    constants = [tab[k] for k in ("perm", "back", "wave_yt", "place_c", "place_w")]
    early = pl.pallas_call(
        early_kernel,
        name="early",
        out_shape=(
            sds((local_x, 2 * depth, half), F32),
            sds((4 * local_x, span), F32),
            sds((2 * depth, half), F32),
            *(sds(v.shape, v.dtype) for v in constants),
        ),
        in_specs=vmem(2) + hbm(7),
        out_specs=vmem(8),
        scratch_shapes=[
            pltpu.VMEM((1, span), jnp.int32), pltpu.VMEM(inlet_profiles.shape, F32), pltpu.SemaphoreType.DMA((7,)),
        ],
        compiler_params=params(8),
        cost_estimate=cost(1.5),
    )(conc, walls, *map(in_hbm, (inlet_index.reshape(1, span), inlet_profiles, *constants)))
    cover_out, conc_z, cover_z, send = pl.pallas_call(
        functools.partial(transport_kernel, devices),
        name="transport",
        out_shape=(
            sds((local_x, span), F32),
            sds((2 * depth, local_x, half), F32),
            sds((local_x, span), F32),
            sds((KY, 4 * local_x * KZ), F32),
        ),
        in_specs=vmem(10),
        out_specs=vmem(4),
        scratch_shapes=[pltpu.VMEM((2, 3 * local_x, 2 * depth, half), F32)],
        compiler_params=params(8),
        cost_estimate=cost(3.0),
    )(across, within, *early)
    cot_z, mapped, terms, weigh, conc_out = pl.pallas_call(
        prepare_kernel,
        name="prepare",
        out_shape=(
            sds((2 * depth, local_x, half), F32),
            sds((3, 2, channels, modes), F32),
            sds((local_x * channels, 32), BF16),
            sds((16, local_x * channels), BF16),
            sds(conc_init.shape, F32),
        ),
        in_specs=hbm(1) + [smem] + hbm(1) + vmem(5),
        out_specs=vmem(5),
        scratch_shapes=[
            pltpu.VMEM((local_x, half, 2 * depth), F32),
            pltpu.VMEM(cotangent.shape, F32),
            pltpu.VMEM((2, channels, channels, modes), BF16),
            pltpu.SemaphoreType.DMA((3,)),
        ],
        compiler_params=params(8),
        cost_estimate=cost(2.0),
    )(
        in_hbm(cotangent), lift, in_hbm(mode_weight.transpose(1, 2, 3, 0)),
        lift, point_weight, point_bias.reshape(1, -1), readout.reshape(1, -1), conc_z,
    )
    if own_j != KZ:
        send = send.reshape(KY, 4 * local_x, KZ // own_j, own_j).transpose(0, 2, 1, 3)
        send = send.reshape(devices, 4 * local_x * own_j)
    got = lax.all_to_all(send, "slab", 0, 0, tiled=True)
    ones = math.sqrt(total_x * plane)
    inv, spec = pl.pallas_call(
        functools.partial(mixing_kernel, ones),
        name="mixing",
        out_shape=(
            sds((2 * KY * KZ, local_x * channels), BF16),
            sds((8, 2 * modes), F32),
        ),
        in_specs=vmem(4),
        out_specs=vmem(2),
        scratch_shapes=[pltpu.VMEM((local_x * channels // 128, 2 * KY * KZ, 128), F32)],
        compiler_params=params(4),
        cost_estimate=cost(1.6),
    )(got, tab["ax"], tab["bx"], mapped)
    inv = lax.all_to_all(inv, "slab", 0, 0, tiled=True)
    rows = local_x * channels
    wide = ZG * 2 * KY
    grad, lhs = pl.pallas_call(
        functools.partial(layer_kernel, own_j),
        name="layer",
        out_shape=(
            sds((2 * KY * KZ, rows + 128 * tail_blocks(own_j)), BF16),
            sds((depth // ZG, rows, wide), BF16),
        ),
        in_specs=vmem(8),
        out_specs=vmem(2),
        scratch_shapes=[
            pltpu.VMEM((depth * 2 * KY, rows), BF16),
            pltpu.VMEM((depth, 16, span), BF16),
            pltpu.VMEM((24, rows), F32),
        ]
        + [pltpu.VMEM((rows, span), F32)] * 2
        + [pltpu.VMEM((rows, span), BF16)] * 2,
        compiler_params=params(16),
        cost_estimate=cost(11.0),
    )(inv, conc_z, cot_z, cover_z, terms, readout.reshape(1, -1), tab["ez"], tab["fwd"])
    grad = lax.all_to_all(grad, "slab", 0, 0, tiled=True)
    pred = pl.pallas_call(
        predict_kernel,
        name="predict",
        out_shape=sds((local_x, plane), F32),
        in_specs=vmem(6),
        out_specs=pl.BlockSpec(memory_space=pltpu.VMEM),
        scratch_shapes=[pltpu.VMEM((2 * depth, local_x, half), F32), pltpu.VMEM((local_x, half, 2 * depth), F32)]
        + [pltpu.VMEM((rows, span), F32)] * 2
        + [pltpu.VMEM((rows, span), BF16)] * 2,
        compiler_params=params(8),
        cost_estimate=cost(5.5),
    )(lhs, conc_z, cover_z, terms, weigh, tab["fwd"])
    grad_modes, grad_point = pl.pallas_call(
        functools.partial(outer_kernel, own_j),
        name="outer",
        out_shape=(
            sds((2, channels, channels, modes), F32),
            sds((channels, channels), F32),
        ),
        in_specs=vmem(4),
        out_specs=hbm(1) + vmem(1),
        scratch_shapes=[
            pltpu.VMEM((2, channels, channels, modes), F32),
            pltpu.VMEM((2, channels, modes), F32),
            pltpu.VMEM((rows // 128, 2 * KY * KZ, 128), F32),
            pltpu.SemaphoreType.DMA((2, OUT_BLOCKS)),
        ],
        compiler_params=params(12),
        cost_estimate=cost(3.0),
    )(grad, spec, tab["gx"], lift)
    return (
        conc_out,
        cover_out,
        pred,
        grad_modes.transpose(3, 0, 1, 2),
        grad_point,
    )


def solution(mesh):
    placed = (
        P(("groups", "slab"), None),
        P(("groups", "slab"), None),
        P(("groups", "slab"), None),
        P(("groups", "slab"), None),
        P(("groups", "slab"), None),
        P("groups", None),
        P("groups"),
        P(),
        P("slab", None, None, None),
        P(),
        P(),
        P(),
        P(("groups", "slab"), None),
    )
    return jax.shard_map(
        body,
        mesh=mesh,
        in_specs=placed,
        out_specs=(
            P(("groups", "slab"), None),
            P(("groups", "slab"), None),
            P(("groups", "slab"), None),
            P(("groups", "slab"), None, None, None),
            P("groups", None),
        ),
        check_vma=False,
    )
```

```python
import functools
import math

import jax
import jax.numpy as jnp
import numpy as np
from jax import lax
from jax.experimental import pallas as pl
from jax.experimental.pallas import tpu as pltpu
from jax.sharding import PartitionSpec as P

KX = 16
KY = 16
KZ = 8
STEPS = 4
PROFILES = 8

PEAK_SPEED = 0.6
DIFFUSIVITY = 0.06
CENTRE = 1.1
OUT_BLOCKS = 8
ZG = 4

HI = lax.Precision.HIGHEST
F32 = jnp.float32
BF16 = jnp.bfloat16


def dot(a, b, precision=None):
    return jnp.dot(a, b, preferred_element_type=F32, precision=precision)


def dot_nt(a, b, precision=None):
    return lax.dot_general(a, b, (((1,), (1,)), ((), ())), preferred_element_type=F32, precision=precision)


def dot_tn(a, b, precision=None):
    return lax.dot_general(a, b, (((0,), (0,)), ((), ())), preferred_element_type=F32, precision=precision)


def split(table):
    high = table.astype(np.float32).astype(jnp.bfloat16)
    return high, (table - high.astype(np.float64)).astype(np.float32).astype(jnp.bfloat16)


def tables(span, depth, total_x, devices, local_x):
    half = span // 2
    own_j = KY * KZ // devices
    tab = {}
    lane = np.arange(half)
    perm = np.zeros((half, 4 * half), np.float32)
    for h in range(2):
        for par in range(2):
            k = (h * half + lane - par) / 2.0
            good = (k == np.floor(k)) & (k >= 0)
            perm[lane[good], (2 * h + par) * half + k[good].astype(int)] = 1.0
    tab["perm"] = perm
    back = np.zeros((span, span), np.float32)
    for par in range(2):
        back[par * half + lane, 2 * lane + par] = 1.0
    tab["back"] = back
    ky = np.arange(KY)
    kz = np.arange(KZ)
    kx = np.arange(KX)
    y_of = np.concatenate([2 * lane, 2 * lane + 1])
    alpha = 2 * np.pi * ((y_of[:, None] * ky[None, :]) % span) / span
    tab["wave_yt"] = np.concatenate([np.cos(alpha), np.sin(alpha)], axis=1).T.astype(np.float32)
    z = np.arange(depth)
    beta = 2 * np.pi * ((kz[:, None] * z[None, :]) % depth) / depth
    place_c = np.zeros((2, local_x, depth, 2, 2, local_x, KZ), np.float32)
    place_w = np.zeros((2, 8, 2, 2, local_x, KZ), np.float32)
    for i in range(local_x):
        place_c[0, i, :, 0, 0, i] = np.cos(beta).T
        place_c[1, i, :, 0, 0, i] = -np.sin(beta).T
        place_c[0, i, :, 0, 1, i] = -np.sin(beta).T
        place_c[1, i, :, 0, 1, i] = -np.cos(beta).T
        place_w[0, i, 1, 0, i] = 1.0
        place_w[1, i, 1, 1, i] = -1.0
    tab["place_c"] = place_c.reshape(2, local_x * depth, 4 * local_x * KZ)
    tab["place_w"] = place_w.reshape(2, 8, 4 * local_x * KZ)
    pairs = 2 * KY
    ez = np.zeros((2 * KY * KZ, depth, KY, 2), np.float32)
    for j in range(KY * KZ):
        a, b = j // KZ, j % KZ
        row = (j // own_j) * 2 * own_j + j % own_j
        ez[row, :, a, 0] = np.cos(beta[b])
        ez[row + own_j, :, a, 0] = -np.sin(beta[b])
        ez[row, :, a, 1] = -np.sin(beta[b])
        ez[row + own_j, :, a, 1] = -np.cos(beta[b])
    tab["ez"] = ez.reshape(2 * KY * KZ, depth * pairs).astype(jnp.bfloat16)
    by = np.stack([np.cos(alpha), np.sin(alpha)], axis=2).reshape(span, pairs)
    fwd = np.zeros((ZG, ZG * pairs + 16, span), np.float32)
    for i in range(ZG):
        fwd[i, i * pairs : (i + 1) * pairs] = by.T
        fwd[i, ZG * pairs : ZG * pairs + 2] = 1.0
    tab["fwd"] = fwd.astype(jnp.bfloat16)
    x = np.arange(total_x)
    gamma = 2 * np.pi * ((x[:, None] * kx[None, :]) % total_x) / total_x
    cg, sg = np.cos(gamma), np.sin(gamma)
    scale = 1.0 / math.sqrt(total_x * span * depth)
    ax = np.zeros((total_x, 2, 2, KX))
    ax[:, 0, 0], ax[:, 1, 0] = cg, sg
    ax[:, 0, 1], ax[:, 1, 1] = -sg, cg
    by_owner = ax.reshape(devices, local_x, 2, 2 * KX)
    tab["ax"] = (by_owner.transpose(0, 2, 1, 3) * scale).reshape(devices, -1).astype(np.float32)
    iscale = 1.0 / math.sqrt(KX * KY * KZ)
    bx = np.zeros((total_x, 2, 2, KX))
    bx[:, 0, 0], bx[:, 0, 1] = cg, -sg
    bx[:, 1, 0], bx[:, 1, 1] = sg, cg
    bx = bx.reshape(devices, local_x, 2, 2 * KX).transpose(1, 0, 2, 3) * iscale
    tab["bx"] = np.concatenate(split(bx.reshape(2 * total_x, 2 * KX)), axis=1)
    gx = by_owner.transpose(3, 1, 0, 2).reshape(2 * KX, 2 * total_x)
    tab["gx"] = np.concatenate(split(gx), axis=0)
    return tab


def pack_kernel(
    conc_hbm, cover_hbm, on_hbm, off_hbm, mask_hbm, packed, conc_out, walls_out,
    conc, cover, rate_on, rate_off, mask, sems,
):
    pairs = ((cover_hbm, cover), (on_hbm, rate_on), (off_hbm, rate_off), (mask_hbm, mask), (conc_hbm, conc))
    copies = [pltpu.make_async_copy(src, dst, sems.at[k]) for k, (src, dst) in enumerate(pairs)]
    for copy in copies:
        copy.start()
    for copy in copies:
        copy.wait()
    local_x = conc.shape[0]
    half = conc_out.shape[1]
    for k in range(half):
        conc_out[:, k, :] = conc[:, k * 128 : (k + 1) * 128]
    for f, ref in enumerate((cover, rate_on, rate_off, mask)):
        for h in range(2):
            walls_out[:, h * 4 + f, :] = ref[:, h * half : (h + 1) * half].astype(F32)
    for x in range(local_x):
        packed[x, :half, :] = (conc_out[x] - CENTRE).astype(BF16)
        tail = jnp.concatenate([walls_out[x], jnp.zeros((8, half), F32)], axis=0)
        packed[x, half:, :] = tail.astype(BF16)


def tanh_units():
    c1 = math.sqrt(2.0 / math.pi)
    unit = (c1 * 0.044715) ** (1.0 / 3.0)
    return unit, c1 / unit


def high(v):
    return v.astype(BF16).astype(F32)


def prepare_kernel(
    cot_hbm, lift, weight_hbm, lift_rows, point_weight, bias, readout, conc_z,
    cot_z, mapped, terms, weigh, conc_out, flat, cot, weight, sems,
):
    cot_copy = pltpu.make_async_copy(cot_hbm, cot, sems.at[0])
    halves = [pltpu.make_async_copy(weight_hbm.at[p], weight.at[p], sems.at[1 + p]) for p in range(2)]
    for copy in (cot_copy, *halves):
        copy.start()
    cot_copy.wait()
    local_x = cot.shape[0]
    half = flat.shape[1]
    for k in range(half):
        flat[:, k, :] = cot[:, k * 128 : (k + 1) * 128]
    for x in range(local_x):
        cot_z[:, x, :] = flat[x].T
    for x in range(local_x):
        flat[x] = conc_z[:, x, :].T
    for k in range(half):
        conc_out[:, k * 128 : (k + 1) * 128] = flat[:, k, :]
    channels = weight.shape[1]
    rows = local_x * channels
    unit, _ = tanh_units()
    factors = jnp.concatenate([lift_rows[...], jnp.zeros((5, channels), F32)], axis=0)
    pointwise = dot_nt(point_weight[...].astype(F32), factors, HI)
    eye = (
        lax.broadcasted_iota(jnp.int32, (channels, channels), 0)
        == lax.broadcasted_iota(jnp.int32, (channels, channels), 1)
    ).astype(F32)
    columns = dot_nt(eye, jnp.concatenate([bias[...], jnp.zeros((7, channels), F32)], axis=0), HI)
    a0, a1 = unit * pointwise[:, 0:1], unit * pointwise[:, 1:2]
    a2 = unit * (pointwise[:, 2:3] + columns[:, 0:1]) + CENTRE * a0
    lane = lax.broadcasted_iota(jnp.int32, (channels, 32), 1)
    a0_high, a2_high = high(a0), high(a2)
    for x in range(local_x):
        block = jnp.zeros((channels, 32), F32)
        for at, value in (
            (0, a2_high), (1, a2 - a2_high),
            (16 + x, a0_high), (20 + x, a0_high), (24 + x, a0 - a0_high), (28 + x, a1),
        ):
            block = jnp.where(lane == at, value, block)
        terms[x * channels : (x + 1) * channels, :] = block.astype(BF16)
    owner = lax.broadcasted_iota(jnp.int32, (16, rows), 1) // channels
    slot = lax.broadcasted_iota(jnp.int32, (16, rows), 0)
    scaled = (0.5 / unit) * jnp.concatenate([readout[...]] * local_x, axis=1)
    weigh[...] = jnp.where(
        slot == owner, high(scaled), jnp.where(slot - 8 == owner, scaled - high(scaled), 0.0)
    ).astype(BF16)
    for p in range(2):
        halves[p].wait()
        acc = [jnp.zeros(weight.shape[2:], F32) for _ in range(3)]
        for c in range(channels):
            w = weight[p, c].astype(F32)
            acc = [acc[r] + lift[r, c] * w for r in range(3)]
        for r in range(3):
            mapped[r, p] = acc[r]


def split_parity(spread, at, count):
    wide = spread.shape[1] // 2
    return spread[at : at + count, :wide] + spread[at + 4 : at + 4 + count, wide:]


def early_kernel(
    own, own_walls, index_hbm, profiles_hbm, perm_hbm, back_hbm, wave_hbm, place_c_hbm, place_w_hbm,
    planes, fields, inlet, perm, back, wave_yt, place_c, place_w, index, profiles, sems,
):
    moves = (
        (index_hbm, index), (perm_hbm, perm), (profiles_hbm, profiles), (wave_hbm, wave_yt),
        (place_c_hbm, place_c), (place_w_hbm, place_w), (back_hbm, back),
    )
    copies = [pltpu.make_async_copy(src, dst, sems.at[k]) for k, (src, dst) in enumerate(moves)]
    for copy in copies:
        copy.start()
    local_x = own.shape[0]
    half = own.shape[1]
    for x in range(local_x):
        planes[x] = own[x].T
    for copy in copies[:3]:
        copy.wait()
    profile = index[...].astype(F32)
    gap = jnp.zeros((3, half), F32)
    walls = [own_walls[x] for x in range(local_x)]
    walls.append(jnp.concatenate([profile[:, :half], gap, profile[:, half:], gap], axis=0))
    spread = dot(jnp.concatenate(walls, axis=0), perm[...], HI)
    for x in range(local_x):
        fields[4 * x : 4 * x + 4] = split_parity(spread, 8 * x, 4)
    chosen = split_parity(spread, 8 * local_x, 1)
    pick = lax.broadcasted_iota(jnp.int32, (PROFILES, 2 * half), 0).astype(F32)
    onehot = (jnp.abs(pick - chosen) < 0.5).astype(F32)
    plane = dot_tn(profiles[...], onehot, HI)
    inlet[...] = jnp.concatenate([plane[:, :half], plane[:, half:]], axis=0)
    for copy in copies[3:]:
        copy.wait()


def transport_kernel(
    devices, across, within, own, own_fields, inlet, perm, back, wave_yt, place_c, place_w,
    cover_out, conc_z, cover_z, send, buf,
):
    local_x = own.shape[0]
    half = own.shape[2]
    depth = own.shape[1] // 2
    rows = 3 * local_x
    sides = [r for r in range(rows) if r // local_x != 1]
    walls = []
    even = lax.axis_index("slab") % 2 == 0
    for r in sides:
        x = r % local_x
        near, far = within[x].astype(F32), across[x].astype(F32)
        here = jnp.where(even, far, near) if r < local_x else jnp.where(even, near, far)
        buf[0, r] = (here[:half] + CENTRE).T
        walls.append(here[half : half + 8])
    for x in range(local_x):
        buf[0, local_x + x] = own[x]
    spread = dot(jnp.concatenate(walls, axis=0), perm[...], HI)
    fields = [own_fields[4 * (r % local_x) : 4 * (r % local_x) + 4] for r in range(rows)]
    for k, r in enumerate(sides):
        fields[r] = split_parity(spread, 8 * k, 4)
    height = lax.broadcasted_iota(jnp.int32, (depth, half), 0).astype(F32)
    height = (height + 0.5) / depth
    speed = PEAK_SPEED * 4.0 * height * (1.0 - height)
    speed = jnp.concatenate([speed, speed], axis=0)
    keep = (1.0 - 6.0 * DIFFUSIVITY) - speed
    carried = DIFFUSIVITY + speed
    first = lax.axis_index("slab") == 0
    last = lax.axis_index("slab") == devices - 1
    cover = [f[0:1] for f in fields]
    for step in range(STEPS):
        cur, nxt = step % 2, (step + 1) % 2
        for r in range(1 + step, rows - 1 - step):
            c = buf[cur, r]
            behind = buf[cur, r - 1]
            ahead = buf[cur, r + 1]
            if r == local_x:
                behind = jnp.where(first, inlet[...], behind)
            if r == 2 * local_x - 1:
                ahead = jnp.where(last, c, ahead)
            even, odd = c[:depth], c[depth:]
            side = jnp.concatenate(
                [odd + pltpu.roll(odd, 1, 1), even + pltpu.roll(even, half - 1, 1)], axis=0
            )
            below = jnp.concatenate([even[:1], even[:-1], odd[:1], odd[:-1]], axis=0)
            above = jnp.concatenate([even[1:], even[-1:], odd[1:], odd[-1:]], axis=0)
            around = ahead + side + below + above
            f = fields[r]
            wall = jnp.concatenate([even[:1], odd[:1]], axis=1)
            uptake = f[3:4] * (f[1:2] * wall * (1.0 - cover[r]) - f[2:3] * cover[r])
            new = keep * c + carried * behind + DIFFUSIVITY * around
            buf[nxt, r] = new
            buf[nxt, r, 0:1] = new[0:1] - uptake[:, :half]
            buf[nxt, r, depth : depth + 1] = new[depth : depth + 1] - uptake[:, half:]
            cover[r] = cover[r] + uptake
    cur = STEPS % 2
    covers = jnp.concatenate(cover[local_x : 2 * local_x], axis=0)
    cover_z[...] = covers
    planes = [buf[cur, local_x + i] for i in range(local_x)]
    evens = jnp.concatenate([p[:depth] for p in planes], axis=0)
    odds = jnp.concatenate([p[depth:] for p in planes], axis=0)
    along = dot_nt(wave_yt[:, :half], evens, HI) + dot_nt(wave_yt[:, half:], odds, HI)
    padded = jnp.concatenate([covers, jnp.zeros((8 - local_x, 2 * half), F32)], axis=0)
    walls_y = dot_nt(wave_yt[...], padded, HI)
    send[...] = (
        dot(along[:KY], place_c[0], HI)
        + dot(along[KY:], place_c[1], HI)
        + dot(walls_y[:KY], place_w[0], HI)
        + dot(walls_y[KY:], place_w[1], HI)
    )
    cover_out[...] = dot(covers, back[...], HI)
    for i in range(local_x):
        conc_z[:, i, :] = planes[i]


def mixing_kernel(ones_value, got, ax, bx, mapped, inv_out, spec_out, stage):
    modes = mapped.shape[3]
    channels = mapped.shape[2]
    own_j = modes // KX
    local_x = inv_out.shape[1] // channels
    blocks = inv_out.shape[0] // own_j
    spread = dot_tn(got[...], ax[...], HI)
    keep = lax.broadcasted_iota(jnp.int32, (own_j, modes), 1) // KX == lax.broadcasted_iota(
        jnp.int32, (own_j, modes), 0
    )
    spec = []
    for f in range(2):
        acc = jnp.zeros((own_j, 2 * KX), F32)
        for k in range(2 * local_x):
            at = (f * 2 * local_x + k) * own_j
            acc = acc + spread[at : at + own_j, k * 2 * KX : (k + 1) * 2 * KX]
        for q in range(2):
            tiled = jnp.concatenate([acc[:, q * KX : (q + 1) * KX]] * own_j, axis=1)
            spec.append(jnp.sum(jnp.where(keep, tiled, 0.0), axis=0, keepdims=True))
    cr, ci, wr, wi = spec
    lane = lax.broadcasted_iota(jnp.int32, (1, modes), 1)
    ones = jnp.where((lane == 0) & (lax.axis_index("slab") == 0), ones_value, 0.0)
    zero = jnp.zeros((1, modes), F32)
    spec_out[:, :modes] = jnp.concatenate([cr, wr, ones] + [zero] * 5, axis=0)
    spec_out[:, modes:] = jnp.concatenate([ci, wi] + [zero] * 6, axis=0)
    mixed_r = cr * mapped[0, 0] - ci * mapped[0, 1] + wr * mapped[1, 0] - wi * mapped[1, 1] + ones * mapped[2, 0]
    mixed_i = cr * mapped[0, 1] + ci * mapped[0, 0] + wr * mapped[1, 1] + wi * mapped[1, 0] + ones * mapped[2, 1]
    mixed_r = mixed_r.astype(BF16).astype(F32).T
    mixed_i = mixed_i.astype(BF16).astype(F32).T
    rhs = [
        jnp.concatenate([part[j * KX : (j + 1) * KX] for j in range(own_j)], axis=1) for part in (mixed_r, mixed_i)
    ]
    all_out = dot(bx[...], jnp.concatenate(rhs + rhs, axis=0).astype(BF16))
    for j in range(own_j):
        out = all_out[:, j * channels : (j + 1) * channels]
        line = jnp.concatenate([out[i * blocks : (i + 1) * blocks] for i in range(local_x)], axis=1)
        for h in range(line.shape[1] // 128):
            if own_j == 1:
                stage[h] = line[:, h * 128 : (h + 1) * 128]
            else:
                stage[h, pl.ds(j, blocks, own_j), :] = line[:, h * 128 : (h + 1) * 128]
    for h in range(stage.shape[0]):
        inv_out[:, h * 128 : (h + 1) * 128] = stage[h].astype(BF16)


def tail_blocks(own_j):
    return -(-3 // (2 * own_j))


def extra_rows(conc_z, cover_z, z):
    depth = conc_z.shape[0] // 2
    conc = jnp.concatenate([conc_z[z], conc_z[depth + z]], axis=1) - CENTRE
    wall = jnp.where(z == 0, cover_z[...], 0.0)
    return jnp.concatenate([high(conc), conc - high(conc), high(conc), wall], axis=0).astype(BF16)


def layer_kernel(
    own_j, inv, conc_z, cot_z, cover_z, terms, readout, ez, fwd,
    grad_out, lhs, waves, ext_all, point, pre_a, pre_b, grads_a, grads_b,
):
    channels = readout.shape[1]
    local_x = cover_z.shape[0]
    half = cot_z.shape[2]
    span = 2 * half
    depth = cot_z.shape[0] // 2
    groups = depth // ZG
    rows = local_x * channels
    pairs = 2 * KY
    wide = ZG * pairs
    iscale = 1.0 / math.sqrt(KX * KY * KZ)
    unit, kappa = tanh_units()
    flipped = inv[...].astype(F32).T.astype(BF16)
    lifted = (unit * dot(flipped, ez[...])).astype(BF16)
    for g in range(groups):
        lhs[g] = lifted[:, g * wide : (g + 1) * wide]
    wide_readout = jnp.concatenate([readout[...]] * local_x, axis=1)
    owner = lax.broadcasted_iota(jnp.int32, (16, rows), 1) // channels
    slot = lax.broadcasted_iota(jnp.int32, (16, rows), 0)
    point[...] = jnp.zeros(point.shape, F32)
    grads_b[...] = jnp.zeros(grads_b.shape, BF16)
    by = fwd[0, :pairs, :]
    pres, grads = (pre_a, pre_b), (grads_a, grads_b)

    def before(g, i, pre):
        z = g * ZG + i
        ext = extra_rows(conc_z, cover_z, z)
        ext_all[z] = ext
        both = jnp.concatenate([lhs[g], terms[...]], axis=1)
        pre[...] = dot(both, jnp.concatenate([fwd[i], ext], axis=0))

    def after(z, grad):
        sums = dot_nt(jnp.concatenate([by, ext_all[z]], axis=0), grad[...])
        waves[pl.ds(pl.multiple_of(z * pairs, pairs), pairs), :] = sums[:pairs].astype(BF16)
        point[:16] += sums[pairs:]
        point[16:] += sums[:8]

    before(0, 0, pre_a)

    def group(g, carry):
        for i in range(ZG):
            z = g * ZG + i
            this, other = i % 2, (i + 1) % 2
            if i < ZG - 1:
                before(g, i + 1, pres[other])
            else:
                before(jnp.minimum(g + 1, groups - 1), 0, pres[other])
            after(jnp.maximum(z - 1, 0), grads[other])
            cot = jnp.concatenate([cot_z[z], cot_z[depth + z]], axis=1)
            for x in range(local_x):
                here = slice(x * channels, (x + 1) * channels)
                y = pres[this][here, :]
                u = y * (y * y + kappa)
                t = jnp.tanh(u)
                s = 1.0 + t
                slope = u - (2.0 / 3.0 * kappa) * y
                grad = s * (1.0 / 3.0 + slope * (1.0 - t)) * cot[x : x + 1]
                grads[this][here, :] = grad.astype(BF16)
        return carry

    def pair(h, carry):
        return group(2 * h + 1, group(2 * h, carry))

    lax.fori_loop(0, groups // 2, pair, 0)
    after(depth - 1, grads_b)
    total = dot(ez[...], waves[...])
    grad_row = 1.5 * wide_readout
    grad_out[:, :rows] = (total * (iscale * grad_row)).astype(BF16)
    mine = point[:16]
    with_conc = jnp.sum(jnp.where((slot < 8) & (slot % 4 == owner), mine, 0.0), axis=0, keepdims=True)
    with_wall = jnp.sum(jnp.where(slot == 12 + owner, mine, 0.0), axis=0, keepdims=True)
    sums = jnp.concatenate([with_conc, with_wall, point[16:17], jnp.zeros((13, rows), F32)], axis=0) * grad_row
    parts = [sums[:, x * channels : (x + 1) * channels] for x in range(local_x)]
    sums = parts[0]
    for part in parts[1:]:
        sums = sums + part
    both = jnp.concatenate([high(sums), sums - high(sums)], axis=1).astype(BF16)
    out_rows = grad_out.shape[0]
    for b in range(tail_blocks(own_j)):
        row = lax.broadcasted_iota(jnp.int32, (out_rows, 16), 0) % (2 * own_j) + b * 2 * own_j
        pick = (row == lax.broadcasted_iota(jnp.int32, (out_rows, 16), 1)).astype(BF16)
        grad_out[:, rows + b * 128 : rows + (b + 1) * 128] = dot(pick, both).astype(BF16)


def predict_kernel(
    lhs, conc_z, cover_z, terms, weigh, fwd, pred_out, pred, flat, pre_a, pre_b, hidden_a, hidden_b
):
    local_x = pred_out.shape[0]
    half = conc_z.shape[2]
    groups = lhs.shape[0]
    depth = groups * ZG
    _, kappa = tanh_units()
    pres, hiddens = (pre_a, pre_b), (hidden_a, hidden_b)
    hidden_b[...] = jnp.zeros(hidden_b.shape, BF16)

    def before(g, i, pre):
        both = jnp.concatenate([lhs[g], terms[...]], axis=1)
        pre[...] = dot(both, jnp.concatenate([fwd[i], extra_rows(conc_z, cover_z, g * ZG + i)], axis=0))

    def after(z, hidden):
        line = dot(weigh[...], hidden[...])
        line = line[:local_x] + line[8 : 8 + local_x]
        pred[z] = line[:, :half]
        pred[depth + z] = line[:, half:]

    before(0, 0, pre_a)

    def group(g, carry):
        for i in range(ZG):
            z = g * ZG + i
            this, other = i % 2, (i + 1) % 2
            if i < ZG - 1:
                before(g, i + 1, pres[other])
            else:
                before(jnp.minimum(g + 1, groups - 1), 0, pres[other])
            after(jnp.maximum(z - 1, 0), hiddens[other])
            for k in range(local_x):
                here = slice(k * pre_a.shape[0] // local_x, (k + 1) * pre_a.shape[0] // local_x)
                y = pres[this][here, :]
                t = jnp.tanh(y * (y * y + kappa))
                hiddens[this][here, :] = (y * (1.0 + t)).astype(BF16)
        return carry

    def pair(h, carry):
        return group(2 * h + 1, group(2 * h, carry))

    lax.fori_loop(0, groups // 2, pair, 0)
    after(depth - 1, hidden_b)
    for x in range(local_x):
        flat[x] = pred[:, x, :].T
    for k in range(half):
        pred_out[:, k * 128 : (k + 1) * 128] = flat[:, k, :]


def outer_kernel(own_j, got, spec, gx, lift, modes_hbm, point_out, result, factor, stage, sems):
    channels = lift.shape[1]
    modes = spec.shape[1] // 2
    rows = got.shape[1] - 128 * tail_blocks(own_j)
    local_x = rows // channels
    factors = jnp.concatenate([lift[...], jnp.zeros((5, channels), F32)], axis=0)
    v = dot_tn(factors, spec[...], HI)
    v_r, v_i = v[:, :modes], v[:, modes:]
    blocks = got.shape[0] // own_j
    halves = rows // 128
    for h in range(halves):
        stage[h] = got[:, h * 128 : (h + 1) * 128].astype(F32)
    lines = [
        [stage[h, pl.ds(j, blocks, own_j), :] if own_j > 1 else stage[h] for h in range(halves)]
        for j in range(own_j)
    ]
    per_half = 128 // channels
    parts_r, parts_i = [], []
    tall = []
    for x in range(local_x):
        h, at = x // per_half, (x % per_half) * channels
        tall.append(jnp.concatenate([lines[j][h][:, at : at + channels] for j in range(own_j)], axis=1))
    acc = dot(gx[...], jnp.concatenate(tall, axis=0).astype(BF16))
    acc = acc[: 2 * KX] + acc[2 * KX :]
    for j in range(own_j):
        parts_r.append(acc[:KX, j * channels : (j + 1) * channels])
        parts_i.append(acc[KX:, j * channels : (j + 1) * channels])
    dr = jnp.concatenate(parts_r, axis=0).T
    di = jnp.concatenate(parts_i, axis=0).T
    factor[0], factor[1] = v_r, v_i
    per = channels // OUT_BLOCKS

    def leave(b, q):
        here = pl.ds(b * per, per)
        return pltpu.make_async_copy(result.at[q, here], modes_hbm.at[q, here], sems.at[q, b])

    def block(b, carry):
        for k in range(per):
            c = b * per + k
            vr, vi = factor[0, pl.ds(c, 1), :], factor[1, pl.ds(c, 1), :]
            result[0, c] = vr * dr + vi * di
            result[1, c] = vr * di - vi * dr
        leave(b, 0).start()
        leave(b, 1).start()
        return carry

    lax.fori_loop(0, OUT_BLOCKS, block, 0)
    sums = jnp.zeros((8, 128), F32)
    for b in range(tail_blocks(own_j)):
        tail = got[:, rows + b * 128 : rows + (b + 1) * 128]
        at = lax.broadcasted_iota(jnp.int32, (8, got.shape[0]), 1) % (2 * own_j) + b * 2 * own_j
        pick = (at == lax.broadcasted_iota(jnp.int32, (8, got.shape[0]), 0)).astype(BF16)
        sums = sums + dot(pick, tail)
    sums = sums[:, :channels] + sums[:, channels:]
    row = lax.broadcasted_iota(jnp.int32, (8, channels), 0)
    base = jnp.where(row == 2, factors + CENTRE * lift[0:1], factors)
    point_out[...] = dot_tn(jnp.where(row < 3, sums, 0.0), base, HI)
    for b in range(OUT_BLOCKS):
        leave(b, 0).wait()
        leave(b, 1).wait()


def params(mib):
    return pltpu.CompilerParams(vmem_limit_bytes=mib * 1024 * 1024)


def cost(micros):
    return pl.CostEstimate(flops=int(micros * 6e8), transcendentals=0, bytes_accessed=int(micros * 3.4e6))


def in_hbm(array):
    return pltpu.with_memory_space_constraint(array, pltpu.HBM)


def hbm(count):
    return [pl.BlockSpec(memory_space=pltpu.HBM) for _ in range(count)]


def vmem(count):
    return [pl.BlockSpec(memory_space=pltpu.VMEM) for _ in range(count)]


def body(
    conc_init, cover_init, rate_on, rate_off, site_mask, inlet_profiles, inlet_index, lift,
    mode_weight, point_weight, point_bias, readout, cotangent,
):
    devices = lax.axis_size("slab")
    local_x, plane = conc_init.shape
    depth = inlet_profiles.shape[1]
    span = plane // depth
    half = span // 2
    channels = lift.shape[1]
    modes = mode_weight.shape[0]
    own_j = modes // KX
    total_x = local_x * devices
    tab = {k: jnp.asarray(v) for k, v in tables(span, depth, total_x, devices, local_x).items()}
    sds = jax.ShapeDtypeStruct
    smem = pl.BlockSpec(memory_space=pltpu.SMEM)

    pack, conc, walls = pl.pallas_call(
        pack_kernel,
        name="pack",
        out_shape=(
            sds((local_x, half + 16, 2 * depth), BF16),
            sds((local_x, half, 2 * depth), F32),
            sds((local_x, 8, half), F32),
        ),
        in_specs=hbm(5),
        out_specs=vmem(3),
        scratch_shapes=[pltpu.VMEM(conc_init.shape, F32)]
        + [pltpu.VMEM(cover_init.shape, F32)] * 3
        + [pltpu.VMEM(site_mask.shape, jnp.int32), pltpu.SemaphoreType.DMA((5,))],
        compiler_params=params(4),
        cost_estimate=cost(0.3),
    )(*map(in_hbm, (conc_init, cover_init, rate_on, rate_off, site_mask)))
    seams = [(i, i + 1) for i in range(1, devices - 1, 2)]
    across = lax.ppermute(pack, "slab", seams + [(j, i) for i, j in seams])
    within = lax.ppermute(pack, "slab", [(i, i ^ 1) for i in range(devices)])
    constants = [tab[k] for k in ("perm", "back", "wave_yt", "place_c", "place_w")]
    early = pl.pallas_call(
        early_kernel,
        name="early",
        out_shape=(
            sds((local_x, 2 * depth, half), F32),
            sds((4 * local_x, span), F32),
            sds((2 * depth, half), F32),
            *(sds(v.shape, v.dtype) for v in constants),
        ),
        in_specs=vmem(2) + hbm(7),
        out_specs=vmem(8),
        scratch_shapes=[
            pltpu.VMEM((1, span), jnp.int32), pltpu.VMEM(inlet_profiles.shape, F32), pltpu.SemaphoreType.DMA((7,)),
        ],
        compiler_params=params(8),
        cost_estimate=cost(1.5),
    )(conc, walls, *map(in_hbm, (inlet_index.reshape(1, span), inlet_profiles, *constants)))
    cover_out, conc_z, cover_z, send = pl.pallas_call(
        functools.partial(transport_kernel, devices),
        name="transport",
        out_shape=(
            sds((local_x, span), F32),
            sds((2 * depth, local_x, half), F32),
            sds((local_x, span), F32),
            sds((KY, 4 * local_x * KZ), F32),
        ),
        in_specs=vmem(10),
        out_specs=vmem(4),
        scratch_shapes=[pltpu.VMEM((2, 3 * local_x, 2 * depth, half), F32)],
        compiler_params=params(8),
        cost_estimate=cost(3.0),
    )(across, within, *early)
    cot_z, mapped, terms, weigh, conc_out = pl.pallas_call(
        prepare_kernel,
        name="prepare",
        out_shape=(
            sds((2 * depth, local_x, half), F32),
            sds((3, 2, channels, modes), F32),
            sds((local_x * channels, 32), BF16),
            sds((16, local_x * channels), BF16),
            sds(conc_init.shape, F32),
        ),
        in_specs=hbm(1) + [smem] + hbm(1) + vmem(5),
        out_specs=vmem(5),
        scratch_shapes=[
            pltpu.VMEM((local_x, half, 2 * depth), F32),
            pltpu.VMEM(cotangent.shape, F32),
            pltpu.VMEM((2, channels, channels, modes), BF16),
            pltpu.SemaphoreType.DMA((3,)),
        ],
        compiler_params=params(8),
        cost_estimate=cost(2.0),
    )(
        in_hbm(cotangent), lift, in_hbm(mode_weight.transpose(1, 2, 3, 0)),
        lift, point_weight, point_bias.reshape(1, -1), readout.reshape(1, -1), conc_z,
    )
    if own_j != KZ:
        send = send.reshape(KY, 4 * local_x, KZ // own_j, own_j).transpose(0, 2, 1, 3)
        send = send.reshape(devices, 4 * local_x * own_j)
    got = lax.all_to_all(send, "slab", 0, 0, tiled=True)
    ones = math.sqrt(total_x * plane)
    inv, spec = pl.pallas_call(
        functools.partial(mixing_kernel, ones),
        name="mixing",
        out_shape=(
            sds((2 * KY * KZ, local_x * channels), BF16),
            sds((8, 2 * modes), F32),
        ),
        in_specs=vmem(4),
        out_specs=vmem(2),
        scratch_shapes=[pltpu.VMEM((local_x * channels // 128, 2 * KY * KZ, 128), F32)],
        compiler_params=params(4),
        cost_estimate=cost(1.6),
    )(got, tab["ax"], tab["bx"], mapped)
    inv = lax.all_to_all(inv, "slab", 0, 0, tiled=True)
    rows = local_x * channels
    wide = ZG * 2 * KY
    grad, lhs = pl.pallas_call(
        functools.partial(layer_kernel, own_j),
        name="layer",
        out_shape=(
            sds((2 * KY * KZ, rows + 128 * tail_blocks(own_j)), BF16),
            sds((depth // ZG, rows, wide), BF16),
        ),
        in_specs=vmem(8),
        out_specs=vmem(2),
        scratch_shapes=[
            pltpu.VMEM((depth * 2 * KY, rows), BF16),
            pltpu.VMEM((depth, 16, span), BF16),
            pltpu.VMEM((24, rows), F32),
        ]
        + [pltpu.VMEM((rows, span), F32)] * 2
        + [pltpu.VMEM((rows, span), BF16)] * 2,
        compiler_params=params(16),
        cost_estimate=cost(11.0),
    )(inv, conc_z, cot_z, cover_z, terms, readout.reshape(1, -1), tab["ez"], tab["fwd"])
    grad = lax.all_to_all(grad, "slab", 0, 0, tiled=True)
    pred = pl.pallas_call(
        predict_kernel,
        name="predict",
        out_shape=sds((local_x, plane), F32),
        in_specs=vmem(6),
        out_specs=pl.BlockSpec(memory_space=pltpu.VMEM),
        scratch_shapes=[pltpu.VMEM((2 * depth, local_x, half), F32), pltpu.VMEM((local_x, half, 2 * depth), F32)]
        + [pltpu.VMEM((rows, span), F32)] * 2
        + [pltpu.VMEM((rows, span), BF16)] * 2,
        compiler_params=params(8),
        cost_estimate=cost(5.5),
    )(lhs, conc_z, cover_z, terms, weigh, tab["fwd"])
    grad_modes, grad_point = pl.pallas_call(
        functools.partial(outer_kernel, own_j),
        name="outer",
        out_shape=(
            sds((2, channels, channels, modes), F32),
            sds((channels, channels), F32),
        ),
        in_specs=vmem(4),
        out_specs=hbm(1) + vmem(1),
        scratch_shapes=[
            pltpu.VMEM((2, channels, channels, modes), F32),
            pltpu.VMEM((2, channels, modes), F32),
            pltpu.VMEM((rows // 128, 2 * KY * KZ, 128), F32),
            pltpu.SemaphoreType.DMA((2, OUT_BLOCKS)),
        ],
        compiler_params=params(12),
        cost_estimate=cost(3.0),
    )(grad, spec, tab["gx"], lift)
    return (
        conc_out,
        cover_out,
        pred,
        grad_modes.transpose(3, 0, 1, 2),
        grad_point,
    )


def solution(mesh):
    placed = (
        P(("groups", "slab"), None),
        P(("groups", "slab"), None),
        P(("groups", "slab"), None),
        P(("groups", "slab"), None),
        P(("groups", "slab"), None),
        P("groups", None),
        P("groups"),
        P(),
        P("slab", None, None, None),
        P(),
        P(),
        P(),
        P(("groups", "slab"), None),
    )
    return jax.shard_map(
        body,
        mesh=mesh,
        in_specs=placed,
        out_specs=(
            P(("groups", "slab"), None),
            P(("groups", "slab"), None),
            P(("groups", "slab"), None),
            P(("groups", "slab"), None, None, None),
            P("groups", None),
        ),
        check_vma=False,
    )
```
